512 devices in a mesh: batch: 32 (over z, y_hi), weight: 16 (over x, y_lo, core).
Axes of the slice: x: 4, y: 8 (y_hi: 4, y_lo: 2; y = y_hi * 2 + y_lo), z: 8, core: 2. Of those that a mesh axis runs over, the one named last changes fastest.
Arguments:
- tokens: bfloat16 [16384, 8192], P(('batch', 'weight')), may hold values from -6 to 6
- segment_ids: int32 [16384], P('batch'), may hold values from 0 to 511, never falling along the last dimension, each value on 1 to 64 neighbouring positions
- norm_gain: float32 [8192], replicated, may hold values from 0.1 to 1.9
- query_weight: bfloat16 [8192, 8192], P('batch', 'weight'), may hold values from -0.0625 to 0.0625
- key_weight: bfloat16 [8192, 1024], P('batch'), may hold values from -0.0625 to 0.0625
- value_weight: bfloat16 [8192, 1024], P('batch'), may hold values from -0.0625 to 0.0625
Outputs:
- attended: bfloat16 [16384, 8192], P('batch', 'weight')
The draws below stay inside these ranges and needn't reach their ends.
Inputs may be any that keep to these rules, and one draw needn't show every extreme that they name: `segment_ids`: segment ids never fall along the tokens; each id covers 1 to 64 consecutive tokens, one of them exactly 64.
All inputs are finite; a program needn't handle non-finite values.
Results may differ from the reference program's by a relative error of at most 0.0079.
Values may be sent and summed in bfloat16 or wider, within the bound.
No kernel may reach another device: no remote copies, remote signals or barrier semaphores. Data moves between devices by JAX's collectives and lax.ppermute only.
A program may use at most 64 MiB of HBM per device.

```python
import math
import jax
import jax.numpy as jnp
import numpy as np
from jax import lax

D = 8192
HEADS = 64
KV_HEADS = 8
HEAD_DIM = 128
MOST = 64
PACK = 512
TOKENS = 16384
SEGMENTS = 512


def shard_levels(stream_key, shape, shards, smallest, top_value):
    loudness = 1.0
    for dim, parts in shards:
        steps = jax.random.uniform(jax.random.fold_in(jax.random.fold_in(stream_key, 6), dim), (parts,), jnp.float32, smallest / len(shards), top_value / len(shards))
        loudness = loudness * jnp.repeat(jnp.exp(steps), shape[dim] // parts).reshape((-1,) + (1,) * (len(shape) - 1 - dim))
    return loudness


def length_profile(amount, total, bound, slope):
    loads = [(1 << 20) // math.isqrt(rank ** slope) + 1 for rank in range(2, amount + 1)]
    spare, given = total - bound - (amount - 1), [1] * (amount - 1)
    while spare > 0:
        movable = [i for i in range(amount - 1) if given[i] < bound]
        pool, remaining = sum([loads[i] for i in movable]), spare
        for i in movable:
            addition = min(bound - given[i], max(1, remaining * loads[i] // pool), spare)
            given[i] = given[i] + addition
            spare = spare - addition
    return np.array([bound] + given)


def ragged(rng, count, total, reach, lean):
    if count == 2:
        one = jax.random.randint(rng, (), max(1, total - reach), min(reach, total - 1) + 1)
        return jnp.stack([one, total - one])
    lengths = jnp.asarray(length_profile(count, total, reach, lean), jnp.int32)
    couples = (count - 1) // 2
    giver, taker = lengths[1:1 + 2 * couples:2], lengths[2:2 + 2 * couples:2]
    slack = jnp.minimum(giver - 1, reach - taker)
    moved = jax.random.randint(jax.random.fold_in(rng, 1), (couples,), 0, 1 << 20) % (slack + 1)
    lengths = lengths.at[1:1 + 2 * couples:2].set(giver - moved).at[2:2 + 2 * couples:2].set(taker + moved)
    return lengths[jax.random.permutation(jax.random.fold_in(rng, 2), count)]


def gaussian(key, extent, width, limit, pieces=(), held_as=jnp.bfloat16):
    level = shard_levels(key, extent, pieces, -0.22, 0.18) if pieces else 1.0
    array = jax.random.normal(key, extent, jnp.float32) * width * level
    return jnp.minimum(jnp.maximum(array, -limit), limit).astype(held_as)


def setup_inputs(seed: int = 0) -> dict:
    keys = jax.random.split(jax.random.key(seed), 7)
    tokens = gaussian(keys[0], (TOKENS, D), 1.0, 6.0, ((0, 512),))
    segment_ids = jnp.searchsorted(jnp.cumsum(ragged(keys[1], SEGMENTS, TOKENS, MOST, 2)), jnp.arange(TOKENS), side="right").astype(jnp.int32)
    norm_gain = jnp.clip(1.0 + 0.18 * jax.random.normal(keys[2], (D,), jnp.float32), 0.1, 1.9)
    query_weight = gaussian(keys[3], (D, HEADS * HEAD_DIM), D ** -0.5, 0.0625, ((0, 32), (1, 16)))
    key_weight = gaussian(keys[4], (D, KV_HEADS * HEAD_DIM), D ** -0.5, 0.0625, ((0, 32),))
    value_weight = gaussian(keys[5], (D, KV_HEADS * HEAD_DIM), D ** -0.5, 0.0625, ((0, 32),))
    return dict(tokens=tokens, segment_ids=segment_ids, norm_gain=norm_gain, query_weight=query_weight, key_weight=key_weight, value_weight=value_weight)


ROPE_BASE = 500000.0
EPSILON = 1e-05

def positions_in_segment(seg_ids):
    places = jnp.arange(seg_ids.shape[0], dtype=jnp.int32)
    earlier = jnp.concatenate([seg_ids[:1] - 1, seg_ids[:-1]])
    starts = jnp.where(seg_ids != earlier, places, 0).astype(jnp.int32)
    leading = lax.cummax(starts, axis=0)
    return (places - leading).astype(jnp.int32)

def rotate(vectors, positions):
    half_dim = vectors.shape[-1] // 2
    ratios = jnp.arange(half_dim, dtype=jnp.float32) * (2.0 / vectors.shape[-1])
    frequency = jnp.exp(-math.log(ROPE_BASE) * ratios)
    angles = positions.astype(jnp.float32)[:, None] * frequency[None, :]
    cosine = jnp.cos(angles)[:, None, :]
    sine_part = jnp.sin(angles)[:, None, :]
    front_half = vectors[..., :half_dim]
    back_half = vectors[..., half_dim:]
    return jnp.concatenate([front_half * cosine - back_half * sine_part, back_half * cosine + front_half * sine_part], axis=-1)

def reference(tokens, segment_ids, norm_gain, query_weight, key_weight, value_weight):
    values = tokens.astype(jnp.float32)
    inverse_rms = lax.rsqrt(lax.optimization_barrier(jnp.mean(values * values, axis=1, keepdims=True)) + EPSILON)
    normed = (values * inverse_rms * norm_gain[None, :]).astype(jnp.bfloat16)
    queries = jnp.dot(normed, query_weight, preferred_element_type=jnp.float32)
    key_rows = jnp.dot(normed, key_weight, preferred_element_type=jnp.float32).astype(jnp.bfloat16)
    value_rows = jnp.dot(normed, value_weight, preferred_element_type=jnp.float32).astype(jnp.bfloat16)
    pack_count = TOKENS // PACK
    group_size = HEADS // KV_HEADS

    def one_pack(pack_items):
        query_pack, key_pack, value_pack, seg_ids = pack_items
        positions = positions_in_segment(seg_ids)
        rotated = rotate(query_pack.reshape(PACK, HEADS, HEAD_DIM), positions).astype(jnp.bfloat16)
        rotated_keys = rotate(key_pack.astype(jnp.float32).reshape(PACK, KV_HEADS, HEAD_DIM), positions).astype(jnp.bfloat16)
        grouped = rotated.reshape(PACK, KV_HEADS, group_size, HEAD_DIM).astype(jnp.float32)
        scores = jnp.einsum('ingd,jnd->ngij', grouped, rotated_keys.astype(jnp.float32)) * HEAD_DIM ** (-0.5)
        places = jnp.arange(PACK, dtype=jnp.int32)
        allowed = (seg_ids[:, None] == seg_ids[None, :]) & (places[None, :] <= places[:, None])
        weights = jnp.where(allowed, jnp.exp(scores), 0.0)
        probabilities = (weights / lax.optimization_barrier(jnp.sum(weights, axis=-1, keepdims=True))).astype(jnp.bfloat16)
        mixed = jnp.einsum('ngij,jnd->ingd', probabilities.astype(jnp.float32), value_pack.reshape(PACK, KV_HEADS, HEAD_DIM).astype(jnp.float32))
        return mixed.reshape(PACK, HEADS * HEAD_DIM).astype(jnp.bfloat16)
    stacked = lax.map(one_pack, (queries.reshape(pack_count, PACK, HEADS * HEAD_DIM), key_rows.reshape(pack_count, PACK, KV_HEADS * HEAD_DIM), value_rows.reshape(pack_count, PACK, KV_HEADS * HEAD_DIM), segment_ids.reshape(pack_count, PACK)))
    return stacked.reshape(TOKENS, HEADS * HEAD_DIM)
```

```python
import math

import jax
import jax.numpy as jnp
from jax import lax
from jax.sharding import Mesh
from jax.sharding import PartitionSpec as P

HEADS = 64
KV_HEADS = 8
HEAD_DIM = 128


ROPE_BASE = 500000.0
EPSILON = 1e-05

Z, YH, WC, CORE = "z", "yh", "wc", "core"


def positions_in_segment(seg_ids):
    places = jnp.arange(seg_ids.shape[0], dtype=jnp.int32)
    earlier = jnp.concatenate([seg_ids[:1] - 1, seg_ids[:-1]])
    starts = jnp.where(seg_ids != earlier, places, 0)
    leading = lax.cummax(starts, axis=0)
    return places - leading


def rotate(vectors, positions):
    half_dim = vectors.shape[-1] // 2
    ratios = jnp.arange(half_dim, dtype=jnp.float32) * (2.0 / vectors.shape[-1])
    frequency = jnp.exp(-math.log(ROPE_BASE) * ratios)
    angles = positions.astype(jnp.float32)[:, None] * frequency[None, :]
    cosine = jnp.cos(angles)[:, None, :]
    sine_part = jnp.sin(angles)[:, None, :]
    front_half = vectors[..., :half_dim]
    back_half = vectors[..., half_dim:]
    return jnp.concatenate(
        [front_half * cosine - back_half * sine_part, back_half * cosine + front_half * sine_part],
        axis=-1,
    )


def attend(grouped, rotated_keys, value_rows, seg_ids):
    scores = jnp.einsum(
        "ingd,jnd->ngij", grouped, rotated_keys, preferred_element_type=jnp.float32
    ) * grouped.shape[-1] ** (-0.5)
    places = jnp.arange(seg_ids.shape[0], dtype=jnp.int32)
    allowed = (seg_ids[:, None] == seg_ids[None, :]) & (places[None, :] <= places[:, None])
    weights = jnp.where(allowed, jnp.exp(scores), 0.0)
    probabilities = (weights / jnp.sum(weights, axis=-1, keepdims=True)).astype(jnp.bfloat16)
    mixed = jnp.einsum(
        "ngij,jnd->ingd", probabilities, value_rows, preferred_element_type=jnp.float32
    )
    return mixed.astype(jnp.bfloat16)


def per_device(tokens, segment_ids, norm_gain, query_weight, key_weight, value_weight):
    head_dim = HEAD_DIM
    query_cols = query_weight.shape[1]
    heads_dev = query_cols // head_dim
    group_size = HEADS // KV_HEADS
    core = lax.axis_index(CORE)
    n_core = lax.psum(1, CORE)
    first_kv = (lax.axis_index(WC) * n_core + core) * heads_dev // group_size
    key_block = lax.dynamic_slice_in_dim(key_weight, first_kv * head_dim, head_dim, 1)
    value_block = lax.dynamic_slice_in_dim(value_weight, first_kv * head_dim, head_dim, 1)
    kv_block = jnp.where(core == 0, key_block, value_block)
    values = tokens.astype(jnp.float32)
    inverse_rms = lax.rsqrt(jnp.mean(values * values, axis=1, keepdims=True) + EPSILON)
    normed = (values * inverse_rms * norm_gain[None, :]).astype(jnp.bfloat16)
    local_weights = jnp.concatenate([query_weight, kv_block], axis=1)
    full_weights = lax.all_gather(
        lax.all_gather(local_weights, YH, axis=0, tiled=True), Z, axis=0, tiled=True
    )
    gathered = lax.all_gather(lax.all_gather(normed, WC, axis=0), CORE, axis=0)
    pack_rows = gathered.shape[0] * gathered.shape[1] * gathered.shape[2]
    projected = jnp.dot(
        gathered.reshape(pack_rows, -1), full_weights, preferred_element_type=jnp.float32
    )
    projected = projected.reshape(gathered.shape[0], gathered.shape[1], gathered.shape[2], -1)
    projected = jnp.swapaxes(projected, 0, 1).reshape(pack_rows, -1)
    query_part = projected[:, :query_cols]
    own_rows = projected[:, query_cols:].astype(jnp.bfloat16)
    other_rows = lax.ppermute(own_rows, CORE, perm=[(0, 1), (1, 0)])
    key_rows = jnp.where(core == 0, own_rows, other_rows)
    value_rows = jnp.where(core == 0, other_rows, own_rows)
    local_kv = 1
    positions = positions_in_segment(segment_ids)
    queries = rotate(query_part.reshape(pack_rows, heads_dev, head_dim), positions).astype(
        jnp.bfloat16
    )
    rotated_keys = rotate(
        key_rows.astype(jnp.float32).reshape(pack_rows, local_kv, head_dim), positions
    ).astype(jnp.bfloat16)
    grouped = queries.reshape(pack_rows, local_kv, heads_dev // local_kv, head_dim)
    attended = attend(
        grouped, rotated_keys, value_rows.reshape(pack_rows, local_kv, head_dim), segment_ids
    )
    return attended.reshape(pack_rows, query_cols)


def split_mesh(mesh):
    n_batch, n_weight = mesh.devices.shape
    yh = n_batch // 8 if n_batch % 8 == 0 else 1
    devices = mesh.devices.reshape(n_batch // yh, yh, n_weight // 2, 2)
    return Mesh(devices, (Z, YH, WC, CORE))


def solution(mesh):
    fine = split_mesh(mesh)
    batch, weight = (Z, YH), (WC, CORE)
    placed = (
        P(batch + weight, None),
        P(batch),
        P(),
        P(batch, weight),
        P(batch, None),
        P(batch, None),
    )
    return jax.shard_map(
        per_device, mesh=fine, in_specs=placed, out_specs=P(batch, weight), check_vma=False
    )
```

```python
import math

import jax
import jax.numpy as jnp
from jax import lax
from jax.sharding import PartitionSpec as P

HEADS = 64
KV_HEADS = 8
HEAD_DIM = 128


ROPE_BASE = 500000.0
EPSILON = 1e-05

CHIP_CYCLE = (0, 2, 4, 6, 7, 5, 3, 1)


def positions_in_segment(seg_ids):
    places = jnp.arange(seg_ids.shape[0], dtype=jnp.int32)
    earlier = jnp.concatenate([seg_ids[:1] - 1, seg_ids[:-1]])
    starts = jnp.where(seg_ids != earlier, places, 0)
    leading = lax.cummax(starts, axis=0)
    return places - leading


def rotate(vectors, positions):
    half_dim = vectors.shape[-1] // 2
    ratios = jnp.arange(half_dim, dtype=jnp.float32) * (2.0 / vectors.shape[-1])
    frequency = jnp.exp(-math.log(ROPE_BASE) * ratios)
    angles = positions.astype(jnp.float32)[:, None] * frequency[None, :]
    cosine = jnp.cos(angles)[:, None, :]
    sine_part = jnp.sin(angles)[:, None, :]
    front_half = vectors[..., :half_dim]
    back_half = vectors[..., half_dim:]
    return jnp.concatenate(
        [front_half * cosine - back_half * sine_part, back_half * cosine + front_half * sine_part],
        axis=-1,
    )


def attend(grouped, rotated_keys, value_rows, seg_ids):
    scores = jnp.einsum(
        "ingd,jnd->ngij", grouped, rotated_keys, preferred_element_type=jnp.float32
    ) * grouped.shape[-1] ** (-0.5)
    places = jnp.arange(seg_ids.shape[0], dtype=jnp.int32)
    allowed = (seg_ids[:, None] == seg_ids[None, :]) & (places[None, :] <= places[:, None])
    weights = jnp.where(allowed, jnp.exp(scores), 0.0)
    probabilities = (weights / jnp.sum(weights, axis=-1, keepdims=True)).astype(jnp.bfloat16)
    mixed = jnp.einsum(
        "ngij,jnd->ingd", probabilities, value_rows, preferred_element_type=jnp.float32
    )
    return mixed.astype(jnp.bfloat16)


def device_cycle():
    cycle = []
    for i, chip in enumerate(CHIP_CYCLE):
        cores = (0, 1) if i % 2 == 0 else (1, 0)
        cycle += [chip * 2 + c for c in cores]
    return cycle


def ring_gather(block, n):
    cycle = device_cycle()
    where_in = [0] * n
    for q, w in enumerate(cycle):
        where_in[w] = q
    to_prev = [(cycle[q], cycle[(q - 1) % n]) for q in range(n)]
    to_next = [(cycle[q], cycle[(q + 1) % n]) for q in range(n)]
    right, left = [], []
    from_right, from_left = block, block
    for step in range(1, n // 2 + 1):
        if step < n // 2:
            from_right = lax.ppermute(from_right, "weight", perm=to_prev)
            right.append(from_right)
        from_left = lax.ppermute(from_left, "weight", perm=to_next)
        left.append(from_left)
    slots = jnp.stack([block] + right + left)
    me = jnp.asarray(where_in, jnp.int32)[lax.axis_index("weight")]
    distance = (jnp.asarray(where_in, jnp.int32) - me) % n
    slot_of = jnp.where(distance < n // 2, distance, n + n // 2 - 1 - distance)
    return slots, slot_of


def per_device(tokens, segment_ids, norm_gain, query_weight, key_weight, value_weight):
    head_dim = HEAD_DIM
    query_cols = query_weight.shape[1]
    heads_dev = query_cols // head_dim
    group_size = HEADS // KV_HEADS
    n_weight = lax.psum(1, "weight")
    me = lax.axis_index("weight")
    core = me % 2
    first_kv = me * heads_dev // group_size
    key_block = lax.dynamic_slice_in_dim(key_weight, first_kv * head_dim, head_dim, 1)
    value_block = lax.dynamic_slice_in_dim(value_weight, first_kv * head_dim, head_dim, 1)
    kv_block = jnp.where(core == 0, key_block, value_block)
    values = tokens.astype(jnp.float32)
    inverse_rms = lax.rsqrt(jnp.mean(values * values, axis=1, keepdims=True) + EPSILON)
    normed = (values * inverse_rms * norm_gain[None, :]).astype(jnp.bfloat16)
    local_weights = jnp.concatenate([query_weight, kv_block], axis=1)
    full_weights = lax.all_gather(local_weights, "batch", axis=0, tiled=True)
    slots, slot_of = ring_gather(normed, n_weight)
    block_rows = normed.shape[0]
    pack_rows = n_weight * block_rows
    projected = jnp.dot(
        slots.reshape(pack_rows, -1), full_weights, preferred_element_type=jnp.float32
    )
    projected = jnp.take(projected.reshape(n_weight, block_rows, -1), slot_of, axis=0)
    projected = projected.reshape(pack_rows, -1)
    query_part = projected[:, :query_cols]
    own_rows = projected[:, query_cols:].astype(jnp.bfloat16)
    partner = [(w, w ^ 1) for w in range(n_weight)]
    other_rows = lax.ppermute(own_rows, "weight", perm=partner)
    key_rows = jnp.where(core == 0, own_rows, other_rows)
    value_rows = jnp.where(core == 0, other_rows, own_rows)
    local_kv = 1
    positions = positions_in_segment(segment_ids)
    queries = rotate(query_part.reshape(pack_rows, heads_dev, head_dim), positions).astype(
        jnp.bfloat16
    )
    rotated_keys = rotate(
        key_rows.astype(jnp.float32).reshape(pack_rows, local_kv, head_dim), positions
    ).astype(jnp.bfloat16)
    grouped = queries.reshape(pack_rows, local_kv, heads_dev // local_kv, head_dim)
    attended = attend(
        grouped, rotated_keys, value_rows.reshape(pack_rows, local_kv, head_dim), segment_ids
    )
    return attended.reshape(pack_rows, query_cols)


def solution(mesh):
    placed = (
        P(("batch", "weight"), None),
        P("batch"),
        P(),
        P("batch", "weight"),
        P("batch", None),
        P("batch", None),
    )
    return jax.shard_map(
        per_device, mesh=mesh, in_specs=placed, out_specs=P("batch", "weight"), check_vma=False
    )
```

```python
import math

import jax
import jax.numpy as jnp
from jax import lax
from jax.sharding import PartitionSpec as P

HEADS = 64
KV_HEADS = 8
HEAD_DIM = 128


ROPE_BASE = 500000.0
EPSILON = 1e-05

Z_CHIPS = 8


def positions_in_segment(seg_ids):
    places = jnp.arange(seg_ids.shape[0], dtype=jnp.int32)
    earlier = jnp.concatenate([seg_ids[:1] - 1, seg_ids[:-1]])
    starts = jnp.where(seg_ids != earlier, places, 0)
    leading = lax.cummax(starts, axis=0)
    return places - leading


def rotate(vectors, positions):
    half_dim = vectors.shape[-1] // 2
    ratios = jnp.arange(half_dim, dtype=jnp.float32) * (2.0 / vectors.shape[-1])
    frequency = jnp.exp(-math.log(ROPE_BASE) * ratios)
    angles = positions.astype(jnp.float32)[:, None] * frequency[None, :]
    cosine = jnp.cos(angles)[:, None, :]
    sine_part = jnp.sin(angles)[:, None, :]
    front_half = vectors[..., :half_dim]
    back_half = vectors[..., half_dim:]
    return jnp.concatenate(
        [front_half * cosine - back_half * sine_part, back_half * cosine + front_half * sine_part],
        axis=-1,
    )


def attend(grouped, rotated_keys, value_rows, seg_ids):
    scores = jnp.einsum(
        "ingd,jnd->ngij", grouped, rotated_keys, preferred_element_type=jnp.float32
    ) * grouped.shape[-1] ** (-0.5)
    places = jnp.arange(seg_ids.shape[0], dtype=jnp.int32)
    allowed = (seg_ids[:, None] == seg_ids[None, :]) & (places[None, :] <= places[:, None])
    weights = jnp.where(allowed, jnp.exp(scores), 0.0)
    probabilities = (weights / jnp.sum(weights, axis=-1, keepdims=True)).astype(jnp.bfloat16)
    mixed = jnp.einsum(
        "ngij,jnd->ingd", probabilities, value_rows, preferred_element_type=jnp.float32
    )
    return mixed.astype(jnp.bfloat16)


def ring_gather(block, axis, stride, count):
    n = lax.psum(1, axis)
    me = lax.axis_index(axis)
    here = (me // stride) % count

    def moved(step):
        pairs = []
        for src in range(n):
            k = (src // stride) % count
            pairs.append((src, src + (((k + step) % count) - k) * stride))
        return pairs

    out = jnp.zeros((count,) + block.shape, block.dtype)
    out = lax.dynamic_update_index_in_dim(out, block, here, 0)
    from_right, from_left = block, block
    for step in range(1, count // 2 + 1):
        if step < count - step:
            from_right = lax.ppermute(from_right, axis, perm=moved(-1))
            out = lax.dynamic_update_index_in_dim(out, from_right, (here + step) % count, 0)
        from_left = lax.ppermute(from_left, axis, perm=moved(1))
        out = lax.dynamic_update_index_in_dim(out, from_left, (here - step) % count, 0)
    return out


def per_device(tokens, segment_ids, norm_gain, query_weight, key_weight, value_weight):
    head_dim = HEAD_DIM
    query_cols = query_weight.shape[1]
    heads_dev = query_cols // head_dim
    group_size = HEADS // KV_HEADS
    n_weight = lax.psum(1, "weight")
    me = lax.axis_index("weight")
    core = me % 2
    first_kv = me * heads_dev // group_size
    key_block = lax.dynamic_slice_in_dim(key_weight, first_kv * head_dim, head_dim, 1)
    value_block = lax.dynamic_slice_in_dim(value_weight, first_kv * head_dim, head_dim, 1)
    kv_block = jnp.where(core == 0, key_block, value_block)
    values = tokens.astype(jnp.float32)
    inverse_rms = lax.rsqrt(jnp.mean(values * values, axis=1, keepdims=True) + EPSILON)
    normed = (values * inverse_rms * norm_gain[None, :]).astype(jnp.bfloat16)
    local_weights = jnp.concatenate([query_weight, kv_block], axis=1)
    n_batch = lax.psum(1, "batch")
    y_hi = n_batch // Z_CHIPS
    near = ring_gather(local_weights, "batch", 1, y_hi)
    near = near.reshape(-1, local_weights.shape[1])
    full_weights = ring_gather(near, "batch", y_hi, Z_CHIPS).reshape(-1, near.shape[1])
    gathered = lax.all_gather(normed, "weight", axis=0, tiled=True)
    pack_rows = gathered.shape[0]
    projected = jnp.dot(gathered, full_weights, preferred_element_type=jnp.float32)
    query_part = projected[:, :query_cols]
    own_rows = projected[:, query_cols:].astype(jnp.bfloat16)
    partner = [(w, w ^ 1) for w in range(n_weight)]
    other_rows = lax.ppermute(own_rows, "weight", perm=partner)
    key_rows = jnp.where(core == 0, own_rows, other_rows)
    value_rows = jnp.where(core == 0, other_rows, own_rows)
    local_kv = 1
    positions = positions_in_segment(segment_ids)
    queries = rotate(query_part.reshape(pack_rows, heads_dev, head_dim), positions).astype(
        jnp.bfloat16
    )
    rotated_keys = rotate(
        key_rows.astype(jnp.float32).reshape(pack_rows, local_kv, head_dim), positions
    ).astype(jnp.bfloat16)
    grouped = queries.reshape(pack_rows, local_kv, heads_dev // local_kv, head_dim)
    attended = attend(
        grouped, rotated_keys, value_rows.reshape(pack_rows, local_kv, head_dim), segment_ids
    )
    return attended.reshape(pack_rows, query_cols)


def solution(mesh):
    placed = (
        P(("batch", "weight"), None),
        P("batch"),
        P(),
        P("batch", "weight"),
        P("batch", None),
        P("batch", None),
    )
    return jax.shard_map(
        per_device, mesh=mesh, in_specs=placed, out_specs=P("batch", "weight"), check_vma=False
    )
```

```python
import math

import jax
import jax.numpy as jnp
from jax import lax
from jax.sharding import PartitionSpec as P

HEADS = 64
KV_HEADS = 8
HEAD_DIM = 128


ROPE_BASE = 500000.0
EPSILON = 1e-05

Z_CHIPS = 8


def positions_in_segment(seg_ids):
    places = jnp.arange(seg_ids.shape[0], dtype=jnp.int32)
    earlier = jnp.concatenate([seg_ids[:1] - 1, seg_ids[:-1]])
    starts = jnp.where(seg_ids != earlier, places, 0)
    leading = lax.cummax(starts, axis=0)
    return places - leading


def rotate(vectors, positions):
    half_dim = vectors.shape[-1] // 2
    ratios = jnp.arange(half_dim, dtype=jnp.float32) * (2.0 / vectors.shape[-1])
    frequency = jnp.exp(-math.log(ROPE_BASE) * ratios)
    angles = positions.astype(jnp.float32)[:, None] * frequency[None, :]
    cosine = jnp.cos(angles)[:, None, :]
    sine_part = jnp.sin(angles)[:, None, :]
    front_half = vectors[..., :half_dim]
    back_half = vectors[..., half_dim:]
    return jnp.concatenate(
        [front_half * cosine - back_half * sine_part, back_half * cosine + front_half * sine_part],
        axis=-1,
    )


def attend(grouped, rotated_keys, value_rows, seg_ids):
    scores = jnp.einsum(
        "ingd,jnd->ngij", grouped, rotated_keys, preferred_element_type=jnp.float32
    ) * grouped.shape[-1] ** (-0.5)
    places = jnp.arange(seg_ids.shape[0], dtype=jnp.int32)
    allowed = (seg_ids[:, None] == seg_ids[None, :]) & (places[None, :] <= places[:, None])
    weights = jnp.where(allowed, jnp.exp(scores), 0.0)
    probabilities = (weights / jnp.sum(weights, axis=-1, keepdims=True)).astype(jnp.bfloat16)
    mixed = jnp.einsum(
        "ngij,jnd->ingd", probabilities, value_rows, preferred_element_type=jnp.float32
    )
    return mixed.astype(jnp.bfloat16)


def ring_gather(block, axis, stride, count):
    n = lax.psum(1, axis)
    me = lax.axis_index(axis)
    here = (me // stride) % count

    def moved(step):
        pairs = []
        for src in range(n):
            k = (src // stride) % count
            pairs.append((src, src + (((k + step) % count) - k) * stride))
        return pairs

    out = jnp.zeros((count,) + block.shape, block.dtype)
    out = lax.dynamic_update_index_in_dim(out, block, here, 0)
    from_right, from_left = block, block
    for step in range(1, count // 2 + 1):
        if step < count - step:
            from_right = lax.ppermute(from_right, axis, perm=moved(-1))
            out = lax.dynamic_update_index_in_dim(out, from_right, (here + step) % count, 0)
        from_left = lax.ppermute(from_left, axis, perm=moved(1))
        out = lax.dynamic_update_index_in_dim(out, from_left, (here - step) % count, 0)
    return out


def per_device(tokens, segment_ids, norm_gain, query_weight, key_weight, value_weight):
    head_dim = HEAD_DIM
    query_cols = query_weight.shape[1]
    heads_dev = query_cols // head_dim
    group_size = HEADS // KV_HEADS
    n_weight = lax.psum(1, "weight")
    me = lax.axis_index("weight")
    core = me % 2
    first_kv = me * heads_dev // group_size
    key_block = lax.dynamic_slice_in_dim(key_weight, first_kv * head_dim, head_dim, 1)
    value_block = lax.dynamic_slice_in_dim(value_weight, first_kv * head_dim, head_dim, 1)
    kv_block = jnp.where(core == 0, key_block, value_block)
    values = tokens.astype(jnp.float32)
    inverse_rms = lax.rsqrt(jnp.mean(values * values, axis=1, keepdims=True) + EPSILON)
    normed = (values * inverse_rms * norm_gain[None, :]).astype(jnp.bfloat16)
    n_batch = lax.psum(1, "batch")
    y_hi = n_batch // Z_CHIPS
    near = ring_gather(query_weight, "batch", 1, y_hi).reshape(-1, query_cols)
    query_full = ring_gather(near, "batch", y_hi, Z_CHIPS).reshape(-1, query_cols)
    far = ring_gather(kv_block, "batch", y_hi, Z_CHIPS)
    kv_full = ring_gather(far, "batch", 1, y_hi)
    kv_full = jnp.swapaxes(kv_full, 0, 1).reshape(-1, head_dim)
    gathered = lax.all_gather(normed, "weight", axis=0, tiled=True)
    pack_rows = gathered.shape[0]
    query_part = jnp.dot(gathered, query_full, preferred_element_type=jnp.float32)
    own_rows = jnp.dot(gathered, kv_full, preferred_element_type=jnp.float32).astype(jnp.bfloat16)
    partner = [(w, w ^ 1) for w in range(n_weight)]
    other_rows = lax.ppermute(own_rows, "weight", perm=partner)
    key_rows = jnp.where(core == 0, own_rows, other_rows)
    value_rows = jnp.where(core == 0, other_rows, own_rows)
    local_kv = 1
    positions = positions_in_segment(segment_ids)
    queries = rotate(query_part.reshape(pack_rows, heads_dev, head_dim), positions).astype(
        jnp.bfloat16
    )
    rotated_keys = rotate(
        key_rows.astype(jnp.float32).reshape(pack_rows, local_kv, head_dim), positions
    ).astype(jnp.bfloat16)
    grouped = queries.reshape(pack_rows, local_kv, heads_dev // local_kv, head_dim)
    attended = attend(
        grouped, rotated_keys, value_rows.reshape(pack_rows, local_kv, head_dim), segment_ids
    )
    return attended.reshape(pack_rows, query_cols)


def solution(mesh):
    placed = (
        P(("batch", "weight"), None),
        P("batch"),
        P(),
        P("batch", "weight"),
        P("batch", None),
        P("batch", None),
    )
    return jax.shard_map(
        per_device, mesh=mesh, in_specs=placed, out_specs=P("batch", "weight"), check_vma=False
    )
```

```python
import math

import jax
import jax.numpy as jnp
from jax import lax
from jax.sharding import PartitionSpec as P

HEADS = 64
KV_HEADS = 8
HEAD_DIM = 128


ROPE_BASE = 500000.0
EPSILON = 1e-05

Z_CHIPS = 8


def positions_in_segment(seg_ids):
    places = jnp.arange(seg_ids.shape[0], dtype=jnp.int32)
    earlier = jnp.concatenate([seg_ids[:1] - 1, seg_ids[:-1]])
    starts = jnp.where(seg_ids != earlier, places, 0)
    leading = lax.cummax(starts, axis=0)
    return places - leading


def rotate(vectors, positions):
    half_dim = vectors.shape[-1] // 2
    ratios = jnp.arange(half_dim, dtype=jnp.float32) * (2.0 / vectors.shape[-1])
    frequency = jnp.exp(-math.log(ROPE_BASE) * ratios)
    angles = positions.astype(jnp.float32)[:, None] * frequency[None, :]
    cosine = jnp.cos(angles)[:, None, :]
    sine_part = jnp.sin(angles)[:, None, :]
    front_half = vectors[..., :half_dim]
    back_half = vectors[..., half_dim:]
    return jnp.concatenate(
        [front_half * cosine - back_half * sine_part, back_half * cosine + front_half * sine_part],
        axis=-1,
    )


def attend(grouped, rotated_keys, value_rows, seg_ids):
    scores = jnp.einsum(
        "ingd,jnd->ngij", grouped, rotated_keys, preferred_element_type=jnp.float32
    ) * grouped.shape[-1] ** (-0.5)
    places = jnp.arange(seg_ids.shape[0], dtype=jnp.int32)
    allowed = (seg_ids[:, None] == seg_ids[None, :]) & (places[None, :] <= places[:, None])
    weights = jnp.where(allowed, jnp.exp(scores), 0.0)
    probabilities = (weights / jnp.sum(weights, axis=-1, keepdims=True)).astype(jnp.bfloat16)
    mixed = jnp.einsum(
        "ngij,jnd->ingd", probabilities, value_rows, preferred_element_type=jnp.float32
    )
    return mixed.astype(jnp.bfloat16)


def ring_gather(block, axis, stride, count):
    n = lax.psum(1, axis)
    me = lax.axis_index(axis)
    here = (me // stride) % count

    def moved(step):
        pairs = []
        for src in range(n):
            k = (src // stride) % count
            pairs.append((src, src + (((k + step) % count) - k) * stride))
        return pairs

    out = jnp.zeros((count,) + block.shape, block.dtype)
    out = lax.dynamic_update_index_in_dim(out, block, here, 0)
    from_right, from_left = block, block
    for step in range(1, count // 2 + 1):
        if step < count - step:
            from_right = lax.ppermute(from_right, axis, perm=moved(-1))
            out = lax.dynamic_update_index_in_dim(out, from_right, (here + step) % count, 0)
        from_left = lax.ppermute(from_left, axis, perm=moved(1))
        out = lax.dynamic_update_index_in_dim(out, from_left, (here - step) % count, 0)
    return out


def ring_matmul(rows, block, axis, stride, count):
    n = lax.psum(1, axis)
    me = lax.axis_index(axis)
    here = (me // stride) % count
    depth = block.shape[0]

    def moved(step):
        pairs = []
        for src in range(n):
            k = (src // stride) % count
            pairs.append((src, src + (((k + step) % count) - k) * stride))
        return pairs

    def product(part, owner):
        lhs = lax.dynamic_slice_in_dim(rows, owner * depth, depth, 1)
        return jnp.dot(lhs, part, preferred_element_type=jnp.float32)

    total = product(block, here)
    from_right, from_left = block, block
    for step in range(1, count // 2 + 1):
        if step == 2:
            rows, from_right, from_left = lax.optimization_barrier((rows, from_right, from_left))
        if step < count - step:
            from_right = lax.ppermute(from_right, axis, perm=moved(-1))
            total = total + product(from_right, (here + step) % count)
        from_left = lax.ppermute(from_left, axis, perm=moved(1))
        total = total + product(from_left, (here - step) % count)
    return total


def per_device(tokens, segment_ids, norm_gain, query_weight, key_weight, value_weight):
    head_dim = HEAD_DIM
    query_cols = query_weight.shape[1]
    heads_dev = query_cols // head_dim
    group_size = HEADS // KV_HEADS
    n_weight = lax.psum(1, "weight")
    me = lax.axis_index("weight")
    core = me % 2
    first_kv = me * heads_dev // group_size
    key_block = lax.dynamic_slice_in_dim(key_weight, first_kv * head_dim, head_dim, 1)
    value_block = lax.dynamic_slice_in_dim(value_weight, first_kv * head_dim, head_dim, 1)
    kv_block = jnp.where(core == 0, key_block, value_block)
    values = tokens.astype(jnp.float32)
    inverse_rms = lax.rsqrt(jnp.mean(values * values, axis=1, keepdims=True) + EPSILON)
    normed = (values * inverse_rms * norm_gain[None, :]).astype(jnp.bfloat16)
    local_weights = jnp.concatenate([query_weight, kv_block], axis=1)
    n_batch = lax.psum(1, "batch")
    y_hi = n_batch // Z_CHIPS
    near = ring_gather(local_weights, "batch", 1, y_hi)
    near = near.reshape(-1, local_weights.shape[1])
    gathered = lax.all_gather(normed, "weight", axis=0, tiled=True)
    pack_rows = gathered.shape[0]
    projected = ring_matmul(gathered, near, "batch", y_hi, Z_CHIPS)
    query_part = projected[:, :query_cols]
    own_rows = projected[:, query_cols:].astype(jnp.bfloat16)
    partner = [(w, w ^ 1) for w in range(n_weight)]
    other_rows = lax.ppermute(own_rows, "weight", perm=partner)
    key_rows = jnp.where(core == 0, own_rows, other_rows)
    value_rows = jnp.where(core == 0, other_rows, own_rows)
    local_kv = 1
    positions = positions_in_segment(segment_ids)
    queries = rotate(query_part.reshape(pack_rows, heads_dev, head_dim), positions).astype(
        jnp.bfloat16
    )
    rotated_keys = rotate(
        key_rows.astype(jnp.float32).reshape(pack_rows, local_kv, head_dim), positions
    ).astype(jnp.bfloat16)
    grouped = queries.reshape(pack_rows, local_kv, heads_dev // local_kv, head_dim)
    attended = attend(
        grouped, rotated_keys, value_rows.reshape(pack_rows, local_kv, head_dim), segment_ids
    )
    return attended.reshape(pack_rows, query_cols)


def solution(mesh):
    placed = (
        P(("batch", "weight"), None),
        P("batch"),
        P(),
        P("batch", "weight"),
        P("batch", None),
        P("batch", None),
    )
    return jax.shard_map(
        per_device, mesh=mesh, in_specs=placed, out_specs=P("batch", "weight"), check_vma=False
    )
```

```python
import math

import jax
import jax.numpy as jnp
from jax import lax
from jax.sharding import PartitionSpec as P

HEADS = 64
KV_HEADS = 8
HEAD_DIM = 128


ROPE_BASE = 500000.0
EPSILON = 1e-05

Z_CHIPS = 8


def positions_in_segment(seg_ids):
    places = jnp.arange(seg_ids.shape[0], dtype=jnp.int32)
    earlier = jnp.concatenate([seg_ids[:1] - 1, seg_ids[:-1]])
    starts = jnp.where(seg_ids != earlier, places, 0)
    leading = lax.cummax(starts, axis=0)
    return places - leading


def rotate(vectors, positions):
    half_dim = vectors.shape[-1] // 2
    ratios = jnp.arange(half_dim, dtype=jnp.float32) * (2.0 / vectors.shape[-1])
    frequency = jnp.exp(-math.log(ROPE_BASE) * ratios)
    angles = positions.astype(jnp.float32)[:, None] * frequency[None, :]
    cosine = jnp.cos(angles)[:, None, :]
    sine_part = jnp.sin(angles)[:, None, :]
    front_half = vectors[..., :half_dim]
    back_half = vectors[..., half_dim:]
    return jnp.concatenate(
        [front_half * cosine - back_half * sine_part, back_half * cosine + front_half * sine_part],
        axis=-1,
    )


def attend(grouped, rotated_keys, value_rows, seg_ids):
    scores = jnp.einsum(
        "ingd,jnd->ngij", grouped, rotated_keys, preferred_element_type=jnp.float32
    ) * grouped.shape[-1] ** (-0.5)
    places = jnp.arange(seg_ids.shape[0], dtype=jnp.int32)
    allowed = (seg_ids[:, None] == seg_ids[None, :]) & (places[None, :] <= places[:, None])
    weights = jnp.where(allowed, jnp.exp(scores), 0.0)
    probabilities = (weights / jnp.sum(weights, axis=-1, keepdims=True)).astype(jnp.bfloat16)
    mixed = jnp.einsum(
        "ngij,jnd->ingd", probabilities, value_rows, preferred_element_type=jnp.float32
    )
    return mixed.astype(jnp.bfloat16)


def ring_gather(block, axis, stride, count):
    n = lax.psum(1, axis)
    me = lax.axis_index(axis)
    here = (me // stride) % count

    def moved(step):
        pairs = []
        for src in range(n):
            k = (src // stride) % count
            pairs.append((src, src + (((k + step) % count) - k) * stride))
        return pairs

    out = jnp.zeros((count,) + block.shape, block.dtype)
    out = lax.dynamic_update_index_in_dim(out, block, here, 0)
    from_right, from_left = block, block
    for step in range(1, count // 2 + 1):
        if step < count - step:
            from_right = lax.ppermute(from_right, axis, perm=moved(-1))
            out = lax.dynamic_update_index_in_dim(out, from_right, (here + step) % count, 0)
        from_left = lax.ppermute(from_left, axis, perm=moved(1))
        out = lax.dynamic_update_index_in_dim(out, from_left, (here - step) % count, 0)
    return out


def ring_matmul(rows, block, axis, stride, count):
    n = lax.psum(1, axis)
    me = lax.axis_index(axis)
    here = (me // stride) % count
    depth = block.shape[0]

    def moved(step):
        pairs = []
        for src in range(n):
            k = (src // stride) % count
            pairs.append((src, src + (((k + step) % count) - k) * stride))
        return pairs

    def product(part, owner):
        lhs = lax.dynamic_slice_in_dim(rows, owner * depth, depth, 1)
        return jnp.dot(lhs, part, preferred_element_type=jnp.float32)

    total = product(block, here)
    from_right, from_left = block, block
    for step in range(1, count // 2 + 1):
        if step == 2:
            rows, from_right, from_left = lax.optimization_barrier((rows, from_right, from_left))
        if step < count - step:
            from_right = lax.ppermute(from_right, axis, perm=moved(-1))
            total = total + product(from_right, (here + step) % count)
        from_left = lax.ppermute(from_left, axis, perm=moved(1))
        total = total + product(from_left, (here - step) % count)
    return total


def per_device(tokens, segment_ids, norm_gain, query_weight, key_weight, value_weight):
    head_dim = HEAD_DIM
    query_cols = query_weight.shape[1]
    heads_dev = query_cols // head_dim
    group_size = HEADS // KV_HEADS
    n_weight = lax.psum(1, "weight")
    me = lax.axis_index("weight")
    core = me % 2
    first_kv = me * heads_dev // group_size
    key_block = lax.dynamic_slice_in_dim(key_weight, first_kv * head_dim, head_dim, 1)
    value_block = lax.dynamic_slice_in_dim(value_weight, first_kv * head_dim, head_dim, 1)
    kv_block = jnp.where(core == 0, key_block, value_block)
    values = tokens.astype(jnp.float32)
    inverse_rms = lax.rsqrt(jnp.mean(values * values, axis=1, keepdims=True) + EPSILON)
    normed = (values * inverse_rms * norm_gain[None, :]).astype(jnp.bfloat16)
    n_batch = lax.psum(1, "batch")
    y_hi = n_batch // Z_CHIPS
    near = ring_gather(query_weight, "batch", 1, y_hi).reshape(-1, query_cols)
    kv_full = lax.all_gather(kv_block, "batch", axis=0, tiled=True)
    gathered = lax.all_gather(normed, "weight", axis=0, tiled=True)
    pack_rows = gathered.shape[0]
    query_part = ring_matmul(gathered, near, "batch", y_hi, Z_CHIPS)
    own_rows = jnp.dot(gathered, kv_full, preferred_element_type=jnp.float32).astype(jnp.bfloat16)
    partner = [(w, w ^ 1) for w in range(n_weight)]
    other_rows = lax.ppermute(own_rows, "weight", perm=partner)
    key_rows = jnp.where(core == 0, own_rows, other_rows)
    value_rows = jnp.where(core == 0, other_rows, own_rows)
    local_kv = 1
    positions = positions_in_segment(segment_ids)
    queries = rotate(query_part.reshape(pack_rows, heads_dev, head_dim), positions).astype(
        jnp.bfloat16
    )
    rotated_keys = rotate(
        key_rows.astype(jnp.float32).reshape(pack_rows, local_kv, head_dim), positions
    ).astype(jnp.bfloat16)
    grouped = queries.reshape(pack_rows, local_kv, heads_dev // local_kv, head_dim)
    attended = attend(
        grouped, rotated_keys, value_rows.reshape(pack_rows, local_kv, head_dim), segment_ids
    )
    return attended.reshape(pack_rows, query_cols)


def solution(mesh):
    placed = (
        P(("batch", "weight"), None),
        P("batch"),
        P(),
        P("batch", "weight"),
        P("batch", None),
        P("batch", None),
    )
    return jax.shard_map(
        per_device, mesh=mesh, in_specs=placed, out_specs=P("batch", "weight"), check_vma=False
    )
```

```python
import math

import jax
import jax.numpy as jnp
from jax import lax
from jax.sharding import PartitionSpec as P

HEADS = 64
KV_HEADS = 8
HEAD_DIM = 128


ROPE_BASE = 500000.0
EPSILON = 1e-05

Z_CHIPS = 8


def positions_in_segment(seg_ids):
    places = jnp.arange(seg_ids.shape[0], dtype=jnp.int32)
    earlier = jnp.concatenate([seg_ids[:1] - 1, seg_ids[:-1]])
    starts = jnp.where(seg_ids != earlier, places, 0)
    leading = lax.cummax(starts, axis=0)
    return places - leading


def rotate(vectors, positions):
    half_dim = vectors.shape[-1] // 2
    ratios = jnp.arange(half_dim, dtype=jnp.float32) * (2.0 / vectors.shape[-1])
    frequency = jnp.exp(-math.log(ROPE_BASE) * ratios)
    angles = positions.astype(jnp.float32)[:, None] * frequency[None, :]
    cosine = jnp.cos(angles)[:, None, :]
    sine_part = jnp.sin(angles)[:, None, :]
    front_half = vectors[..., :half_dim]
    back_half = vectors[..., half_dim:]
    return jnp.concatenate(
        [front_half * cosine - back_half * sine_part, back_half * cosine + front_half * sine_part],
        axis=-1,
    )


def attend(grouped, rotated_keys, value_rows, seg_ids):
    scores = jnp.einsum(
        "ingd,jnd->ngij", grouped, rotated_keys, preferred_element_type=jnp.float32
    ) * grouped.shape[-1] ** (-0.5)
    places = jnp.arange(seg_ids.shape[0], dtype=jnp.int32)
    allowed = (seg_ids[:, None] == seg_ids[None, :]) & (places[None, :] <= places[:, None])
    weights = jnp.where(allowed, jnp.exp(scores), 0.0)
    probabilities = (weights / jnp.sum(weights, axis=-1, keepdims=True)).astype(jnp.bfloat16)
    mixed = jnp.einsum(
        "ngij,jnd->ingd", probabilities, value_rows, preferred_element_type=jnp.float32
    )
    return mixed.astype(jnp.bfloat16)


def ring_gather(block, axis, stride, count):
    n = lax.psum(1, axis)
    me = lax.axis_index(axis)
    here = (me // stride) % count

    def moved(step):
        pairs = []
        for src in range(n):
            k = (src // stride) % count
            pairs.append((src, src + (((k + step) % count) - k) * stride))
        return pairs

    out = jnp.zeros((count,) + block.shape, block.dtype)
    out = lax.dynamic_update_index_in_dim(out, block, here, 0)
    from_right, from_left = block, block
    for step in range(1, count // 2 + 1):
        if step < count - step:
            from_right = lax.ppermute(from_right, axis, perm=moved(-1))
            out = lax.dynamic_update_index_in_dim(out, from_right, (here + step) % count, 0)
        from_left = lax.ppermute(from_left, axis, perm=moved(1))
        out = lax.dynamic_update_index_in_dim(out, from_left, (here - step) % count, 0)
    return out


def ring_matmul(rows, block, axis, stride, count):
    n = lax.psum(1, axis)
    me = lax.axis_index(axis)
    here = (me // stride) % count
    depth = block.shape[0]

    def moved(step):
        pairs = []
        for src in range(n):
            k = (src // stride) % count
            pairs.append((src, src + (((k + step) % count) - k) * stride))
        return pairs

    def product(part, owner):
        lhs = lax.dynamic_slice_in_dim(rows, owner * depth, depth, 1)
        return jnp.dot(lhs, part, preferred_element_type=jnp.float32)

    total = product(block, here)
    from_right, from_left = block, block
    for step in range(1, count // 2 + 1):
        if step == 2:
            rows, from_right, from_left = lax.optimization_barrier((rows, from_right, from_left))
        if step < count - step:
            from_right = lax.ppermute(from_right, axis, perm=moved(-1))
            total = total + product(from_right, (here + step) % count)
        from_left = lax.ppermute(from_left, axis, perm=moved(1))
        total = total + product(from_left, (here - step) % count)
    return total


def per_device(tokens, segment_ids, norm_gain, query_weight, key_weight, value_weight):
    head_dim = HEAD_DIM
    query_cols = query_weight.shape[1]
    heads_dev = query_cols // head_dim
    group_size = HEADS // KV_HEADS
    n_weight = lax.psum(1, "weight")
    me = lax.axis_index("weight")
    core = me % 2
    first_kv = me * heads_dev // group_size
    key_block = lax.dynamic_slice_in_dim(key_weight, first_kv * head_dim, head_dim, 1)
    value_block = lax.dynamic_slice_in_dim(value_weight, first_kv * head_dim, head_dim, 1)
    kv_block = jnp.where(core == 0, key_block, value_block)
    values = tokens.astype(jnp.float32)
    inverse_rms = lax.rsqrt(jnp.mean(values * values, axis=1, keepdims=True) + EPSILON)
    normed = (values * inverse_rms * norm_gain[None, :]).astype(jnp.bfloat16)
    local_weights = jnp.concatenate([query_weight, kv_block], axis=1)
    n_batch = lax.psum(1, "batch")
    y_hi = n_batch // Z_CHIPS
    split = (local_weights.shape[1] // 2 + 127) // 128 * 128
    gathered = lax.all_gather(normed, "weight", axis=0, tiled=True)
    pack_rows = gathered.shape[0]
    first, second = local_weights[:, :split], local_weights[:, split:]
    near_first = ring_gather(first, "batch", 1, y_hi).reshape(-1, first.shape[1])
    near_first, second = lax.optimization_barrier((near_first, second))
    near_second = ring_gather(second, "batch", 1, y_hi).reshape(-1, second.shape[1])
    parts = [ring_matmul(gathered, near, "batch", y_hi, Z_CHIPS) for near in (near_first, near_second)]
    projected = jnp.concatenate(parts, axis=1)
    query_part = projected[:, :query_cols]
    own_rows = projected[:, query_cols:].astype(jnp.bfloat16)
    partner = [(w, w ^ 1) for w in range(n_weight)]
    other_rows = lax.ppermute(own_rows, "weight", perm=partner)
    key_rows = jnp.where(core == 0, own_rows, other_rows)
    value_rows = jnp.where(core == 0, other_rows, own_rows)
    local_kv = 1
    positions = positions_in_segment(segment_ids)
    queries = rotate(query_part.reshape(pack_rows, heads_dev, head_dim), positions).astype(
        jnp.bfloat16
    )
    rotated_keys = rotate(
        key_rows.astype(jnp.float32).reshape(pack_rows, local_kv, head_dim), positions
    ).astype(jnp.bfloat16)
    grouped = queries.reshape(pack_rows, local_kv, heads_dev // local_kv, head_dim)
    attended = attend(
        grouped, rotated_keys, value_rows.reshape(pack_rows, local_kv, head_dim), segment_ids
    )
    return attended.reshape(pack_rows, query_cols)


def solution(mesh):
    placed = (
        P(("batch", "weight"), None),
        P("batch"),
        P(),
        P("batch", "weight"),
        P("batch", None),
        P("batch", None),
    )
    return jax.shard_map(
        per_device, mesh=mesh, in_specs=placed, out_specs=P("batch", "weight"), check_vma=False
    )
```

```python
import functools
import math

import jax
import jax.numpy as jnp
from jax import lax
from jax.experimental import pallas as pl
from jax.experimental.pallas import tpu as pltpu
from jax.sharding import PartitionSpec as P

HEADS = 64
KV_HEADS = 8
HEAD_DIM = 128


ROPE_BASE = 500000.0
EPSILON = 1e-05

Z_CHIPS = 8


def positions_in_segment(seg_ids):
    places = jnp.arange(seg_ids.shape[0], dtype=jnp.int32)
    earlier = jnp.concatenate([seg_ids[:1] - 1, seg_ids[:-1]])
    starts = jnp.where(seg_ids != earlier, places, 0)
    leading = lax.cummax(starts, axis=0)
    return places - leading


def rotate(vectors, positions):
    half_dim = vectors.shape[-1] // 2
    ratios = jnp.arange(half_dim, dtype=jnp.float32) * (2.0 / vectors.shape[-1])
    frequency = jnp.exp(-math.log(ROPE_BASE) * ratios)
    angles = positions.astype(jnp.float32)[:, None] * frequency[None, :]
    cosine = jnp.cos(angles)[:, None, :]
    sine_part = jnp.sin(angles)[:, None, :]
    front_half = vectors[..., :half_dim]
    back_half = vectors[..., half_dim:]
    return jnp.concatenate(
        [front_half * cosine - back_half * sine_part, back_half * cosine + front_half * sine_part],
        axis=-1,
    )


def attend(grouped, rotated_keys, value_rows, seg_ids):
    scores = jnp.einsum(
        "ingd,jnd->ngij", grouped, rotated_keys, preferred_element_type=jnp.float32
    ) * grouped.shape[-1] ** (-0.5)
    places = jnp.arange(seg_ids.shape[0], dtype=jnp.int32)
    allowed = (seg_ids[:, None] == seg_ids[None, :]) & (places[None, :] <= places[:, None])
    weights = jnp.where(allowed, jnp.exp(scores), 0.0)
    probabilities = (weights / jnp.sum(weights, axis=-1, keepdims=True)).astype(jnp.bfloat16)
    mixed = jnp.einsum(
        "ngij,jnd->ingd", probabilities, value_rows, preferred_element_type=jnp.float32
    )
    return mixed.astype(jnp.bfloat16)


def attention_kernel(heads, q_ref, k_ref, v_ref, cos_ref, sin_ref, row_seg_ref, col_seg_ref, o_ref):
    half = HEAD_DIM // 2
    cosine, sine = cos_ref[...], sin_ref[...]

    def rope(x):
        a, b = x[:, :half], x[:, half:]
        return jnp.concatenate([a * cosine - b * sine, b * cosine + a * sine], axis=1)

    keys = rope(k_ref[...].astype(jnp.float32)).astype(jnp.bfloat16)
    values = v_ref[...]
    rows = q_ref.shape[0]
    places_i = lax.broadcasted_iota(jnp.int32, (rows, rows), 0)
    places_j = lax.broadcasted_iota(jnp.int32, (rows, rows), 1)
    allowed = (row_seg_ref[...] == col_seg_ref[...]) & (places_j <= places_i)
    scale = HEAD_DIM ** (-0.5)
    for h in range(heads):
        cols = slice(h * HEAD_DIM, (h + 1) * HEAD_DIM)
        query = rope(q_ref[:, cols]).astype(jnp.bfloat16)
        scores = lax.dot_general(
            query, keys, (((1,), (1,)), ((), ())), preferred_element_type=jnp.float32
        ) * scale
        weights = jnp.where(allowed, jnp.exp(scores), 0.0)
        probabilities = (weights / jnp.sum(weights, axis=1, keepdims=True)).astype(jnp.bfloat16)
        mixed = jnp.dot(probabilities, values, preferred_element_type=jnp.float32)
        o_ref[:, cols] = mixed.astype(o_ref.dtype)


def rope_tables(positions):
    half_dim = HEAD_DIM // 2
    ratios = jnp.arange(half_dim, dtype=jnp.float32) * (2.0 / HEAD_DIM)
    frequency = jnp.exp(-math.log(ROPE_BASE) * ratios)
    angles = positions.astype(jnp.float32)[:, None] * frequency[None, :]
    return jnp.cos(angles), jnp.sin(angles)


def attention_kernel_call(projected, cols, key_rows, value_rows, cosine, sine, seg_ids):
    rows = projected.shape[0]
    half_dim = HEAD_DIM // 2
    vmem = pl.BlockSpec(memory_space=pltpu.VMEM)
    heads = cols // HEAD_DIM
    return pl.pallas_call(
        functools.partial(attention_kernel, heads),
        out_shape=jax.ShapeDtypeStruct((rows, cols), jnp.bfloat16),
        in_specs=[vmem] * 7,
        out_specs=vmem,
        cost_estimate=pl.CostEstimate(
            flops=4 * rows * rows * cols + 8 * rows * cols,
            transcendentals=heads * rows * rows,
            bytes_accessed=rows * cols * 6 + rows * HEAD_DIM * 4 + rows * half_dim * 8,
        ),
    )(
        projected,
        key_rows,
        value_rows,
        cosine,
        sine,
        seg_ids[:, None],
        seg_ids[None, :],
    )


def ring_gather(block, axis, stride, count):
    n = lax.psum(1, axis)
    me = lax.axis_index(axis)
    here = (me // stride) % count

    def moved(step):
        pairs = []
        for src in range(n):
            k = (src // stride) % count
            pairs.append((src, src + (((k + step) % count) - k) * stride))
        return pairs

    out = jnp.zeros((count,) + block.shape, block.dtype)
    out = lax.dynamic_update_index_in_dim(out, block, here, 0)
    from_right, from_left = block, block
    for step in range(1, count // 2 + 1):
        if step < count - step:
            from_right = lax.ppermute(from_right, axis, perm=moved(-1))
            out = lax.dynamic_update_index_in_dim(out, from_right, (here + step) % count, 0)
        from_left = lax.ppermute(from_left, axis, perm=moved(1))
        out = lax.dynamic_update_index_in_dim(out, from_left, (here - step) % count, 0)
    return out


def ring_matmul(rows, block, axis, stride, count):
    n = lax.psum(1, axis)
    me = lax.axis_index(axis)
    here = (me // stride) % count
    depth = block.shape[0]

    def moved(step):
        pairs = []
        for src in range(n):
            k = (src // stride) % count
            pairs.append((src, src + (((k + step) % count) - k) * stride))
        return pairs

    def product(part, owner):
        lhs = lax.dynamic_slice_in_dim(rows, owner * depth, depth, 1)
        return jnp.dot(lhs, part, preferred_element_type=jnp.float32)

    total = product(block, here)
    from_right, from_left = block, block
    for step in range(1, count // 2 + 1):
        if step == 2:
            rows, from_right, from_left = lax.optimization_barrier((rows, from_right, from_left))
        if step < count - step:
            from_right = lax.ppermute(from_right, axis, perm=moved(-1))
            total = total + product(from_right, (here + step) % count)
        from_left = lax.ppermute(from_left, axis, perm=moved(1))
        total = total + product(from_left, (here - step) % count)
    return total


def per_device(tokens, segment_ids, norm_gain, query_weight, key_weight, value_weight):
    head_dim = HEAD_DIM
    query_cols = query_weight.shape[1]
    heads_dev = query_cols // head_dim
    group_size = HEADS // KV_HEADS
    n_weight = lax.psum(1, "weight")
    me = lax.axis_index("weight")
    core = me % 2
    first_kv = me * heads_dev // group_size
    key_block = lax.dynamic_slice_in_dim(key_weight, first_kv * head_dim, head_dim, 1)
    value_block = lax.dynamic_slice_in_dim(value_weight, first_kv * head_dim, head_dim, 1)
    kv_block = jnp.where(core == 0, key_block, value_block)
    values = tokens.astype(jnp.float32)
    inverse_rms = lax.rsqrt(jnp.mean(values * values, axis=1, keepdims=True) + EPSILON)
    normed = (values * inverse_rms * norm_gain[None, :]).astype(jnp.bfloat16)
    local_weights = jnp.concatenate([query_weight, kv_block], axis=1)
    n_batch = lax.psum(1, "batch")
    y_hi = n_batch // Z_CHIPS
    near = ring_gather(local_weights, "batch", 1, y_hi)
    near = near.reshape(-1, local_weights.shape[1])
    cosine, sine = rope_tables(positions_in_segment(segment_ids))
    near, cosine, sine = lax.optimization_barrier((near, cosine, sine))
    gathered = lax.all_gather(normed, "weight", axis=0, tiled=True)
    pack_rows = gathered.shape[0]
    projected = ring_matmul(gathered, near, "batch", y_hi, Z_CHIPS)
    own_rows = projected[:, query_cols:].astype(jnp.bfloat16)
    partner = [(w, w ^ 1) for w in range(n_weight)]
    other_rows = lax.ppermute(own_rows, "weight", perm=partner)
    key_rows = jnp.where(core == 0, own_rows, other_rows)
    value_rows = jnp.where(core == 0, other_rows, own_rows)
    return attention_kernel_call(
        projected, query_cols, key_rows, value_rows, cosine, sine, segment_ids
    )


def solution(mesh):
    placed = (
        P(("batch", "weight"), None),
        P("batch"),
        P(),
        P("batch", "weight"),
        P("batch", None),
        P("batch", None),
    )
    return jax.shard_map(
        per_device, mesh=mesh, in_specs=placed, out_specs=P("batch", "weight"), check_vma=False
    )
```

```python
import functools
import math

import jax
import jax.numpy as jnp
from jax import lax
from jax.experimental import pallas as pl
from jax.experimental.pallas import tpu as pltpu
from jax.sharding import PartitionSpec as P

HEADS = 64
KV_HEADS = 8
HEAD_DIM = 128


ROPE_BASE = 500000.0
EPSILON = 1e-05

Z_CHIPS = 8


def positions_in_segment(seg_ids):
    places = jnp.arange(seg_ids.shape[0], dtype=jnp.int32)
    earlier = jnp.concatenate([seg_ids[:1] - 1, seg_ids[:-1]])
    starts = jnp.where(seg_ids != earlier, places, 0)
    leading = lax.cummax(starts, axis=0)
    return places - leading


def rotate(vectors, positions):
    half_dim = vectors.shape[-1] // 2
    ratios = jnp.arange(half_dim, dtype=jnp.float32) * (2.0 / vectors.shape[-1])
    frequency = jnp.exp(-math.log(ROPE_BASE) * ratios)
    angles = positions.astype(jnp.float32)[:, None] * frequency[None, :]
    cosine = jnp.cos(angles)[:, None, :]
    sine_part = jnp.sin(angles)[:, None, :]
    front_half = vectors[..., :half_dim]
    back_half = vectors[..., half_dim:]
    return jnp.concatenate(
        [front_half * cosine - back_half * sine_part, back_half * cosine + front_half * sine_part],
        axis=-1,
    )


def attend(grouped, rotated_keys, value_rows, seg_ids):
    scores = jnp.einsum(
        "ingd,jnd->ngij", grouped, rotated_keys, preferred_element_type=jnp.float32
    ) * grouped.shape[-1] ** (-0.5)
    places = jnp.arange(seg_ids.shape[0], dtype=jnp.int32)
    allowed = (seg_ids[:, None] == seg_ids[None, :]) & (places[None, :] <= places[:, None])
    weights = jnp.where(allowed, jnp.exp(scores), 0.0)
    probabilities = (weights / jnp.sum(weights, axis=-1, keepdims=True)).astype(jnp.bfloat16)
    mixed = jnp.einsum(
        "ngij,jnd->ingd", probabilities, value_rows, preferred_element_type=jnp.float32
    )
    return mixed.astype(jnp.bfloat16)


ROW_TILE = 128
SEGMENT_MOST = 64


def attention_kernel(heads, q_ref, k_ref, v_ref, cos_ref, sin_ref, row_seg_ref, col_seg_ref, o_ref):
    half = HEAD_DIM // 2

    def rope(x, rows):
        cosine, sine = cos_ref[rows, :], sin_ref[rows, :]
        a, b = x[:, :half], x[:, half:]
        return jnp.concatenate([a * cosine - b * sine, b * cosine + a * sine], axis=1)

    n_rows = q_ref.shape[0]
    keys = rope(k_ref[...].astype(jnp.float32), slice(0, n_rows)).astype(jnp.bfloat16)
    scale = HEAD_DIM ** (-0.5)
    reach = max(ROW_TILE, SEGMENT_MOST)
    for r0 in range(0, n_rows, ROW_TILE):
        c0 = max(0, r0 - reach)
        c1 = r0 + ROW_TILE
        rows = slice(r0, c1)
        places_i = lax.broadcasted_iota(jnp.int32, (ROW_TILE, c1 - c0), 0) + r0
        places_j = lax.broadcasted_iota(jnp.int32, (ROW_TILE, c1 - c0), 1) + c0
        allowed = (row_seg_ref[rows, :] == col_seg_ref[:, c0:c1]) & (places_j <= places_i)
        window_keys = keys[c0:c1]
        window_values = v_ref[c0:c1, :]
        for h in range(heads):
            cols = slice(h * HEAD_DIM, (h + 1) * HEAD_DIM)
            query = rope(q_ref[rows, cols], rows).astype(jnp.bfloat16)
            scores = lax.dot_general(
                query, window_keys, (((1,), (1,)), ((), ())), preferred_element_type=jnp.float32
            ) * scale
            weights = jnp.where(allowed, jnp.exp(scores), 0.0)
            total = jnp.sum(weights, axis=1, keepdims=True)
            probabilities = (weights / total).astype(jnp.bfloat16)
            mixed = jnp.dot(probabilities, window_values, preferred_element_type=jnp.float32)
            o_ref[rows, cols] = mixed.astype(o_ref.dtype)


def rope_tables(positions):
    half_dim = HEAD_DIM // 2
    ratios = jnp.arange(half_dim, dtype=jnp.float32) * (2.0 / HEAD_DIM)
    frequency = jnp.exp(-math.log(ROPE_BASE) * ratios)
    angles = positions.astype(jnp.float32)[:, None] * frequency[None, :]
    return jnp.cos(angles), jnp.sin(angles)


def attention_kernel_call(projected, cols, key_rows, value_rows, cosine, sine, seg_ids):
    rows = projected.shape[0]
    half_dim = HEAD_DIM // 2
    vmem = pl.BlockSpec(memory_space=pltpu.VMEM)
    heads = cols // HEAD_DIM
    return pl.pallas_call(
        functools.partial(attention_kernel, heads),
        out_shape=jax.ShapeDtypeStruct((rows, cols), jnp.bfloat16),
        in_specs=[vmem] * 7,
        out_specs=vmem,
        cost_estimate=pl.CostEstimate(
            flops=4 * rows * rows * cols + 8 * rows * cols,
            transcendentals=heads * rows * rows,
            bytes_accessed=rows * cols * 6 + rows * HEAD_DIM * 4 + rows * half_dim * 8,
        ),
    )(
        projected,
        key_rows,
        value_rows,
        cosine,
        sine,
        seg_ids[:, None],
        seg_ids[None, :],
    )


def ring_gather(block, axis, stride, count):
    n = lax.psum(1, axis)
    me = lax.axis_index(axis)
    here = (me // stride) % count

    def moved(step):
        pairs = []
        for src in range(n):
            k = (src // stride) % count
            pairs.append((src, src + (((k + step) % count) - k) * stride))
        return pairs

    out = jnp.zeros((count,) + block.shape, block.dtype)
    out = lax.dynamic_update_index_in_dim(out, block, here, 0)
    from_right, from_left = block, block
    for step in range(1, count // 2 + 1):
        if step < count - step:
            from_right = lax.ppermute(from_right, axis, perm=moved(-1))
            out = lax.dynamic_update_index_in_dim(out, from_right, (here + step) % count, 0)
        from_left = lax.ppermute(from_left, axis, perm=moved(1))
        out = lax.dynamic_update_index_in_dim(out, from_left, (here - step) % count, 0)
    return out


def ring_matmul(rows, block, axis, stride, count):
    n = lax.psum(1, axis)
    me = lax.axis_index(axis)
    here = (me // stride) % count
    depth = block.shape[0]

    def moved(step):
        pairs = []
        for src in range(n):
            k = (src // stride) % count
            pairs.append((src, src + (((k + step) % count) - k) * stride))
        return pairs

    def product(part, owner):
        lhs = lax.dynamic_slice_in_dim(rows, owner * depth, depth, 1)
        return jnp.dot(lhs, part, preferred_element_type=jnp.float32)

    total = product(block, here)
    from_right, from_left = block, block
    for step in range(1, count // 2 + 1):
        if step == 2:
            rows, from_right, from_left = lax.optimization_barrier((rows, from_right, from_left))
        if step < count - step:
            from_right = lax.ppermute(from_right, axis, perm=moved(-1))
            total = total + product(from_right, (here + step) % count)
        from_left = lax.ppermute(from_left, axis, perm=moved(1))
        total = total + product(from_left, (here - step) % count)
    return total


def per_device(tokens, segment_ids, norm_gain, query_weight, key_weight, value_weight):
    head_dim = HEAD_DIM
    query_cols = query_weight.shape[1]
    heads_dev = query_cols // head_dim
    group_size = HEADS // KV_HEADS
    n_weight = lax.psum(1, "weight")
    me = lax.axis_index("weight")
    core = me % 2
    first_kv = me * heads_dev // group_size
    key_block = lax.dynamic_slice_in_dim(key_weight, first_kv * head_dim, head_dim, 1)
    value_block = lax.dynamic_slice_in_dim(value_weight, first_kv * head_dim, head_dim, 1)
    kv_block = jnp.where(core == 0, key_block, value_block)
    values = tokens.astype(jnp.float32)
    inverse_rms = lax.rsqrt(jnp.mean(values * values, axis=1, keepdims=True) + EPSILON)
    normed = (values * inverse_rms * norm_gain[None, :]).astype(jnp.bfloat16)
    local_weights = jnp.concatenate([query_weight, kv_block], axis=1)
    n_batch = lax.psum(1, "batch")
    y_hi = n_batch // Z_CHIPS
    near = ring_gather(local_weights, "batch", 1, y_hi)
    near = near.reshape(-1, local_weights.shape[1])
    cosine, sine = rope_tables(positions_in_segment(segment_ids))
    near, cosine, sine = lax.optimization_barrier((near, cosine, sine))
    gathered = lax.all_gather(normed, "weight", axis=0, tiled=True)
    pack_rows = gathered.shape[0]
    projected = ring_matmul(gathered, near, "batch", y_hi, Z_CHIPS)
    own_rows = projected[:, query_cols:].astype(jnp.bfloat16)
    partner = [(w, w ^ 1) for w in range(n_weight)]
    other_rows = lax.ppermute(own_rows, "weight", perm=partner)
    key_rows = jnp.where(core == 0, own_rows, other_rows)
    value_rows = jnp.where(core == 0, other_rows, own_rows)
    return attention_kernel_call(
        projected, query_cols, key_rows, value_rows, cosine, sine, segment_ids
    )


def solution(mesh):
    placed = (
        P(("batch", "weight"), None),
        P("batch"),
        P(),
        P("batch", "weight"),
        P("batch", None),
        P("batch", None),
    )
    return jax.shard_map(
        per_device, mesh=mesh, in_specs=placed, out_specs=P("batch", "weight"), check_vma=False
    )
```

```python
import functools
import math

import jax
import jax.numpy as jnp
from jax import lax
from jax.experimental import pallas as pl
from jax.experimental.pallas import tpu as pltpu
from jax.sharding import PartitionSpec as P

HEADS = 64
KV_HEADS = 8
HEAD_DIM = 128


ROPE_BASE = 500000.0
EPSILON = 1e-05

Z_CHIPS = 8


def positions_in_segment(seg_ids):
    places = jnp.arange(seg_ids.shape[0], dtype=jnp.int32)
    earlier = jnp.concatenate([seg_ids[:1] - 1, seg_ids[:-1]])
    starts = jnp.where(seg_ids != earlier, places, 0)
    leading = lax.cummax(starts, axis=0)
    return places - leading


def rotate(vectors, positions):
    half_dim = vectors.shape[-1] // 2
    ratios = jnp.arange(half_dim, dtype=jnp.float32) * (2.0 / vectors.shape[-1])
    frequency = jnp.exp(-math.log(ROPE_BASE) * ratios)
    angles = positions.astype(jnp.float32)[:, None] * frequency[None, :]
    cosine = jnp.cos(angles)[:, None, :]
    sine_part = jnp.sin(angles)[:, None, :]
    front_half = vectors[..., :half_dim]
    back_half = vectors[..., half_dim:]
    return jnp.concatenate(
        [front_half * cosine - back_half * sine_part, back_half * cosine + front_half * sine_part],
        axis=-1,
    )


def attend(grouped, rotated_keys, value_rows, seg_ids):
    scores = jnp.einsum(
        "ingd,jnd->ngij", grouped, rotated_keys, preferred_element_type=jnp.float32
    ) * grouped.shape[-1] ** (-0.5)
    places = jnp.arange(seg_ids.shape[0], dtype=jnp.int32)
    allowed = (seg_ids[:, None] == seg_ids[None, :]) & (places[None, :] <= places[:, None])
    weights = jnp.where(allowed, jnp.exp(scores), 0.0)
    probabilities = (weights / jnp.sum(weights, axis=-1, keepdims=True)).astype(jnp.bfloat16)
    mixed = jnp.einsum(
        "ngij,jnd->ingd", probabilities, value_rows, preferred_element_type=jnp.float32
    )
    return mixed.astype(jnp.bfloat16)


ROW_TILE = 64
SEGMENT_MOST = 64


def attention_kernel(heads, q_ref, k_ref, v_ref, cos_ref, sin_ref, row_seg_ref, col_seg_ref, o_ref):
    half = HEAD_DIM // 2

    def rope(x, rows):
        cosine, sine = cos_ref[rows, :], sin_ref[rows, :]
        a, b = x[:, :half], x[:, half:]
        return jnp.concatenate([a * cosine - b * sine, b * cosine + a * sine], axis=1)

    n_rows = q_ref.shape[0]
    keys = rope(k_ref[...].astype(jnp.float32), slice(0, n_rows)).astype(jnp.bfloat16)
    scale = HEAD_DIM ** (-0.5)
    reach = max(ROW_TILE, SEGMENT_MOST)
    for r0 in range(0, n_rows, ROW_TILE):
        c0 = max(0, r0 - reach)
        c1 = r0 + ROW_TILE
        rows = slice(r0, c1)
        places_i = lax.broadcasted_iota(jnp.int32, (ROW_TILE, c1 - c0), 0) + r0
        places_j = lax.broadcasted_iota(jnp.int32, (ROW_TILE, c1 - c0), 1) + c0
        allowed = (row_seg_ref[rows, :] == col_seg_ref[:, c0:c1]) & (places_j <= places_i)
        allowed = jnp.concatenate([allowed] * heads, axis=0)
        query = jnp.concatenate(
            [rope(q_ref[rows, h * HEAD_DIM : (h + 1) * HEAD_DIM], rows) for h in range(heads)],
            axis=0,
        ).astype(jnp.bfloat16)
        scores = lax.dot_general(
            query, keys[c0:c1], (((1,), (1,)), ((), ())), preferred_element_type=jnp.float32
        ) * scale
        weights = jnp.where(allowed, jnp.exp(scores), 0.0)
        total = jnp.sum(weights, axis=1, keepdims=True)
        probabilities = (weights / total).astype(jnp.bfloat16)
        mixed = jnp.dot(probabilities, v_ref[c0:c1, :], preferred_element_type=jnp.float32)
        for h in range(heads):
            o_ref[rows, h * HEAD_DIM : (h + 1) * HEAD_DIM] = mixed[
                h * ROW_TILE : (h + 1) * ROW_TILE
            ].astype(o_ref.dtype)


def rope_tables(positions):
    half_dim = HEAD_DIM // 2
    ratios = jnp.arange(half_dim, dtype=jnp.float32) * (2.0 / HEAD_DIM)
    frequency = jnp.exp(-math.log(ROPE_BASE) * ratios)
    angles = positions.astype(jnp.float32)[:, None] * frequency[None, :]
    return jnp.cos(angles), jnp.sin(angles)


def attention_kernel_call(projected, cols, key_rows, value_rows, cosine, sine, row_seg, col_seg):
    rows = projected.shape[0]
    half_dim = HEAD_DIM // 2
    vmem = pl.BlockSpec(memory_space=pltpu.VMEM)
    heads = cols // HEAD_DIM
    return pl.pallas_call(
        functools.partial(attention_kernel, heads),
        out_shape=jax.ShapeDtypeStruct((rows, cols), jnp.bfloat16),
        in_specs=[vmem] * 7,
        out_specs=vmem,
        cost_estimate=pl.CostEstimate(
            flops=4 * rows * rows * cols + 8 * rows * cols,
            transcendentals=heads * rows * rows,
            bytes_accessed=rows * cols * 6 + rows * HEAD_DIM * 4 + rows * half_dim * 8,
        ),
    )(
        projected,
        key_rows,
        value_rows,
        cosine,
        sine,
        row_seg,
        col_seg,
    )


def ring_gather(block, axis, stride, count):
    n = lax.psum(1, axis)
    me = lax.axis_index(axis)
    here = (me // stride) % count

    def moved(step):
        pairs = []
        for src in range(n):
            k = (src // stride) % count
            pairs.append((src, src + (((k + step) % count) - k) * stride))
        return pairs

    out = jnp.zeros((count,) + block.shape, block.dtype)
    out = lax.dynamic_update_index_in_dim(out, block, here, 0)
    from_right, from_left = block, block
    for step in range(1, count // 2 + 1):
        if step < count - step:
            from_right = lax.ppermute(from_right, axis, perm=moved(-1))
            out = lax.dynamic_update_index_in_dim(out, from_right, (here + step) % count, 0)
        from_left = lax.ppermute(from_left, axis, perm=moved(1))
        out = lax.dynamic_update_index_in_dim(out, from_left, (here - step) % count, 0)
    return out


def ring_matmul(rows, block, axis, stride, count):
    n = lax.psum(1, axis)
    me = lax.axis_index(axis)
    here = (me // stride) % count
    depth = block.shape[0]

    def moved(step):
        pairs = []
        for src in range(n):
            k = (src // stride) % count
            pairs.append((src, src + (((k + step) % count) - k) * stride))
        return pairs

    def product(part, owner):
        lhs = lax.dynamic_slice_in_dim(rows, owner * depth, depth, 1)
        return jnp.dot(lhs, part, preferred_element_type=jnp.float32)

    total = product(block, here)
    from_right, from_left = block, block
    for step in range(1, count // 2 + 1):
        if step == 2:
            rows, from_right, from_left = lax.optimization_barrier((rows, from_right, from_left))
        if step < count - step:
            from_right = lax.ppermute(from_right, axis, perm=moved(-1))
            total = total + product(from_right, (here + step) % count)
        from_left = lax.ppermute(from_left, axis, perm=moved(1))
        total = total + product(from_left, (here - step) % count)
    return total


def per_device(tokens, segment_ids, norm_gain, query_weight, key_weight, value_weight):
    head_dim = HEAD_DIM
    query_cols = query_weight.shape[1]
    heads_dev = query_cols // head_dim
    group_size = HEADS // KV_HEADS
    n_weight = lax.psum(1, "weight")
    me = lax.axis_index("weight")
    core = me % 2
    first_kv = me * heads_dev // group_size
    key_block = lax.dynamic_slice_in_dim(key_weight, first_kv * head_dim, head_dim, 1)
    value_block = lax.dynamic_slice_in_dim(value_weight, first_kv * head_dim, head_dim, 1)
    kv_block = jnp.where(core == 0, key_block, value_block)
    values = tokens.astype(jnp.float32)
    inverse_rms = lax.rsqrt(jnp.mean(values * values, axis=1, keepdims=True) + EPSILON)
    normed = (values * inverse_rms * norm_gain[None, :]).astype(jnp.bfloat16)
    local_weights = jnp.concatenate([query_weight, kv_block], axis=1)
    n_batch = lax.psum(1, "batch")
    y_hi = n_batch // Z_CHIPS
    near = ring_gather(local_weights, "batch", 1, y_hi)
    near = near.reshape(-1, local_weights.shape[1])
    cosine, sine = rope_tables(positions_in_segment(segment_ids))
    row_seg, col_seg = segment_ids[:, None], segment_ids[None, :]
    near, cosine, sine, row_seg, col_seg = lax.optimization_barrier(
        (near, cosine, sine, row_seg, col_seg)
    )
    gathered = lax.all_gather(normed, "weight", axis=0, tiled=True)
    pack_rows = gathered.shape[0]
    projected = ring_matmul(gathered, near, "batch", y_hi, Z_CHIPS)
    own_rows = projected[:, query_cols:].astype(jnp.bfloat16)
    partner = [(w, w ^ 1) for w in range(n_weight)]
    other_rows = lax.ppermute(own_rows, "weight", perm=partner)
    key_rows = jnp.where(core == 0, own_rows, other_rows)
    value_rows = jnp.where(core == 0, other_rows, own_rows)
    return attention_kernel_call(
        projected, query_cols, key_rows, value_rows, cosine, sine, row_seg, col_seg
    )


def solution(mesh):
    placed = (
        P(("batch", "weight"), None),
        P("batch"),
        P(),
        P("batch", "weight"),
        P("batch", None),
        P("batch", None),
    )
    return jax.shard_map(
        per_device, mesh=mesh, in_specs=placed, out_specs=P("batch", "weight"), check_vma=False
    )
```

```python
import functools
import math

import jax
import jax.numpy as jnp
from jax import lax
from jax.experimental import pallas as pl
from jax.experimental.pallas import tpu as pltpu
from jax.sharding import PartitionSpec as P

HEADS = 64
KV_HEADS = 8
HEAD_DIM = 128


ROPE_BASE = 500000.0
EPSILON = 1e-05

Z_CHIPS = 8


def positions_in_segment(seg_ids):
    places = jnp.arange(seg_ids.shape[0], dtype=jnp.int32)
    earlier = jnp.concatenate([seg_ids[:1] - 1, seg_ids[:-1]])
    starts = jnp.where(seg_ids != earlier, places, 0)
    leading = lax.cummax(starts, axis=0)
    return places - leading


def rotate(vectors, positions):
    half_dim = vectors.shape[-1] // 2
    ratios = jnp.arange(half_dim, dtype=jnp.float32) * (2.0 / vectors.shape[-1])
    frequency = jnp.exp(-math.log(ROPE_BASE) * ratios)
    angles = positions.astype(jnp.float32)[:, None] * frequency[None, :]
    cosine = jnp.cos(angles)[:, None, :]
    sine_part = jnp.sin(angles)[:, None, :]
    front_half = vectors[..., :half_dim]
    back_half = vectors[..., half_dim:]
    return jnp.concatenate(
        [front_half * cosine - back_half * sine_part, back_half * cosine + front_half * sine_part],
        axis=-1,
    )


def attend(grouped, rotated_keys, value_rows, seg_ids):
    scores = jnp.einsum(
        "ingd,jnd->ngij", grouped, rotated_keys, preferred_element_type=jnp.float32
    ) * grouped.shape[-1] ** (-0.5)
    places = jnp.arange(seg_ids.shape[0], dtype=jnp.int32)
    allowed = (seg_ids[:, None] == seg_ids[None, :]) & (places[None, :] <= places[:, None])
    weights = jnp.where(allowed, jnp.exp(scores), 0.0)
    probabilities = (weights / jnp.sum(weights, axis=-1, keepdims=True)).astype(jnp.bfloat16)
    mixed = jnp.einsum(
        "ngij,jnd->ingd", probabilities, value_rows, preferred_element_type=jnp.float32
    )
    return mixed.astype(jnp.bfloat16)


ROW_TILE = 64
SEGMENT_MOST = 64


def attention_kernel(heads, q_ref, k_ref, v_ref, cos_ref, sin_ref, row_seg_ref, col_seg_ref, o_ref):
    half = HEAD_DIM // 2

    def rope(x, rows):
        cosine, sine = cos_ref[rows, :], sin_ref[rows, :]
        a, b = x[:, :half], x[:, half:]
        return jnp.concatenate([a * cosine - b * sine, b * cosine + a * sine], axis=1)

    n_rows = q_ref.shape[0]
    keys = rope(k_ref[...].astype(jnp.float32), slice(0, n_rows)).astype(jnp.bfloat16)
    scale = HEAD_DIM ** (-0.5)
    reach = max(ROW_TILE, SEGMENT_MOST)
    for r0 in range(0, n_rows, ROW_TILE):
        c0 = max(0, r0 - reach)
        c1 = r0 + ROW_TILE
        rows = slice(r0, c1)
        places_i = lax.broadcasted_iota(jnp.int32, (ROW_TILE, c1 - c0), 0) + r0
        places_j = lax.broadcasted_iota(jnp.int32, (ROW_TILE, c1 - c0), 1) + c0
        allowed = (row_seg_ref[rows, :] == col_seg_ref[:, c0:c1]) & (places_j <= places_i)
        allowed = jnp.concatenate([allowed] * heads, axis=0)
        query = jnp.concatenate(
            [rope(q_ref[rows, h * HEAD_DIM : (h + 1) * HEAD_DIM], rows) for h in range(heads)],
            axis=0,
        ).astype(jnp.bfloat16)
        scores = lax.dot_general(
            query, keys[c0:c1], (((1,), (1,)), ((), ())), preferred_element_type=jnp.float32
        ) * scale
        weights = jnp.where(allowed, jnp.exp(scores), 0.0)
        total = jnp.sum(weights, axis=1, keepdims=True)
        probabilities = (weights / total).astype(jnp.bfloat16)
        mixed = jnp.dot(probabilities, v_ref[c0:c1, :], preferred_element_type=jnp.float32)
        for h in range(heads):
            o_ref[rows, h * HEAD_DIM : (h + 1) * HEAD_DIM] = mixed[
                h * ROW_TILE : (h + 1) * ROW_TILE
            ].astype(o_ref.dtype)


def rope_tables(positions):
    half_dim = HEAD_DIM // 2
    ratios = jnp.arange(half_dim, dtype=jnp.float32) * (2.0 / HEAD_DIM)
    frequency = jnp.exp(-math.log(ROPE_BASE) * ratios)
    angles = positions.astype(jnp.float32)[:, None] * frequency[None, :]
    return jnp.cos(angles), jnp.sin(angles)


def attention_kernel_call(projected, cols, key_rows, value_rows, cosine, sine, row_seg, col_seg):
    rows = projected.shape[0]
    half_dim = HEAD_DIM // 2
    vmem = pl.BlockSpec(memory_space=pltpu.VMEM)
    heads = cols // HEAD_DIM
    return pl.pallas_call(
        functools.partial(attention_kernel, heads),
        out_shape=jax.ShapeDtypeStruct((rows, cols), jnp.bfloat16),
        in_specs=[vmem] * 7,
        out_specs=vmem,
        cost_estimate=pl.CostEstimate(
            flops=4 * rows * rows * cols + 8 * rows * cols,
            transcendentals=heads * rows * rows,
            bytes_accessed=rows * cols * 6 + rows * HEAD_DIM * 4 + rows * half_dim * 8,
        ),
    )(
        projected,
        key_rows,
        value_rows,
        cosine,
        sine,
        row_seg,
        col_seg,
    )


def ring_gather(block, axis, stride, count):
    n = lax.psum(1, axis)
    me = lax.axis_index(axis)
    here = (me // stride) % count

    def moved(step):
        pairs = []
        for src in range(n):
            k = (src // stride) % count
            pairs.append((src, src + (((k + step) % count) - k) * stride))
        return pairs

    out = jnp.zeros((count,) + block.shape, block.dtype)
    out = lax.dynamic_update_index_in_dim(out, block, here, 0)
    from_right, from_left = block, block
    for step in range(1, count // 2 + 1):
        if step < count - step:
            from_right = lax.ppermute(from_right, axis, perm=moved(-1))
            out = lax.dynamic_update_index_in_dim(out, from_right, (here + step) % count, 0)
        from_left = lax.ppermute(from_left, axis, perm=moved(1))
        out = lax.dynamic_update_index_in_dim(out, from_left, (here - step) % count, 0)
    return out


def ring_matmul(rows, block, axis, stride, count):
    n = lax.psum(1, axis)
    me = lax.axis_index(axis)
    here = (me // stride) % count
    depth = block.shape[0]

    def moved(step):
        pairs = []
        for src in range(n):
            k = (src // stride) % count
            pairs.append((src, src + (((k + step) % count) - k) * stride))
        return pairs

    def product(part, owner):
        lhs = lax.dynamic_slice_in_dim(rows, owner * depth, depth, 1)
        return jnp.dot(lhs, part, preferred_element_type=jnp.float32)

    total = product(block, here)
    from_right, from_left = block, block
    for step in range(1, count // 2 + 1):
        if step == 2:
            rows, from_right, from_left = lax.optimization_barrier((rows, from_right, from_left))
        if step < count - step:
            from_right = lax.ppermute(from_right, axis, perm=moved(-1))
            total = total + product(from_right, (here + step) % count)
        from_left = lax.ppermute(from_left, axis, perm=moved(1))
        total = total + product(from_left, (here - step) % count)
    return total


def per_device(tokens, segment_ids, norm_gain, query_weight, key_weight, value_weight):
    head_dim = HEAD_DIM
    query_cols = query_weight.shape[1]
    heads_dev = query_cols // head_dim
    group_size = HEADS // KV_HEADS
    n_weight = lax.psum(1, "weight")
    me = lax.axis_index("weight")
    core = me % 2
    first_kv = me * heads_dev // group_size
    key_block = lax.dynamic_slice_in_dim(key_weight, first_kv * head_dim, head_dim, 1)
    value_block = lax.dynamic_slice_in_dim(value_weight, first_kv * head_dim, head_dim, 1)
    kv_block = jnp.where(core == 0, key_block, value_block)
    values = tokens.astype(jnp.float32)
    inverse_rms = lax.rsqrt(jnp.mean(values * values, axis=1, keepdims=True) + EPSILON)
    normed = (values * inverse_rms * norm_gain[None, :]).astype(jnp.bfloat16)
    local_weights = jnp.concatenate([query_weight, kv_block], axis=1)
    n_batch = lax.psum(1, "batch")
    y_hi = n_batch // Z_CHIPS
    near = ring_gather(local_weights, "batch", 1, y_hi)
    near = near.reshape(-1, local_weights.shape[1])
    cosine, sine = rope_tables(positions_in_segment(segment_ids))
    row_seg, col_seg = segment_ids[:, None], segment_ids[None, :]
    near, cosine, sine, row_seg, col_seg = lax.optimization_barrier(
        (near, cosine, sine, row_seg, col_seg)
    )
    n_weight = lax.psum(1, "weight")
    repeated = jnp.broadcast_to(normed[None], (n_weight,) + normed.shape)
    gathered = lax.all_to_all(repeated, "weight", 0, 0, tiled=True).reshape(-1, normed.shape[1])
    pack_rows = gathered.shape[0]
    projected = ring_matmul(gathered, near, "batch", y_hi, Z_CHIPS)
    own_rows = projected[:, query_cols:].astype(jnp.bfloat16)
    partner = [(w, w ^ 1) for w in range(n_weight)]
    other_rows = lax.ppermute(own_rows, "weight", perm=partner)
    key_rows = jnp.where(core == 0, own_rows, other_rows)
    value_rows = jnp.where(core == 0, other_rows, own_rows)
    return attention_kernel_call(
        projected, query_cols, key_rows, value_rows, cosine, sine, row_seg, col_seg
    )


def solution(mesh):
    placed = (
        P(("batch", "weight"), None),
        P("batch"),
        P(),
        P("batch", "weight"),
        P("batch", None),
        P("batch", None),
    )
    return jax.shard_map(
        per_device, mesh=mesh, in_specs=placed, out_specs=P("batch", "weight"), check_vma=False
    )
```

```python
import functools
import math

import jax
import jax.numpy as jnp
from jax import lax
from jax.experimental import pallas as pl
from jax.experimental.pallas import tpu as pltpu
from jax.sharding import PartitionSpec as P

HEADS = 64
KV_HEADS = 8
HEAD_DIM = 128


ROPE_BASE = 500000.0
EPSILON = 1e-05

Z_CHIPS = 8


def positions_in_segment(seg_ids):
    places = jnp.arange(seg_ids.shape[0], dtype=jnp.int32)
    earlier = jnp.concatenate([seg_ids[:1] - 1, seg_ids[:-1]])
    starts = jnp.where(seg_ids != earlier, places, 0)
    leading = lax.cummax(starts, axis=0)
    return places - leading


def rotate(vectors, positions):
    half_dim = vectors.shape[-1] // 2
    ratios = jnp.arange(half_dim, dtype=jnp.float32) * (2.0 / vectors.shape[-1])
    frequency = jnp.exp(-math.log(ROPE_BASE) * ratios)
    angles = positions.astype(jnp.float32)[:, None] * frequency[None, :]
    cosine = jnp.cos(angles)[:, None, :]
    sine_part = jnp.sin(angles)[:, None, :]
    front_half = vectors[..., :half_dim]
    back_half = vectors[..., half_dim:]
    return jnp.concatenate(
        [front_half * cosine - back_half * sine_part, back_half * cosine + front_half * sine_part],
        axis=-1,
    )


def attend(grouped, rotated_keys, value_rows, seg_ids):
    scores = jnp.einsum(
        "ingd,jnd->ngij", grouped, rotated_keys, preferred_element_type=jnp.float32
    ) * grouped.shape[-1] ** (-0.5)
    places = jnp.arange(seg_ids.shape[0], dtype=jnp.int32)
    allowed = (seg_ids[:, None] == seg_ids[None, :]) & (places[None, :] <= places[:, None])
    weights = jnp.where(allowed, jnp.exp(scores), 0.0)
    probabilities = (weights / jnp.sum(weights, axis=-1, keepdims=True)).astype(jnp.bfloat16)
    mixed = jnp.einsum(
        "ngij,jnd->ingd", probabilities, value_rows, preferred_element_type=jnp.float32
    )
    return mixed.astype(jnp.bfloat16)


ROW_TILE = 64
SEGMENT_MOST = 64


def attention_kernel(heads, q_ref, k_ref, v_ref, cos_ref, sin_ref, row_seg_ref, col_seg_ref, o_ref):
    half = HEAD_DIM // 2

    def rope(x, rows):
        cosine, sine = cos_ref[rows, :], sin_ref[rows, :]
        a, b = x[:, :half], x[:, half:]
        return jnp.concatenate([a * cosine - b * sine, b * cosine + a * sine], axis=1)

    n_rows = q_ref.shape[0]
    keys = rope(k_ref[...].astype(jnp.float32), slice(0, n_rows)).astype(jnp.bfloat16)
    scale = HEAD_DIM ** (-0.5)
    reach = max(ROW_TILE, SEGMENT_MOST)
    for r0 in range(0, n_rows, ROW_TILE):
        c0 = max(0, r0 - reach)
        c1 = r0 + ROW_TILE
        rows = slice(r0, c1)
        places_i = lax.broadcasted_iota(jnp.int32, (ROW_TILE, c1 - c0), 0) + r0
        places_j = lax.broadcasted_iota(jnp.int32, (ROW_TILE, c1 - c0), 1) + c0
        allowed = (row_seg_ref[rows, :] == col_seg_ref[:, c0:c1]) & (places_j <= places_i)
        allowed = jnp.concatenate([allowed] * heads, axis=0)
        query = jnp.concatenate(
            [rope(q_ref[rows, h * HEAD_DIM : (h + 1) * HEAD_DIM], rows) for h in range(heads)],
            axis=0,
        ).astype(jnp.bfloat16)
        scores = lax.dot_general(
            query, keys[c0:c1], (((1,), (1,)), ((), ())), preferred_element_type=jnp.float32
        ) * scale
        weights = jnp.where(allowed, jnp.exp(scores), 0.0)
        total = jnp.sum(weights, axis=1, keepdims=True)
        probabilities = (weights / total).astype(jnp.bfloat16)
        mixed = jnp.dot(probabilities, v_ref[c0:c1, :], preferred_element_type=jnp.float32)
        for h in range(heads):
            o_ref[rows, h * HEAD_DIM : (h + 1) * HEAD_DIM] = mixed[
                h * ROW_TILE : (h + 1) * ROW_TILE
            ].astype(o_ref.dtype)


def rope_tables(positions):
    half_dim = HEAD_DIM // 2
    ratios = jnp.arange(half_dim, dtype=jnp.float32) * (2.0 / HEAD_DIM)
    frequency = jnp.exp(-math.log(ROPE_BASE) * ratios)
    angles = positions.astype(jnp.float32)[:, None] * frequency[None, :]
    return jnp.cos(angles), jnp.sin(angles)


def attention_kernel_call(projected, cols, key_rows, value_rows, cosine, sine, row_seg, col_seg):
    rows = projected.shape[0]
    half_dim = HEAD_DIM // 2
    vmem = pl.BlockSpec(memory_space=pltpu.VMEM)
    heads = cols // HEAD_DIM
    return pl.pallas_call(
        functools.partial(attention_kernel, heads),
        out_shape=jax.ShapeDtypeStruct((rows, cols), jnp.bfloat16),
        in_specs=[vmem] * 7,
        out_specs=vmem,
        cost_estimate=pl.CostEstimate(
            flops=4 * rows * rows * cols + 8 * rows * cols,
            transcendentals=heads * rows * rows,
            bytes_accessed=rows * cols * 6 + rows * HEAD_DIM * 4 + rows * half_dim * 8,
        ),
    )(
        projected,
        key_rows,
        value_rows,
        cosine,
        sine,
        row_seg,
        col_seg,
    )


def ring_gather(block, axis, stride, count):
    n = lax.psum(1, axis)
    me = lax.axis_index(axis)
    here = (me // stride) % count

    def moved(step):
        pairs = []
        for src in range(n):
            k = (src // stride) % count
            pairs.append((src, src + (((k + step) % count) - k) * stride))
        return pairs

    out = jnp.zeros((count,) + block.shape, block.dtype)
    out = lax.dynamic_update_index_in_dim(out, block, here, 0)
    from_right, from_left = block, block
    for step in range(1, count // 2 + 1):
        if step < count - step:
            from_right = lax.ppermute(from_right, axis, perm=moved(-1))
            out = lax.dynamic_update_index_in_dim(out, from_right, (here + step) % count, 0)
            from_left = lax.ppermute(from_left, axis, perm=moved(1))
        else:
            cut = lane_cut(block.shape[-1])
            from_left = jnp.concatenate(
                [
                    lax.ppermute(from_left[..., :cut], axis, perm=moved(1)),
                    lax.ppermute(from_right[..., cut:], axis, perm=moved(-1)),
                ],
                axis=-1,
            )
        out = lax.dynamic_update_index_in_dim(out, from_left, (here - step) % count, 0)
    return out


def lane_cut(width):
    return min(width, (width // 2 + 127) // 128 * 128)


def ring_matmul(rows, block, axis, stride, count):
    n = lax.psum(1, axis)
    me = lax.axis_index(axis)
    here = (me // stride) % count
    depth = block.shape[0]

    def moved(step):
        pairs = []
        for src in range(n):
            k = (src // stride) % count
            pairs.append((src, src + (((k + step) % count) - k) * stride))
        return pairs

    def product(part, owner):
        lhs = lax.dynamic_slice_in_dim(rows, owner * depth, depth, 1)
        return jnp.dot(lhs, part, preferred_element_type=jnp.float32)

    total = product(block, here)
    from_right, from_left = block, block
    for step in range(1, count // 2 + 1):
        if step == 2:
            rows, from_right, from_left = lax.optimization_barrier((rows, from_right, from_left))
        if step < count - step:
            from_right = lax.ppermute(from_right, axis, perm=moved(-1))
            total = total + product(from_right, (here + step) % count)
            from_left = lax.ppermute(from_left, axis, perm=moved(1))
        else:
            cut = lane_cut(block.shape[-1])
            from_left = jnp.concatenate(
                [
                    lax.ppermute(from_left[..., :cut], axis, perm=moved(1)),
                    lax.ppermute(from_right[..., cut:], axis, perm=moved(-1)),
                ],
                axis=-1,
            )
        total = total + product(from_left, (here - step) % count)
    return total


def per_device(tokens, segment_ids, norm_gain, query_weight, key_weight, value_weight):
    head_dim = HEAD_DIM
    query_cols = query_weight.shape[1]
    heads_dev = query_cols // head_dim
    group_size = HEADS // KV_HEADS
    n_weight = lax.psum(1, "weight")
    me = lax.axis_index("weight")
    core = me % 2
    first_kv = me * heads_dev // group_size
    key_block = lax.dynamic_slice_in_dim(key_weight, first_kv * head_dim, head_dim, 1)
    value_block = lax.dynamic_slice_in_dim(value_weight, first_kv * head_dim, head_dim, 1)
    kv_block = jnp.where(core == 0, key_block, value_block)
    values = tokens.astype(jnp.float32)
    inverse_rms = lax.rsqrt(jnp.mean(values * values, axis=1, keepdims=True) + EPSILON)
    normed = (values * inverse_rms * norm_gain[None, :]).astype(jnp.bfloat16)
    local_weights = jnp.concatenate([query_weight, kv_block], axis=1)
    n_batch = lax.psum(1, "batch")
    y_hi = n_batch // Z_CHIPS
    near = ring_gather(local_weights, "batch", 1, y_hi)
    near = near.reshape(-1, local_weights.shape[1])
    cosine, sine = rope_tables(positions_in_segment(segment_ids))
    row_seg, col_seg = segment_ids[:, None], segment_ids[None, :]
    near, cosine, sine, row_seg, col_seg = lax.optimization_barrier(
        (near, cosine, sine, row_seg, col_seg)
    )
    gathered = lax.all_gather(normed, "weight", axis=0, tiled=True)
    pack_rows = gathered.shape[0]
    projected = ring_matmul(gathered, near, "batch", y_hi, Z_CHIPS)
    own_rows = projected[:, query_cols:].astype(jnp.bfloat16)
    partner = [(w, w ^ 1) for w in range(n_weight)]
    other_rows = lax.ppermute(own_rows, "weight", perm=partner)
    key_rows = jnp.where(core == 0, own_rows, other_rows)
    value_rows = jnp.where(core == 0, other_rows, own_rows)
    return attention_kernel_call(
        projected, query_cols, key_rows, value_rows, cosine, sine, row_seg, col_seg
    )


def solution(mesh):
    placed = (
        P(("batch", "weight"), None),
        P("batch"),
        P(),
        P("batch", "weight"),
        P("batch", None),
        P("batch", None),
    )
    return jax.shard_map(
        per_device, mesh=mesh, in_specs=placed, out_specs=P("batch", "weight"), check_vma=False
    )
```

```python
import functools
import math

import jax
import jax.numpy as jnp
from jax import lax
from jax.experimental import pallas as pl
from jax.experimental.pallas import tpu as pltpu
from jax.sharding import PartitionSpec as P

HEADS = 64
KV_HEADS = 8
HEAD_DIM = 128


ROPE_BASE = 500000.0
EPSILON = 1e-05

Z_CHIPS = 8


def positions_in_segment(seg_ids):
    places = jnp.arange(seg_ids.shape[0], dtype=jnp.int32)
    earlier = jnp.concatenate([seg_ids[:1] - 1, seg_ids[:-1]])
    starts = jnp.where(seg_ids != earlier, places, 0)
    leading = lax.cummax(starts, axis=0)
    return places - leading


def rotate(vectors, positions):
    half_dim = vectors.shape[-1] // 2
    ratios = jnp.arange(half_dim, dtype=jnp.float32) * (2.0 / vectors.shape[-1])
    frequency = jnp.exp(-math.log(ROPE_BASE) * ratios)
    angles = positions.astype(jnp.float32)[:, None] * frequency[None, :]
    cosine = jnp.cos(angles)[:, None, :]
    sine_part = jnp.sin(angles)[:, None, :]
    front_half = vectors[..., :half_dim]
    back_half = vectors[..., half_dim:]
    return jnp.concatenate(
        [front_half * cosine - back_half * sine_part, back_half * cosine + front_half * sine_part],
        axis=-1,
    )


def attend(grouped, rotated_keys, value_rows, seg_ids):
    scores = jnp.einsum(
        "ingd,jnd->ngij", grouped, rotated_keys, preferred_element_type=jnp.float32
    ) * grouped.shape[-1] ** (-0.5)
    places = jnp.arange(seg_ids.shape[0], dtype=jnp.int32)
    allowed = (seg_ids[:, None] == seg_ids[None, :]) & (places[None, :] <= places[:, None])
    weights = jnp.where(allowed, jnp.exp(scores), 0.0)
    probabilities = (weights / jnp.sum(weights, axis=-1, keepdims=True)).astype(jnp.bfloat16)
    mixed = jnp.einsum(
        "ngij,jnd->ingd", probabilities, value_rows, preferred_element_type=jnp.float32
    )
    return mixed.astype(jnp.bfloat16)


ROW_TILE = 64
SEGMENT_MOST = 64


def attention_kernel(heads, q_ref, k_ref, v_ref, cos_ref, sin_ref, row_seg_ref, col_seg_ref, o_ref):
    half = HEAD_DIM // 2

    def rope(x, rows):
        cosine, sine = cos_ref[rows, :], sin_ref[rows, :]
        a, b = x[:, :half], x[:, half:]
        return jnp.concatenate([a * cosine - b * sine, b * cosine + a * sine], axis=1)

    n_rows = q_ref.shape[0]
    keys = rope(k_ref[...].astype(jnp.float32), slice(0, n_rows)).astype(jnp.bfloat16)
    scale = HEAD_DIM ** (-0.5)
    reach = max(ROW_TILE, SEGMENT_MOST)
    for r0 in range(0, n_rows, ROW_TILE):
        c0 = max(0, r0 - reach)
        c1 = r0 + ROW_TILE
        rows = slice(r0, c1)
        places_i = lax.broadcasted_iota(jnp.int32, (ROW_TILE, c1 - c0), 0) + r0
        places_j = lax.broadcasted_iota(jnp.int32, (ROW_TILE, c1 - c0), 1) + c0
        allowed = (row_seg_ref[rows, :] == col_seg_ref[:, c0:c1]) & (places_j <= places_i)
        allowed = jnp.concatenate([allowed] * heads, axis=0)
        query = jnp.concatenate(
            [rope(q_ref[rows, h * HEAD_DIM : (h + 1) * HEAD_DIM], rows) for h in range(heads)],
            axis=0,
        ).astype(jnp.bfloat16)
        scores = lax.dot_general(
            query, keys[c0:c1], (((1,), (1,)), ((), ())), preferred_element_type=jnp.float32
        ) * scale
        weights = jnp.where(allowed, jnp.exp(scores), 0.0)
        total = jnp.sum(weights, axis=1, keepdims=True)
        probabilities = (weights / total).astype(jnp.bfloat16)
        mixed = jnp.dot(probabilities, v_ref[c0:c1, :], preferred_element_type=jnp.float32)
        for h in range(heads):
            o_ref[rows, h * HEAD_DIM : (h + 1) * HEAD_DIM] = mixed[
                h * ROW_TILE : (h + 1) * ROW_TILE
            ].astype(o_ref.dtype)


def rope_tables(positions):
    half_dim = HEAD_DIM // 2
    ratios = jnp.arange(half_dim, dtype=jnp.float32) * (2.0 / HEAD_DIM)
    frequency = jnp.exp(-math.log(ROPE_BASE) * ratios)
    angles = positions.astype(jnp.float32)[:, None] * frequency[None, :]
    return jnp.cos(angles), jnp.sin(angles)


def attention_kernel_call(projected, cols, key_rows, value_rows, cosine, sine, row_seg, col_seg):
    rows = projected.shape[0]
    half_dim = HEAD_DIM // 2
    vmem = pl.BlockSpec(memory_space=pltpu.VMEM)
    heads = cols // HEAD_DIM
    return pl.pallas_call(
        functools.partial(attention_kernel, heads),
        out_shape=jax.ShapeDtypeStruct((rows, cols), jnp.bfloat16),
        in_specs=[vmem] * 7,
        out_specs=vmem,
        cost_estimate=pl.CostEstimate(
            flops=4 * rows * rows * cols + 8 * rows * cols,
            transcendentals=heads * rows * rows,
            bytes_accessed=rows * cols * 6 + rows * HEAD_DIM * 4 + rows * half_dim * 8,
        ),
    )(
        projected,
        key_rows,
        value_rows,
        cosine,
        sine,
        row_seg,
        col_seg,
    )


def ring_gather(block, axis, stride, count):
    n = lax.psum(1, axis)
    me = lax.axis_index(axis)
    here = (me // stride) % count

    def moved(step):
        pairs = []
        for src in range(n):
            k = (src // stride) % count
            pairs.append((src, src + (((k + step) % count) - k) * stride))
        return pairs

    out = jnp.zeros((count,) + block.shape, block.dtype)
    out = lax.dynamic_update_index_in_dim(out, block, here, 0)
    from_right, from_left = block, block
    for step in range(1, count // 2 + 1):
        if step < count - step:
            from_right = lax.ppermute(from_right, axis, perm=moved(-1))
            out = lax.dynamic_update_index_in_dim(out, from_right, (here + step) % count, 0)
            from_left = lax.ppermute(from_left, axis, perm=moved(1))
        else:
            cut = lane_cut(block.shape[-1])
            from_left = jnp.concatenate(
                [
                    lax.ppermute(from_left[..., :cut], axis, perm=moved(1)),
                    lax.ppermute(from_right[..., cut:], axis, perm=moved(-1)),
                ],
                axis=-1,
            )
        out = lax.dynamic_update_index_in_dim(out, from_left, (here - step) % count, 0)
    return out


def lane_cut(width):
    return min(width, (width // 2 + 127) // 128 * 128)


def ring_matmul(rows, block, axis, stride, count, starts, wait_rows):
    n = lax.psum(1, axis)
    me = lax.axis_index(axis)
    here = (me // stride) % count
    depth = block.shape[1]

    def moved(step):
        pairs = []
        for src in range(n):
            k = (src // stride) % count
            pairs.append((src, src + (((k + step) % count) - k) * stride))
        return pairs

    def product(part, owner):
        result = None
        for piece, start in enumerate(starts(owner)):
            lhs = lax.dynamic_slice_in_dim(rows, start, depth, 1)
            term = jnp.dot(lhs, part[piece], preferred_element_type=jnp.float32)
            result = term if result is None else result + term
        return result

    total = product(block, here)
    from_right, from_left = block, block
    for step in range(1, count // 2 + 1):
        if step == 2 and wait_rows:
            rows, from_right, from_left = lax.optimization_barrier((rows, from_right, from_left))
        if step < count - step:
            from_right = lax.ppermute(from_right, axis, perm=moved(-1))
            total = total + product(from_right, (here + step) % count)
            from_left = lax.ppermute(from_left, axis, perm=moved(1))
        else:
            cut = lane_cut(block.shape[-1])
            from_left = jnp.concatenate(
                [
                    lax.ppermute(from_left[..., :cut], axis, perm=moved(1)),
                    lax.ppermute(from_right[..., cut:], axis, perm=moved(-1)),
                ],
                axis=-1,
            )
        total = total + product(from_left, (here - step) % count)
    return total


def per_device(tokens, segment_ids, norm_gain, query_weight, key_weight, value_weight):
    head_dim = HEAD_DIM
    query_cols = query_weight.shape[1]
    heads_dev = query_cols // head_dim
    group_size = HEADS // KV_HEADS
    n_weight = lax.psum(1, "weight")
    me = lax.axis_index("weight")
    core = me % 2
    first_kv = me * heads_dev // group_size
    key_block = lax.dynamic_slice_in_dim(key_weight, first_kv * head_dim, head_dim, 1)
    value_block = lax.dynamic_slice_in_dim(value_weight, first_kv * head_dim, head_dim, 1)
    kv_block = jnp.where(core == 0, key_block, value_block)
    values = tokens.astype(jnp.float32)
    inverse_rms = lax.rsqrt(jnp.mean(values * values, axis=1, keepdims=True) + EPSILON)
    normed = (values * inverse_rms * norm_gain[None, :]).astype(jnp.bfloat16)
    local_weights = jnp.concatenate([query_weight, kv_block], axis=1)
    n_batch = lax.psum(1, "batch")
    y_hi = n_batch // Z_CHIPS
    shard = local_weights.shape[0]
    yh = lax.axis_index("batch") % y_hi
    near = ring_gather(local_weights, "batch", 1, y_hi)
    others = jnp.stack([near[(yh + r) % y_hi] for r in range(1, y_hi)])
    cosine, sine = rope_tables(positions_in_segment(segment_ids))
    row_seg, col_seg = segment_ids[:, None], segment_ids[None, :]
    others, cosine, sine, row_seg, col_seg = lax.optimization_barrier(
        (others, cosine, sine, row_seg, col_seg)
    )
    gathered = lax.all_gather(normed, "weight", axis=0, tiled=True)
    pack_rows = gathered.shape[0]
    own_part = ring_matmul(
        gathered,
        local_weights[None],
        "batch",
        y_hi,
        Z_CHIPS,
        lambda z: [(z * y_hi + yh) * shard],
        False,
    )
    other_part = ring_matmul(
        gathered,
        others,
        "batch",
        y_hi,
        Z_CHIPS,
        lambda z: [(z * y_hi + (yh + r) % y_hi) * shard for r in range(1, y_hi)],
        True,
    )
    projected = own_part + other_part
    own_rows = projected[:, query_cols:].astype(jnp.bfloat16)
    partner = [(w, w ^ 1) for w in range(n_weight)]
    other_rows = lax.ppermute(own_rows, "weight", perm=partner)
    key_rows = jnp.where(core == 0, own_rows, other_rows)
    value_rows = jnp.where(core == 0, other_rows, own_rows)
    return attention_kernel_call(
        projected, query_cols, key_rows, value_rows, cosine, sine, row_seg, col_seg
    )


def solution(mesh):
    placed = (
        P(("batch", "weight"), None),
        P("batch"),
        P(),
        P("batch", "weight"),
        P("batch", None),
        P("batch", None),
    )
    return jax.shard_map(
        per_device, mesh=mesh, in_specs=placed, out_specs=P("batch", "weight"), check_vma=False
    )
```

```python
import functools
import math

import jax
import jax.numpy as jnp
from jax import lax
from jax.experimental import pallas as pl
from jax.experimental.pallas import tpu as pltpu
from jax.sharding import PartitionSpec as P

HEADS = 64
KV_HEADS = 8
HEAD_DIM = 128


ROPE_BASE = 500000.0
EPSILON = 1e-05

Z_CHIPS = 8


def positions_in_segment(seg_ids):
    places = jnp.arange(seg_ids.shape[0], dtype=jnp.int32)
    earlier = jnp.concatenate([seg_ids[:1] - 1, seg_ids[:-1]])
    starts = jnp.where(seg_ids != earlier, places, 0)
    leading = lax.cummax(starts, axis=0)
    return places - leading


def rotate(vectors, positions):
    half_dim = vectors.shape[-1] // 2
    ratios = jnp.arange(half_dim, dtype=jnp.float32) * (2.0 / vectors.shape[-1])
    frequency = jnp.exp(-math.log(ROPE_BASE) * ratios)
    angles = positions.astype(jnp.float32)[:, None] * frequency[None, :]
    cosine = jnp.cos(angles)[:, None, :]
    sine_part = jnp.sin(angles)[:, None, :]
    front_half = vectors[..., :half_dim]
    back_half = vectors[..., half_dim:]
    return jnp.concatenate(
        [front_half * cosine - back_half * sine_part, back_half * cosine + front_half * sine_part],
        axis=-1,
    )


def attend(grouped, rotated_keys, value_rows, seg_ids):
    scores = jnp.einsum(
        "ingd,jnd->ngij", grouped, rotated_keys, preferred_element_type=jnp.float32
    ) * grouped.shape[-1] ** (-0.5)
    places = jnp.arange(seg_ids.shape[0], dtype=jnp.int32)
    allowed = (seg_ids[:, None] == seg_ids[None, :]) & (places[None, :] <= places[:, None])
    weights = jnp.where(allowed, jnp.exp(scores), 0.0)
    probabilities = (weights / jnp.sum(weights, axis=-1, keepdims=True)).astype(jnp.bfloat16)
    mixed = jnp.einsum(
        "ngij,jnd->ingd", probabilities, value_rows, preferred_element_type=jnp.float32
    )
    return mixed.astype(jnp.bfloat16)


ROW_TILE = 64
SEGMENT_MOST = 64


def attention_kernel(
    heads, q_ref, own_ref, other_ref, core_ref, cos_ref, sin_ref, row_seg_ref, col_seg_ref, o_ref
):
    half = HEAD_DIM // 2

    def rope(x, rows):
        cosine, sine = cos_ref[rows, :], sin_ref[rows, :]
        a, b = x[:, :half], x[:, half:]
        return jnp.concatenate([a * cosine - b * sine, b * cosine + a * sine], axis=1)

    n_rows = q_ref.shape[0]
    key_first = core_ref[0:1, 0:1] == 0
    own, other = own_ref[...], other_ref[...]
    key_rows = jnp.where(key_first, own, other)
    value_rows = jnp.where(key_first, other, own)
    keys = rope(key_rows.astype(jnp.float32), slice(0, n_rows)).astype(jnp.bfloat16)
    scale = HEAD_DIM ** (-0.5)
    reach = max(ROW_TILE, SEGMENT_MOST)
    for r0 in range(0, n_rows, ROW_TILE):
        c0 = max(0, r0 - reach)
        c1 = r0 + ROW_TILE
        rows = slice(r0, c1)
        places_i = lax.broadcasted_iota(jnp.int32, (ROW_TILE, c1 - c0), 0) + r0
        places_j = lax.broadcasted_iota(jnp.int32, (ROW_TILE, c1 - c0), 1) + c0
        allowed = (row_seg_ref[rows, 0:1] == col_seg_ref[:, c0:c1]) & (places_j <= places_i)
        allowed = jnp.concatenate([allowed] * heads, axis=0)
        query = jnp.concatenate(
            [rope(q_ref[rows, h * HEAD_DIM : (h + 1) * HEAD_DIM], rows) for h in range(heads)],
            axis=0,
        ).astype(jnp.bfloat16)
        scores = lax.dot_general(
            query, keys[c0:c1], (((1,), (1,)), ((), ())), preferred_element_type=jnp.float32
        ) * scale
        weights = jnp.where(allowed, jnp.exp(scores), 0.0)
        total = jnp.sum(weights, axis=1, keepdims=True)
        probabilities = (weights / total).astype(jnp.bfloat16)
        mixed = jnp.dot(probabilities, value_rows[c0:c1], preferred_element_type=jnp.float32)
        for h in range(heads):
            o_ref[rows, h * HEAD_DIM : (h + 1) * HEAD_DIM] = mixed[
                h * ROW_TILE : (h + 1) * ROW_TILE
            ].astype(o_ref.dtype)


def rope_tables(positions):
    half_dim = HEAD_DIM // 2
    ratios = jnp.arange(half_dim, dtype=jnp.float32) * (2.0 / HEAD_DIM)
    frequency = jnp.exp(-math.log(ROPE_BASE) * ratios)
    angles = positions.astype(jnp.float32)[:, None] * frequency[None, :]
    return jnp.cos(angles), jnp.sin(angles)


def attention_kernel_call(projected, cols, own_rows, other_rows, core, cosine, sine, row_seg, col_seg):
    rows = projected.shape[0]
    half_dim = HEAD_DIM // 2
    vmem = pl.BlockSpec(memory_space=pltpu.VMEM)
    heads = cols // HEAD_DIM
    return pl.pallas_call(
        functools.partial(attention_kernel, heads),
        out_shape=jax.ShapeDtypeStruct((rows, cols), jnp.bfloat16),
        in_specs=[vmem] * 8,
        out_specs=vmem,
        cost_estimate=pl.CostEstimate(
            flops=4 * rows * rows * cols + 8 * rows * cols,
            transcendentals=heads * rows * rows,
            bytes_accessed=rows * cols * 6 + rows * HEAD_DIM * 4 + rows * half_dim * 8,
        ),
    )(
        projected,
        own_rows,
        other_rows,
        jnp.full((1, 128), core, jnp.int32),
        cosine,
        sine,
        row_seg,
        col_seg,
    )


def ring_gather(block, axis, stride, count):
    n = lax.psum(1, axis)
    me = lax.axis_index(axis)
    here = (me // stride) % count

    def moved(step):
        pairs = []
        for src in range(n):
            k = (src // stride) % count
            pairs.append((src, src + (((k + step) % count) - k) * stride))
        return pairs

    out = jnp.zeros((count,) + block.shape, block.dtype)
    out = lax.dynamic_update_index_in_dim(out, block, here, 0)
    from_right, from_left = block, block
    for step in range(1, count // 2 + 1):
        if step < count - step:
            from_right = lax.ppermute(from_right, axis, perm=moved(-1))
            out = lax.dynamic_update_index_in_dim(out, from_right, (here + step) % count, 0)
            from_left = lax.ppermute(from_left, axis, perm=moved(1))
        else:
            cut = lane_cut(block.shape[-1])
            from_left = jnp.concatenate(
                [
                    lax.ppermute(from_left[..., :cut], axis, perm=moved(1)),
                    lax.ppermute(from_right[..., cut:], axis, perm=moved(-1)),
                ],
                axis=-1,
            )
        out = lax.dynamic_update_index_in_dim(out, from_left, (here - step) % count, 0)
    return out


def lane_cut(width):
    return min(width, (width // 2 + 127) // 128 * 128)


def ring_matmul(rows, block, axis, stride, count, starts, wait_rows):
    n = lax.psum(1, axis)
    me = lax.axis_index(axis)
    here = (me // stride) % count
    depth = block.shape[1]

    def moved(step):
        pairs = []
        for src in range(n):
            k = (src // stride) % count
            pairs.append((src, src + (((k + step) % count) - k) * stride))
        return pairs

    def product(part, owner):
        result = None
        for piece, start in enumerate(starts(owner)):
            lhs = lax.dynamic_slice_in_dim(rows, start, depth, 1)
            term = jnp.dot(lhs, part[piece], preferred_element_type=jnp.float32)
            result = term if result is None else result + term
        return result

    total = product(block, here)
    from_right, from_left = block, block
    for step in range(1, count // 2 + 1):
        if step == 2 and wait_rows:
            rows, from_right, from_left = lax.optimization_barrier((rows, from_right, from_left))
        if step < count - step:
            from_right = lax.ppermute(from_right, axis, perm=moved(-1))
            total = total + product(from_right, (here + step) % count)
            from_left = lax.ppermute(from_left, axis, perm=moved(1))
        else:
            cut = lane_cut(block.shape[-1])
            from_left = jnp.concatenate(
                [
                    lax.ppermute(from_left[..., :cut], axis, perm=moved(1)),
                    lax.ppermute(from_right[..., cut:], axis, perm=moved(-1)),
                ],
                axis=-1,
            )
        total = total + product(from_left, (here - step) % count)
    return total


def per_device(tokens, segment_ids, norm_gain, query_weight, key_weight, value_weight):
    head_dim = HEAD_DIM
    query_cols = query_weight.shape[1]
    heads_dev = query_cols // head_dim
    group_size = HEADS // KV_HEADS
    n_weight = lax.psum(1, "weight")
    me = lax.axis_index("weight")
    core = me % 2
    first_kv = me * heads_dev // group_size
    key_block = lax.dynamic_slice_in_dim(key_weight, first_kv * head_dim, head_dim, 1)
    value_block = lax.dynamic_slice_in_dim(value_weight, first_kv * head_dim, head_dim, 1)
    kv_block = jnp.where(core == 0, key_block, value_block)
    values = tokens.astype(jnp.float32)
    inverse_rms = lax.rsqrt(jnp.mean(values * values, axis=1, keepdims=True) + EPSILON)
    normed = (values * inverse_rms * norm_gain[None, :]).astype(jnp.bfloat16)
    local_weights = jnp.concatenate([query_weight, kv_block], axis=1)
    n_batch = lax.psum(1, "batch")
    y_hi = n_batch // Z_CHIPS
    shard = local_weights.shape[0]
    yh = lax.axis_index("batch") % y_hi
    near = ring_gather(local_weights, "batch", 1, y_hi)
    others = jnp.stack([near[(yh + r) % y_hi] for r in range(1, y_hi)])
    cosine, sine = rope_tables(positions_in_segment(segment_ids))
    row_seg = jnp.broadcast_to(segment_ids[:, None], (segment_ids.shape[0], 128))
    col_seg = segment_ids[None, :]
    others, cosine, sine, row_seg, col_seg = lax.optimization_barrier(
        (others, cosine, sine, row_seg, col_seg)
    )
    gathered = lax.all_gather(normed, "weight", axis=0, tiled=True)
    pack_rows = gathered.shape[0]
    own_part = ring_matmul(
        gathered,
        local_weights[None],
        "batch",
        y_hi,
        Z_CHIPS,
        lambda z: [(z * y_hi + yh) * shard],
        False,
    )
    other_part = ring_matmul(
        gathered,
        others,
        "batch",
        y_hi,
        Z_CHIPS,
        lambda z: [(z * y_hi + (yh + r) % y_hi) * shard for r in range(1, y_hi)],
        True,
    )
    projected = own_part + other_part
    own_rows = projected[:, query_cols:].astype(jnp.bfloat16)
    partner = [(w, w ^ 1) for w in range(n_weight)]
    other_rows = lax.ppermute(own_rows, "weight", perm=partner)
    return attention_kernel_call(
        projected, query_cols, own_rows, other_rows, core, cosine, sine, row_seg, col_seg
    )


def solution(mesh):
    placed = (
        P(("batch", "weight"), None),
        P("batch"),
        P(),
        P("batch", "weight"),
        P("batch", None),
        P("batch", None),
    )
    return jax.shard_map(
        per_device, mesh=mesh, in_specs=placed, out_specs=P("batch", "weight"), check_vma=False
    )
```

```python
import functools
import math

import jax
import jax.numpy as jnp
from jax import lax
from jax.experimental import pallas as pl
from jax.experimental.pallas import tpu as pltpu
from jax.sharding import PartitionSpec as P

HEADS = 64
KV_HEADS = 8
HEAD_DIM = 128


ROPE_BASE = 500000.0
EPSILON = 1e-05

Z_CHIPS = 8


def positions_in_segment(seg_ids):
    places = jnp.arange(seg_ids.shape[0], dtype=jnp.int32)
    earlier = jnp.concatenate([seg_ids[:1] - 1, seg_ids[:-1]])
    starts = jnp.where(seg_ids != earlier, places, 0)
    leading = lax.cummax(starts, axis=0)
    return places - leading


def rotate(vectors, positions):
    half_dim = vectors.shape[-1] // 2
    ratios = jnp.arange(half_dim, dtype=jnp.float32) * (2.0 / vectors.shape[-1])
    frequency = jnp.exp(-math.log(ROPE_BASE) * ratios)
    angles = positions.astype(jnp.float32)[:, None] * frequency[None, :]
    cosine = jnp.cos(angles)[:, None, :]
    sine_part = jnp.sin(angles)[:, None, :]
    front_half = vectors[..., :half_dim]
    back_half = vectors[..., half_dim:]
    return jnp.concatenate(
        [front_half * cosine - back_half * sine_part, back_half * cosine + front_half * sine_part],
        axis=-1,
    )


def attend(grouped, rotated_keys, value_rows, seg_ids):
    scores = jnp.einsum(
        "ingd,jnd->ngij", grouped, rotated_keys, preferred_element_type=jnp.float32
    ) * grouped.shape[-1] ** (-0.5)
    places = jnp.arange(seg_ids.shape[0], dtype=jnp.int32)
    allowed = (seg_ids[:, None] == seg_ids[None, :]) & (places[None, :] <= places[:, None])
    weights = jnp.where(allowed, jnp.exp(scores), 0.0)
    probabilities = (weights / jnp.sum(weights, axis=-1, keepdims=True)).astype(jnp.bfloat16)
    mixed = jnp.einsum(
        "ngij,jnd->ingd", probabilities, value_rows, preferred_element_type=jnp.float32
    )
    return mixed.astype(jnp.bfloat16)


ROW_TILE = 64
SEGMENT_MOST = 64


def attention_kernel(
    heads, qa_ref, qb_ref, own_ref, other_ref, core_ref, cos_ref, sin_ref, row_seg_ref, col_seg_ref,
    o_ref,
):
    half = HEAD_DIM // 2

    def rope(x, rows):
        cosine, sine = cos_ref[rows, :], sin_ref[rows, :]
        a, b = x[:, :half], x[:, half:]
        return jnp.concatenate([a * cosine - b * sine, b * cosine + a * sine], axis=1)

    n_rows = qa_ref.shape[0]
    key_first = core_ref[0:1, 0:1] == 0
    own, other = own_ref[...], other_ref[...]
    key_rows = jnp.where(key_first, own, other)
    value_rows = jnp.where(key_first, other, own)
    keys = rope(key_rows.astype(jnp.float32), slice(0, n_rows)).astype(jnp.bfloat16)
    scale = HEAD_DIM ** (-0.5)
    reach = max(ROW_TILE, SEGMENT_MOST)
    for r0 in range(0, n_rows, ROW_TILE):
        c0 = max(0, r0 - reach)
        c1 = r0 + ROW_TILE
        rows = slice(r0, c1)
        places_i = lax.broadcasted_iota(jnp.int32, (ROW_TILE, c1 - c0), 0) + r0
        places_j = lax.broadcasted_iota(jnp.int32, (ROW_TILE, c1 - c0), 1) + c0
        allowed = (row_seg_ref[rows, 0:1] == col_seg_ref[:, c0:c1]) & (places_j <= places_i)
        allowed = jnp.concatenate([allowed] * heads, axis=0)
        query = jnp.concatenate(
            [
                rope(
                    qa_ref[rows, h * HEAD_DIM : (h + 1) * HEAD_DIM]
                    + qb_ref[rows, h * HEAD_DIM : (h + 1) * HEAD_DIM],
                    rows,
                )
                for h in range(heads)
            ],
            axis=0,
        ).astype(jnp.bfloat16)
        scores = lax.dot_general(
            query, keys[c0:c1], (((1,), (1,)), ((), ())), preferred_element_type=jnp.float32
        ) * scale
        weights = jnp.where(allowed, jnp.exp(scores), 0.0)
        total = jnp.sum(weights, axis=1, keepdims=True)
        probabilities = (weights / total).astype(jnp.bfloat16)
        mixed = jnp.dot(probabilities, value_rows[c0:c1], preferred_element_type=jnp.float32)
        for h in range(heads):
            o_ref[rows, h * HEAD_DIM : (h + 1) * HEAD_DIM] = mixed[
                h * ROW_TILE : (h + 1) * ROW_TILE
            ].astype(o_ref.dtype)


def rope_tables(positions):
    half_dim = HEAD_DIM // 2
    ratios = jnp.arange(half_dim, dtype=jnp.float32) * (2.0 / HEAD_DIM)
    frequency = jnp.exp(-math.log(ROPE_BASE) * ratios)
    angles = positions.astype(jnp.float32)[:, None] * frequency[None, :]
    return jnp.cos(angles), jnp.sin(angles)


def attention_kernel_call(
    query_a, query_b, cols, own_rows, other_rows, core_flag, cosine, sine, row_seg, col_seg
):
    rows = query_a.shape[0]
    half_dim = HEAD_DIM // 2
    vmem = pl.BlockSpec(memory_space=pltpu.VMEM)
    heads = cols // HEAD_DIM
    return pl.pallas_call(
        functools.partial(attention_kernel, heads),
        out_shape=jax.ShapeDtypeStruct((rows, cols), jnp.bfloat16),
        in_specs=[vmem] * 9,
        out_specs=vmem,
        cost_estimate=pl.CostEstimate(
            flops=4 * rows * rows * cols + 8 * rows * cols,
            transcendentals=heads * rows * rows,
            bytes_accessed=rows * cols * 6 + rows * HEAD_DIM * 4 + rows * half_dim * 8,
        ),
    )(
        query_a,
        query_b,
        own_rows,
        other_rows,
        core_flag,
        cosine,
        sine,
        row_seg,
        col_seg,
    )


def ring_gather(block, axis, stride, count):
    n = lax.psum(1, axis)
    me = lax.axis_index(axis)
    here = (me // stride) % count

    def moved(step):
        pairs = []
        for src in range(n):
            k = (src // stride) % count
            pairs.append((src, src + (((k + step) % count) - k) * stride))
        return pairs

    out = jnp.zeros((count,) + block.shape, block.dtype)
    out = lax.dynamic_update_index_in_dim(out, block, here, 0)
    from_right, from_left = block, block
    for step in range(1, count // 2 + 1):
        if step < count - step:
            from_right = lax.ppermute(from_right, axis, perm=moved(-1))
            out = lax.dynamic_update_index_in_dim(out, from_right, (here + step) % count, 0)
            from_left = lax.ppermute(from_left, axis, perm=moved(1))
        else:
            cut = lane_cut(block.shape[-1])
            from_left = jnp.concatenate(
                [
                    lax.ppermute(from_left[..., :cut], axis, perm=moved(1)),
                    lax.ppermute(from_right[..., cut:], axis, perm=moved(-1)),
                ],
                axis=-1,
            )
        out = lax.dynamic_update_index_in_dim(out, from_left, (here - step) % count, 0)
    return out


def lane_cut(width):
    return min(width, (width // 2 + 127) // 128 * 128)


def ring_matmul(rows, block, axis, stride, count, starts, wait_rows):
    n = lax.psum(1, axis)
    me = lax.axis_index(axis)
    here = (me // stride) % count
    depth = block.shape[1]

    def moved(step):
        pairs = []
        for src in range(n):
            k = (src // stride) % count
            pairs.append((src, src + (((k + step) % count) - k) * stride))
        return pairs

    def product(part, owner):
        result = None
        for piece, start in enumerate(starts(owner)):
            lhs = lax.dynamic_slice_in_dim(rows, start, depth, 1)
            term = jnp.dot(lhs, part[piece], preferred_element_type=jnp.float32)
            result = term if result is None else result + term
        return result

    total = product(block, here)
    from_right, from_left = block, block
    for step in range(1, count // 2 + 1):
        if step == 2 and wait_rows:
            rows, from_right, from_left = lax.optimization_barrier((rows, from_right, from_left))
        if step < count - step:
            from_right = lax.ppermute(from_right, axis, perm=moved(-1))
            total = total + product(from_right, (here + step) % count)
            from_left = lax.ppermute(from_left, axis, perm=moved(1))
        else:
            cut = lane_cut(block.shape[-1])
            from_left = jnp.concatenate(
                [
                    lax.ppermute(from_left[..., :cut], axis, perm=moved(1)),
                    lax.ppermute(from_right[..., cut:], axis, perm=moved(-1)),
                ],
                axis=-1,
            )
        total = total + product(from_left, (here - step) % count)
    return total


def per_device(tokens, segment_ids, norm_gain, query_weight, key_weight, value_weight):
    head_dim = HEAD_DIM
    query_cols = query_weight.shape[1]
    heads_dev = query_cols // head_dim
    group_size = HEADS // KV_HEADS
    n_weight = lax.psum(1, "weight")
    me = lax.axis_index("weight")
    core = me % 2
    first_kv = me * heads_dev // group_size
    key_block = lax.dynamic_slice_in_dim(key_weight, first_kv * head_dim, head_dim, 1)
    value_block = lax.dynamic_slice_in_dim(value_weight, first_kv * head_dim, head_dim, 1)
    kv_block = jnp.where(core == 0, key_block, value_block)
    values = tokens.astype(jnp.float32)
    inverse_rms = lax.rsqrt(jnp.mean(values * values, axis=1, keepdims=True) + EPSILON)
    normed = (values * inverse_rms * norm_gain[None, :]).astype(jnp.bfloat16)
    local_weights = jnp.concatenate([query_weight, kv_block], axis=1)
    n_batch = lax.psum(1, "batch")
    y_hi = n_batch // Z_CHIPS
    shard = local_weights.shape[0]
    yh = lax.axis_index("batch") % y_hi
    near = ring_gather(local_weights, "batch", 1, y_hi)
    others = jnp.stack([near[(yh + r) % y_hi] for r in range(1, y_hi)])
    cosine, sine = rope_tables(positions_in_segment(segment_ids))
    row_seg = jnp.broadcast_to(segment_ids[:, None], (segment_ids.shape[0], 128))
    col_seg = segment_ids[None, :]
    core_flag = jnp.full((1, 128), core, jnp.int32)
    others, cosine, sine, row_seg, col_seg, core_flag = lax.optimization_barrier(
        (others, cosine, sine, row_seg, col_seg, core_flag)
    )
    gathered = lax.all_gather(normed, "weight", axis=0, tiled=True)
    pack_rows = gathered.shape[0]
    own_part = ring_matmul(
        gathered,
        local_weights[None],
        "batch",
        y_hi,
        Z_CHIPS,
        lambda z: [(z * y_hi + yh) * shard],
        False,
    )
    other_part = ring_matmul(
        gathered,
        others,
        "batch",
        y_hi,
        Z_CHIPS,
        lambda z: [(z * y_hi + (yh + r) % y_hi) * shard for r in range(1, y_hi)],
        True,
    )
    own_rows = (own_part[:, query_cols:] + other_part[:, query_cols:]).astype(jnp.bfloat16)
    partner = [(w, w ^ 1) for w in range(n_weight)]
    other_rows = lax.ppermute(own_rows, "weight", perm=partner)
    return attention_kernel_call(
        own_part,
        other_part,
        query_cols,
        own_rows,
        other_rows,
        core_flag,
        cosine,
        sine,
        row_seg,
        col_seg,
    )


def solution(mesh):
    placed = (
        P(("batch", "weight"), None),
        P("batch"),
        P(),
        P("batch", "weight"),
        P("batch", None),
        P("batch", None),
    )
    return jax.shard_map(
        per_device, mesh=mesh, in_specs=placed, out_specs=P("batch", "weight"), check_vma=False
    )
```

```python
import functools
import math

import jax
import jax.numpy as jnp
from jax import lax
from jax.experimental import pallas as pl
from jax.experimental.pallas import tpu as pltpu
from jax.sharding import PartitionSpec as P

HEADS = 64
KV_HEADS = 8
HEAD_DIM = 128


ROPE_BASE = 500000.0
EPSILON = 1e-05

Z_CHIPS = 8


def positions_in_segment(seg_ids):
    places = jnp.arange(seg_ids.shape[0], dtype=jnp.int32)
    earlier = jnp.concatenate([seg_ids[:1] - 1, seg_ids[:-1]])
    starts = jnp.where(seg_ids != earlier, places, 0)
    leading = lax.cummax(starts, axis=0)
    return places - leading


def rotate(vectors, positions):
    half_dim = vectors.shape[-1] // 2
    ratios = jnp.arange(half_dim, dtype=jnp.float32) * (2.0 / vectors.shape[-1])
    frequency = jnp.exp(-math.log(ROPE_BASE) * ratios)
    angles = positions.astype(jnp.float32)[:, None] * frequency[None, :]
    cosine = jnp.cos(angles)[:, None, :]
    sine_part = jnp.sin(angles)[:, None, :]
    front_half = vectors[..., :half_dim]
    back_half = vectors[..., half_dim:]
    return jnp.concatenate(
        [front_half * cosine - back_half * sine_part, back_half * cosine + front_half * sine_part],
        axis=-1,
    )


def attend(grouped, rotated_keys, value_rows, seg_ids):
    scores = jnp.einsum(
        "ingd,jnd->ngij", grouped, rotated_keys, preferred_element_type=jnp.float32
    ) * grouped.shape[-1] ** (-0.5)
    places = jnp.arange(seg_ids.shape[0], dtype=jnp.int32)
    allowed = (seg_ids[:, None] == seg_ids[None, :]) & (places[None, :] <= places[:, None])
    weights = jnp.where(allowed, jnp.exp(scores), 0.0)
    probabilities = (weights / jnp.sum(weights, axis=-1, keepdims=True)).astype(jnp.bfloat16)
    mixed = jnp.einsum(
        "ngij,jnd->ingd", probabilities, value_rows, preferred_element_type=jnp.float32
    )
    return mixed.astype(jnp.bfloat16)


ROW_TILE = 64
SEGMENT_MOST = 64


def attention_kernel(heads, q_ref, k_ref, v_ref, cos_ref, sin_ref, row_seg_ref, col_seg_ref, o_ref):
    half = HEAD_DIM // 2

    def rope(x, rows):
        cosine, sine = cos_ref[rows, :], sin_ref[rows, :]
        a, b = x[:, :half], x[:, half:]
        return jnp.concatenate([a * cosine - b * sine, b * cosine + a * sine], axis=1)

    n_rows = q_ref.shape[0]
    keys = rope(k_ref[...].astype(jnp.float32), slice(0, n_rows)).astype(jnp.bfloat16)
    scale = HEAD_DIM ** (-0.5)
    reach = max(ROW_TILE, SEGMENT_MOST)
    for r0 in range(0, n_rows, ROW_TILE):
        c0 = max(0, r0 - reach)
        c1 = r0 + ROW_TILE
        rows = slice(r0, c1)
        places_i = lax.broadcasted_iota(jnp.int32, (ROW_TILE, c1 - c0), 0) + r0
        places_j = lax.broadcasted_iota(jnp.int32, (ROW_TILE, c1 - c0), 1) + c0
        allowed = (row_seg_ref[rows, :] == col_seg_ref[:, c0:c1]) & (places_j <= places_i)
        allowed = jnp.concatenate([allowed] * heads, axis=0)
        query = jnp.concatenate(
            [rope(q_ref[rows, h * HEAD_DIM : (h + 1) * HEAD_DIM], rows) for h in range(heads)],
            axis=0,
        ).astype(jnp.bfloat16)
        scores = lax.dot_general(
            query, keys[c0:c1], (((1,), (1,)), ((), ())), preferred_element_type=jnp.float32
        ) * scale
        weights = jnp.where(allowed, jnp.exp(scores), 0.0)
        total = jnp.sum(weights, axis=1, keepdims=True)
        probabilities = (weights / total).astype(jnp.bfloat16)
        mixed = jnp.dot(probabilities, v_ref[c0:c1, :], preferred_element_type=jnp.float32)
        for h in range(heads):
            o_ref[rows, h * HEAD_DIM : (h + 1) * HEAD_DIM] = mixed[
                h * ROW_TILE : (h + 1) * ROW_TILE
            ].astype(o_ref.dtype)


def rope_tables(positions):
    half_dim = HEAD_DIM // 2
    ratios = jnp.arange(half_dim, dtype=jnp.float32) * (2.0 / HEAD_DIM)
    frequency = jnp.exp(-math.log(ROPE_BASE) * ratios)
    angles = positions.astype(jnp.float32)[:, None] * frequency[None, :]
    return jnp.cos(angles), jnp.sin(angles)


def attention_kernel_call(projected, cols, key_rows, value_rows, cosine, sine, row_seg, col_seg):
    rows = projected.shape[0]
    half_dim = HEAD_DIM // 2
    vmem = pl.BlockSpec(memory_space=pltpu.VMEM)
    heads = cols // HEAD_DIM
    return pl.pallas_call(
        functools.partial(attention_kernel, heads),
        out_shape=jax.ShapeDtypeStruct((rows, cols), jnp.bfloat16),
        in_specs=[vmem] * 7,
        out_specs=vmem,
        cost_estimate=pl.CostEstimate(
            flops=4 * rows * rows * cols + 8 * rows * cols,
            transcendentals=heads * rows * rows,
            bytes_accessed=rows * cols * 6 + rows * HEAD_DIM * 4 + rows * half_dim * 8,
        ),
    )(
        projected,
        key_rows,
        value_rows,
        cosine,
        sine,
        row_seg,
        col_seg,
    )


def ring_gather(block, axis, stride, count):
    n = lax.psum(1, axis)
    me = lax.axis_index(axis)
    here = (me // stride) % count

    def moved(step):
        pairs = []
        for src in range(n):
            k = (src // stride) % count
            pairs.append((src, src + (((k + step) % count) - k) * stride))
        return pairs

    out = jnp.zeros((count,) + block.shape, block.dtype)
    out = lax.dynamic_update_index_in_dim(out, block, here, 0)
    from_right, from_left = block, block
    for step in range(1, count // 2 + 1):
        if step < count - step:
            from_right = lax.ppermute(from_right, axis, perm=moved(-1))
            out = lax.dynamic_update_index_in_dim(out, from_right, (here + step) % count, 0)
            from_left = lax.ppermute(from_left, axis, perm=moved(1))
        else:
            cut = block.shape[-2] // 2
            from_left = jnp.concatenate(
                [
                    lax.ppermute(from_left[..., :cut, :], axis, perm=moved(1)),
                    lax.ppermute(from_right[..., cut:, :], axis, perm=moved(-1)),
                ],
                axis=-2,
            )
        out = lax.dynamic_update_index_in_dim(out, from_left, (here - step) % count, 0)
    return out


def ring_matmul(rows, block, axis, stride, count, starts, wait_rows):
    n = lax.psum(1, axis)
    me = lax.axis_index(axis)
    here = (me // stride) % count
    depth = block.shape[1]

    def moved(step):
        pairs = []
        for src in range(n):
            k = (src // stride) % count
            pairs.append((src, src + (((k + step) % count) - k) * stride))
        return pairs

    def product(part, owner):
        result = None
        for piece, start in enumerate(starts(owner)):
            lhs = lax.dynamic_slice_in_dim(rows, start, depth, 1)
            term = jnp.dot(lhs, part[piece], preferred_element_type=jnp.float32)
            result = term if result is None else result + term
        return result

    total = product(block, here)
    from_right, from_left = block, block
    for step in range(1, count // 2 + 1):
        if step == 2 and wait_rows:
            rows, from_right, from_left = lax.optimization_barrier((rows, from_right, from_left))
        if step < count - step:
            from_right = lax.ppermute(from_right, axis, perm=moved(-1))
            total = total + product(from_right, (here + step) % count)
            from_left = lax.ppermute(from_left, axis, perm=moved(1))
        else:
            cut = block.shape[-2] // 2
            from_left = jnp.concatenate(
                [
                    lax.ppermute(from_left[..., :cut, :], axis, perm=moved(1)),
                    lax.ppermute(from_right[..., cut:, :], axis, perm=moved(-1)),
                ],
                axis=-2,
            )
        total = total + product(from_left, (here - step) % count)
    return total


def per_device(tokens, segment_ids, norm_gain, query_weight, key_weight, value_weight):
    head_dim = HEAD_DIM
    query_cols = query_weight.shape[1]
    heads_dev = query_cols // head_dim
    group_size = HEADS // KV_HEADS
    n_weight = lax.psum(1, "weight")
    me = lax.axis_index("weight")
    core = me % 2
    first_kv = me * heads_dev // group_size
    key_block = lax.dynamic_slice_in_dim(key_weight, first_kv * head_dim, head_dim, 1)
    value_block = lax.dynamic_slice_in_dim(value_weight, first_kv * head_dim, head_dim, 1)
    kv_block = jnp.where(core == 0, key_block, value_block)
    values = tokens.astype(jnp.float32)
    inverse_rms = lax.rsqrt(jnp.mean(values * values, axis=1, keepdims=True) + EPSILON)
    normed = (values * inverse_rms * norm_gain[None, :]).astype(jnp.bfloat16)
    local_weights = jnp.concatenate([query_weight, kv_block], axis=1)
    n_batch = lax.psum(1, "batch")
    y_hi = n_batch // Z_CHIPS
    shard = local_weights.shape[0]
    yh = lax.axis_index("batch") % y_hi
    near = ring_gather(local_weights, "batch", 1, y_hi)
    others = jnp.stack([near[(yh + r) % y_hi] for r in range(1, y_hi)])
    cosine, sine = rope_tables(positions_in_segment(segment_ids))
    row_seg, col_seg = segment_ids[:, None], segment_ids[None, :]
    others, cosine, sine, row_seg, col_seg = lax.optimization_barrier(
        (others, cosine, sine, row_seg, col_seg)
    )
    gathered = lax.all_gather(normed, "weight", axis=0, tiled=True)
    pack_rows = gathered.shape[0]
    own_part = ring_matmul(
        gathered,
        local_weights[None],
        "batch",
        y_hi,
        Z_CHIPS,
        lambda z: [(z * y_hi + yh) * shard],
        False,
    )
    other_part = ring_matmul(
        gathered,
        others,
        "batch",
        y_hi,
        Z_CHIPS,
        lambda z: [(z * y_hi + (yh + r) % y_hi) * shard for r in range(1, y_hi)],
        True,
    )
    projected = own_part + other_part
    own_rows = projected[:, query_cols:].astype(jnp.bfloat16)
    partner = [(w, w ^ 1) for w in range(n_weight)]
    other_rows = lax.ppermute(own_rows, "weight", perm=partner)
    key_rows = jnp.where(core == 0, own_rows, other_rows)
    value_rows = jnp.where(core == 0, other_rows, own_rows)
    return attention_kernel_call(
        projected, query_cols, key_rows, value_rows, cosine, sine, row_seg, col_seg
    )


def solution(mesh):
    placed = (
        P(("batch", "weight"), None),
        P("batch"),
        P(),
        P("batch", "weight"),
        P("batch", None),
        P("batch", None),
    )
    return jax.shard_map(
        per_device, mesh=mesh, in_specs=placed, out_specs=P("batch", "weight"), check_vma=False
    )
```

```python
import functools
import math

import jax
import jax.numpy as jnp
from jax import lax
from jax.experimental import pallas as pl
from jax.experimental.pallas import tpu as pltpu
from jax.sharding import PartitionSpec as P

HEADS = 64
KV_HEADS = 8
HEAD_DIM = 128


ROPE_BASE = 500000.0
EPSILON = 1e-05

Z_CHIPS = 8


def positions_in_segment(seg_ids):
    places = jnp.arange(seg_ids.shape[0], dtype=jnp.int32)
    earlier = jnp.concatenate([seg_ids[:1] - 1, seg_ids[:-1]])
    starts = jnp.where(seg_ids != earlier, places, 0)
    leading = lax.cummax(starts, axis=0)
    return places - leading


def rotate(vectors, positions):
    half_dim = vectors.shape[-1] // 2
    ratios = jnp.arange(half_dim, dtype=jnp.float32) * (2.0 / vectors.shape[-1])
    frequency = jnp.exp(-math.log(ROPE_BASE) * ratios)
    angles = positions.astype(jnp.float32)[:, None] * frequency[None, :]
    cosine = jnp.cos(angles)[:, None, :]
    sine_part = jnp.sin(angles)[:, None, :]
    front_half = vectors[..., :half_dim]
    back_half = vectors[..., half_dim:]
    return jnp.concatenate(
        [front_half * cosine - back_half * sine_part, back_half * cosine + front_half * sine_part],
        axis=-1,
    )


def attend(grouped, rotated_keys, value_rows, seg_ids):
    scores = jnp.einsum(
        "ingd,jnd->ngij", grouped, rotated_keys, preferred_element_type=jnp.float32
    ) * grouped.shape[-1] ** (-0.5)
    places = jnp.arange(seg_ids.shape[0], dtype=jnp.int32)
    allowed = (seg_ids[:, None] == seg_ids[None, :]) & (places[None, :] <= places[:, None])
    weights = jnp.where(allowed, jnp.exp(scores), 0.0)
    probabilities = (weights / jnp.sum(weights, axis=-1, keepdims=True)).astype(jnp.bfloat16)
    mixed = jnp.einsum(
        "ngij,jnd->ingd", probabilities, value_rows, preferred_element_type=jnp.float32
    )
    return mixed.astype(jnp.bfloat16)


ROW_TILE = 64
SEGMENT_MOST = 64


def attention_kernel(heads, q_ref, k_ref, v_ref, cos_ref, sin_ref, row_seg_ref, col_seg_ref, o_ref):
    half = HEAD_DIM // 2

    def rope(x, rows):
        cosine, sine = cos_ref[rows, :], sin_ref[rows, :]
        a, b = x[:, :half], x[:, half:]
        return jnp.concatenate([a * cosine - b * sine, b * cosine + a * sine], axis=1)

    n_rows = q_ref.shape[0]
    keys = rope(k_ref[...].astype(jnp.float32), slice(0, n_rows)).astype(jnp.bfloat16)
    scale = HEAD_DIM ** (-0.5)
    reach = max(ROW_TILE, SEGMENT_MOST)
    for r0 in range(0, n_rows, ROW_TILE):
        c0 = max(0, r0 - reach)
        c1 = r0 + ROW_TILE
        rows = slice(r0, c1)
        places_i = lax.broadcasted_iota(jnp.int32, (ROW_TILE, c1 - c0), 0) + r0
        places_j = lax.broadcasted_iota(jnp.int32, (ROW_TILE, c1 - c0), 1) + c0
        allowed = (row_seg_ref[rows, :] == col_seg_ref[:, c0:c1]) & (places_j <= places_i)
        allowed = jnp.concatenate([allowed] * heads, axis=0)
        query = jnp.concatenate(
            [rope(q_ref[rows, h * HEAD_DIM : (h + 1) * HEAD_DIM], rows) for h in range(heads)],
            axis=0,
        ).astype(jnp.bfloat16)
        scores = lax.dot_general(
            query, keys[c0:c1], (((1,), (1,)), ((), ())), preferred_element_type=jnp.float32
        ) * scale
        weights = jnp.where(allowed, jnp.exp(scores), 0.0)
        total = jnp.sum(weights, axis=1, keepdims=True)
        probabilities = (weights / total).astype(jnp.bfloat16)
        mixed = jnp.dot(probabilities, v_ref[c0:c1, :], preferred_element_type=jnp.float32)
        for h in range(heads):
            o_ref[rows, h * HEAD_DIM : (h + 1) * HEAD_DIM] = mixed[
                h * ROW_TILE : (h + 1) * ROW_TILE
            ].astype(o_ref.dtype)


def rope_tables(positions):
    half_dim = HEAD_DIM // 2
    ratios = jnp.arange(half_dim, dtype=jnp.float32) * (2.0 / HEAD_DIM)
    frequency = jnp.exp(-math.log(ROPE_BASE) * ratios)
    angles = positions.astype(jnp.float32)[:, None] * frequency[None, :]
    return jnp.cos(angles), jnp.sin(angles)


def attention_kernel_call(projected, cols, key_rows, value_rows, cosine, sine, row_seg, col_seg):
    rows = projected.shape[0]
    half_dim = HEAD_DIM // 2
    vmem = pl.BlockSpec(memory_space=pltpu.VMEM)
    heads = cols // HEAD_DIM
    return pl.pallas_call(
        functools.partial(attention_kernel, heads),
        out_shape=jax.ShapeDtypeStruct((rows, cols), jnp.bfloat16),
        in_specs=[vmem] * 7,
        out_specs=vmem,
        cost_estimate=pl.CostEstimate(
            flops=4 * rows * rows * cols + 8 * rows * cols,
            transcendentals=heads * rows * rows,
            bytes_accessed=rows * cols * 6 + rows * HEAD_DIM * 4 + rows * half_dim * 8,
        ),
    )(
        projected,
        key_rows,
        value_rows,
        cosine,
        sine,
        row_seg,
        col_seg,
    )


def ring_arrivals(block, axis, stride, count):
    n = lax.psum(1, axis)

    def moved(step):
        pairs = []
        for src in range(n):
            k = (src // stride) % count
            pairs.append((src, src + (((k + step) % count) - k) * stride))
        return pairs

    steps = []
    from_right, from_left = block, block
    for step in range(1, count // 2 + 1):
        if step < count - step:
            from_right = lax.ppermute(from_right, axis, perm=moved(-1))
            from_left = lax.ppermute(from_left, axis, perm=moved(1))
            steps.append([(from_right, step), (from_left, -step)])
        else:
            cut = block.shape[-2] // 2
            from_left = jnp.concatenate(
                [
                    lax.ppermute(from_left[..., :cut, :], axis, perm=moved(1)),
                    lax.ppermute(from_right[..., cut:, :], axis, perm=moved(-1)),
                ],
                axis=-2,
            )
            steps.append([(from_left, -step)])
    return steps


def ring_matmul(rows, block, axis, stride, count, starts, wait_rows):
    n = lax.psum(1, axis)
    me = lax.axis_index(axis)
    here = (me // stride) % count
    depth = block.shape[1]

    def moved(step):
        pairs = []
        for src in range(n):
            k = (src // stride) % count
            pairs.append((src, src + (((k + step) % count) - k) * stride))
        return pairs

    def product(part, owner):
        result = None
        for piece, start in enumerate(starts(owner)):
            lhs = lax.dynamic_slice_in_dim(rows, start, depth, 1)
            term = jnp.dot(lhs, part[piece], preferred_element_type=jnp.float32)
            result = term if result is None else result + term
        return result

    total = product(block, here)
    from_right, from_left = block, block
    for step in range(1, count // 2 + 1):
        if step == 2 and wait_rows:
            rows, from_right, from_left = lax.optimization_barrier((rows, from_right, from_left))
        if step < count - step:
            from_right = lax.ppermute(from_right, axis, perm=moved(-1))
            total = total + product(from_right, (here + step) % count)
            from_left = lax.ppermute(from_left, axis, perm=moved(1))
        else:
            cut = block.shape[-2] // 2
            from_left = jnp.concatenate(
                [
                    lax.ppermute(from_left[..., :cut, :], axis, perm=moved(1)),
                    lax.ppermute(from_right[..., cut:, :], axis, perm=moved(-1)),
                ],
                axis=-2,
            )
        total = total + product(from_left, (here - step) % count)
    return total


def per_device(tokens, segment_ids, norm_gain, query_weight, key_weight, value_weight):
    head_dim = HEAD_DIM
    query_cols = query_weight.shape[1]
    heads_dev = query_cols // head_dim
    group_size = HEADS // KV_HEADS
    n_weight = lax.psum(1, "weight")
    me = lax.axis_index("weight")
    core = me % 2
    first_kv = me * heads_dev // group_size
    key_block = lax.dynamic_slice_in_dim(key_weight, first_kv * head_dim, head_dim, 1)
    value_block = lax.dynamic_slice_in_dim(value_weight, first_kv * head_dim, head_dim, 1)
    kv_block = jnp.where(core == 0, key_block, value_block)
    values = tokens.astype(jnp.float32)
    inverse_rms = lax.rsqrt(jnp.mean(values * values, axis=1, keepdims=True) + EPSILON)
    normed = (values * inverse_rms * norm_gain[None, :]).astype(jnp.bfloat16)
    local_weights = jnp.concatenate([query_weight, kv_block], axis=1)
    n_batch = lax.psum(1, "batch")
    y_hi = n_batch // Z_CHIPS
    shard = local_weights.shape[0]
    yh = lax.axis_index("batch") % y_hi
    arrivals = ring_arrivals(local_weights, "batch", 1, y_hi)
    first = jnp.stack([part for part, _ in arrivals[0]])
    first_offsets = [offset for _, offset in arrivals[0]]
    rest = jnp.stack([part for step in arrivals[1:] for part, _ in step])
    rest_offsets = [offset for step in arrivals[1:] for _, offset in step]
    cosine, sine = rope_tables(positions_in_segment(segment_ids))
    row_seg, col_seg = segment_ids[:, None], segment_ids[None, :]
    first, cosine, sine, row_seg, col_seg = lax.optimization_barrier(
        (first, cosine, sine, row_seg, col_seg)
    )
    gathered = lax.all_gather(normed, "weight", axis=0, tiled=True)
    pack_rows = gathered.shape[0]

    def starts_of(offsets):
        return lambda z: [(z * y_hi + (yh + r) % y_hi) * shard for r in offsets]

    projected = ring_matmul(
        gathered, local_weights[None], "batch", y_hi, Z_CHIPS, starts_of([0]), False
    )
    projected = projected + ring_matmul(
        gathered, first, "batch", y_hi, Z_CHIPS, starts_of(first_offsets), True
    )
    projected = projected + ring_matmul(
        gathered, rest, "batch", y_hi, Z_CHIPS, starts_of(rest_offsets), False
    )
    own_rows = projected[:, query_cols:].astype(jnp.bfloat16)
    partner = [(w, w ^ 1) for w in range(n_weight)]
    other_rows = lax.ppermute(own_rows, "weight", perm=partner)
    key_rows = jnp.where(core == 0, own_rows, other_rows)
    value_rows = jnp.where(core == 0, other_rows, own_rows)
    return attention_kernel_call(
        projected, query_cols, key_rows, value_rows, cosine, sine, row_seg, col_seg
    )


def solution(mesh):
    placed = (
        P(("batch", "weight"), None),
        P("batch"),
        P(),
        P("batch", "weight"),
        P("batch", None),
        P("batch", None),
    )
    return jax.shard_map(
        per_device, mesh=mesh, in_specs=placed, out_specs=P("batch", "weight"), check_vma=False
    )
```

```python
import functools
import math

import jax
import jax.numpy as jnp
from jax import lax
from jax.experimental import pallas as pl
from jax.experimental.pallas import tpu as pltpu
from jax.sharding import PartitionSpec as P

HEADS = 64
KV_HEADS = 8
HEAD_DIM = 128


ROPE_BASE = 500000.0
EPSILON = 1e-05

Z_CHIPS = 8


def positions_in_segment(seg_ids):
    places = jnp.arange(seg_ids.shape[0], dtype=jnp.int32)
    earlier = jnp.concatenate([seg_ids[:1] - 1, seg_ids[:-1]])
    starts = jnp.where(seg_ids != earlier, places, 0)
    leading = lax.cummax(starts, axis=0)
    return places - leading


def rotate(vectors, positions):
    half_dim = vectors.shape[-1] // 2
    ratios = jnp.arange(half_dim, dtype=jnp.float32) * (2.0 / vectors.shape[-1])
    frequency = jnp.exp(-math.log(ROPE_BASE) * ratios)
    angles = positions.astype(jnp.float32)[:, None] * frequency[None, :]
    cosine = jnp.cos(angles)[:, None, :]
    sine_part = jnp.sin(angles)[:, None, :]
    front_half = vectors[..., :half_dim]
    back_half = vectors[..., half_dim:]
    return jnp.concatenate(
        [front_half * cosine - back_half * sine_part, back_half * cosine + front_half * sine_part],
        axis=-1,
    )


def attend(grouped, rotated_keys, value_rows, seg_ids):
    scores = jnp.einsum(
        "ingd,jnd->ngij", grouped, rotated_keys, preferred_element_type=jnp.float32
    ) * grouped.shape[-1] ** (-0.5)
    places = jnp.arange(seg_ids.shape[0], dtype=jnp.int32)
    allowed = (seg_ids[:, None] == seg_ids[None, :]) & (places[None, :] <= places[:, None])
    weights = jnp.where(allowed, jnp.exp(scores), 0.0)
    probabilities = (weights / jnp.sum(weights, axis=-1, keepdims=True)).astype(jnp.bfloat16)
    mixed = jnp.einsum(
        "ngij,jnd->ingd", probabilities, value_rows, preferred_element_type=jnp.float32
    )
    return mixed.astype(jnp.bfloat16)


ROW_TILE = 128
SEGMENT_MOST = 64


def attention_kernel(heads, q_ref, k_ref, v_ref, cos_ref, sin_ref, row_seg_ref, col_seg_ref, o_ref):
    half = HEAD_DIM // 2

    def rope(x, rows):
        cosine, sine = cos_ref[rows, :], sin_ref[rows, :]
        a, b = x[:, :half], x[:, half:]
        return jnp.concatenate([a * cosine - b * sine, b * cosine + a * sine], axis=1)

    n_rows = q_ref.shape[0]
    keys = rope(k_ref[...].astype(jnp.float32), slice(0, n_rows)).astype(jnp.bfloat16)
    scale = HEAD_DIM ** (-0.5)
    reach = max(ROW_TILE, SEGMENT_MOST)
    for r0 in range(0, n_rows, ROW_TILE):
        c0 = max(0, r0 - reach)
        c1 = r0 + ROW_TILE
        rows = slice(r0, c1)
        places_i = lax.broadcasted_iota(jnp.int32, (ROW_TILE, c1 - c0), 0) + r0
        places_j = lax.broadcasted_iota(jnp.int32, (ROW_TILE, c1 - c0), 1) + c0
        allowed = (row_seg_ref[rows, :] == col_seg_ref[:, c0:c1]) & (places_j <= places_i)
        allowed = jnp.concatenate([allowed] * heads, axis=0)
        query = jnp.concatenate(
            [rope(q_ref[rows, h * HEAD_DIM : (h + 1) * HEAD_DIM], rows) for h in range(heads)],
            axis=0,
        ).astype(jnp.bfloat16)
        scores = lax.dot_general(
            query, keys[c0:c1], (((1,), (1,)), ((), ())), preferred_element_type=jnp.float32
        ) * scale
        weights = jnp.where(allowed, jnp.exp(scores), 0.0)
        total = jnp.sum(weights, axis=1, keepdims=True)
        probabilities = (weights / total).astype(jnp.bfloat16)
        mixed = jnp.dot(probabilities, v_ref[c0:c1, :], preferred_element_type=jnp.float32)
        for h in range(heads):
            o_ref[rows, h * HEAD_DIM : (h + 1) * HEAD_DIM] = mixed[
                h * ROW_TILE : (h + 1) * ROW_TILE
            ].astype(o_ref.dtype)


def rope_tables(positions):
    half_dim = HEAD_DIM // 2
    ratios = jnp.arange(half_dim, dtype=jnp.float32) * (2.0 / HEAD_DIM)
    frequency = jnp.exp(-math.log(ROPE_BASE) * ratios)
    angles = positions.astype(jnp.float32)[:, None] * frequency[None, :]
    return jnp.cos(angles), jnp.sin(angles)


def attention_kernel_call(projected, cols, key_rows, value_rows, cosine, sine, row_seg, col_seg):
    rows = projected.shape[0]
    half_dim = HEAD_DIM // 2
    vmem = pl.BlockSpec(memory_space=pltpu.VMEM)
    heads = cols // HEAD_DIM
    return pl.pallas_call(
        functools.partial(attention_kernel, heads),
        out_shape=jax.ShapeDtypeStruct((rows, cols), jnp.bfloat16),
        in_specs=[vmem] * 7,
        out_specs=vmem,
        cost_estimate=pl.CostEstimate(
            flops=4 * rows * rows * cols + 8 * rows * cols,
            transcendentals=heads * rows * rows,
            bytes_accessed=rows * cols * 6 + rows * HEAD_DIM * 4 + rows * half_dim * 8,
        ),
    )(
        projected,
        key_rows,
        value_rows,
        cosine,
        sine,
        row_seg,
        col_seg,
    )


def ring_gather(block, axis, stride, count):
    n = lax.psum(1, axis)
    me = lax.axis_index(axis)
    here = (me // stride) % count

    def moved(step):
        pairs = []
        for src in range(n):
            k = (src // stride) % count
            pairs.append((src, src + (((k + step) % count) - k) * stride))
        return pairs

    out = jnp.zeros((count,) + block.shape, block.dtype)
    out = lax.dynamic_update_index_in_dim(out, block, here, 0)
    from_right, from_left = block, block
    for step in range(1, count // 2 + 1):
        if step < count - step:
            from_right = lax.ppermute(from_right, axis, perm=moved(-1))
            out = lax.dynamic_update_index_in_dim(out, from_right, (here + step) % count, 0)
            from_left = lax.ppermute(from_left, axis, perm=moved(1))
        else:
            cut = block.shape[-2] // 2
            from_left = jnp.concatenate(
                [
                    lax.ppermute(from_left[..., :cut, :], axis, perm=moved(1)),
                    lax.ppermute(from_right[..., cut:, :], axis, perm=moved(-1)),
                ],
                axis=-2,
            )
        out = lax.dynamic_update_index_in_dim(out, from_left, (here - step) % count, 0)
    return out


def ring_matmul(rows, block, axis, stride, count, starts, wait_rows):
    n = lax.psum(1, axis)
    me = lax.axis_index(axis)
    here = (me // stride) % count
    depth = block.shape[1]

    def moved(step):
        pairs = []
        for src in range(n):
            k = (src // stride) % count
            pairs.append((src, src + (((k + step) % count) - k) * stride))
        return pairs

    def product(part, owner):
        result = None
        for piece, start in enumerate(starts(owner)):
            lhs = lax.dynamic_slice_in_dim(rows, start, depth, 1)
            term = jnp.dot(lhs, part[piece], preferred_element_type=jnp.float32)
            result = term if result is None else result + term
        return result

    total = product(block, here)
    from_right, from_left = block, block
    for step in range(1, count // 2 + 1):
        if step == 2 and wait_rows:
            rows, from_right, from_left = lax.optimization_barrier((rows, from_right, from_left))
        if step < count - step:
            from_right = lax.ppermute(from_right, axis, perm=moved(-1))
            total = total + product(from_right, (here + step) % count)
            from_left = lax.ppermute(from_left, axis, perm=moved(1))
        else:
            cut = block.shape[-2] // 2
            from_left = jnp.concatenate(
                [
                    lax.ppermute(from_left[..., :cut, :], axis, perm=moved(1)),
                    lax.ppermute(from_right[..., cut:, :], axis, perm=moved(-1)),
                ],
                axis=-2,
            )
        total = total + product(from_left, (here - step) % count)
    return total


def per_device(tokens, segment_ids, norm_gain, query_weight, key_weight, value_weight):
    head_dim = HEAD_DIM
    query_cols = query_weight.shape[1]
    heads_dev = query_cols // head_dim
    group_size = HEADS // KV_HEADS
    n_weight = lax.psum(1, "weight")
    me = lax.axis_index("weight")
    core = me % 2
    first_kv = me * heads_dev // group_size
    key_block = lax.dynamic_slice_in_dim(key_weight, first_kv * head_dim, head_dim, 1)
    value_block = lax.dynamic_slice_in_dim(value_weight, first_kv * head_dim, head_dim, 1)
    kv_block = jnp.where(core == 0, key_block, value_block)
    values = tokens.astype(jnp.float32)
    inverse_rms = lax.rsqrt(jnp.mean(values * values, axis=1, keepdims=True) + EPSILON)
    normed = (values * inverse_rms * norm_gain[None, :]).astype(jnp.bfloat16)
    local_weights = jnp.concatenate([query_weight, kv_block], axis=1)
    n_batch = lax.psum(1, "batch")
    y_hi = n_batch // Z_CHIPS
    shard = local_weights.shape[0]
    yh = lax.axis_index("batch") % y_hi
    near = ring_gather(local_weights, "batch", 1, y_hi)
    others = jnp.stack([near[(yh + r) % y_hi] for r in range(1, y_hi)])
    cosine, sine = rope_tables(positions_in_segment(segment_ids))
    row_seg, col_seg = segment_ids[:, None], segment_ids[None, :]
    others, cosine, sine, row_seg, col_seg = lax.optimization_barrier(
        (others, cosine, sine, row_seg, col_seg)
    )
    gathered = lax.all_gather(normed, "weight", axis=0, tiled=True)
    pack_rows = gathered.shape[0]
    own_part = ring_matmul(
        gathered,
        local_weights[None],
        "batch",
        y_hi,
        Z_CHIPS,
        lambda z: [(z * y_hi + yh) * shard],
        False,
    )
    other_part = ring_matmul(
        gathered,
        others,
        "batch",
        y_hi,
        Z_CHIPS,
        lambda z: [(z * y_hi + (yh + r) % y_hi) * shard for r in range(1, y_hi)],
        True,
    )
    projected = own_part + other_part
    own_rows = projected[:, query_cols:].astype(jnp.bfloat16)
    partner = [(w, w ^ 1) for w in range(n_weight)]
    other_rows = lax.ppermute(own_rows, "weight", perm=partner)
    key_rows = jnp.where(core == 0, own_rows, other_rows)
    value_rows = jnp.where(core == 0, other_rows, own_rows)
    return attention_kernel_call(
        projected, query_cols, key_rows, value_rows, cosine, sine, row_seg, col_seg
    )


def solution(mesh):
    placed = (
        P(("batch", "weight"), None),
        P("batch"),
        P(),
        P("batch", "weight"),
        P("batch", None),
        P("batch", None),
    )
    return jax.shard_map(
        per_device, mesh=mesh, in_specs=placed, out_specs=P("batch", "weight"), check_vma=False
    )
```

```python
import functools
import math

import jax
import jax.numpy as jnp
from jax import lax
from jax.experimental import pallas as pl
from jax.experimental.pallas import tpu as pltpu
from jax.sharding import PartitionSpec as P

HEADS = 64
KV_HEADS = 8
HEAD_DIM = 128


ROPE_BASE = 500000.0
EPSILON = 1e-05

Z_CHIPS = 8


def positions_in_segment(seg_ids):
    places = jnp.arange(seg_ids.shape[0], dtype=jnp.int32)
    earlier = jnp.concatenate([seg_ids[:1] - 1, seg_ids[:-1]])
    starts = jnp.where(seg_ids != earlier, places, 0)
    leading = lax.cummax(starts, axis=0)
    return places - leading


def rotate(vectors, positions):
    half_dim = vectors.shape[-1] // 2
    ratios = jnp.arange(half_dim, dtype=jnp.float32) * (2.0 / vectors.shape[-1])
    frequency = jnp.exp(-math.log(ROPE_BASE) * ratios)
    angles = positions.astype(jnp.float32)[:, None] * frequency[None, :]
    cosine = jnp.cos(angles)[:, None, :]
    sine_part = jnp.sin(angles)[:, None, :]
    front_half = vectors[..., :half_dim]
    back_half = vectors[..., half_dim:]
    return jnp.concatenate(
        [front_half * cosine - back_half * sine_part, back_half * cosine + front_half * sine_part],
        axis=-1,
    )


def attend(grouped, rotated_keys, value_rows, seg_ids):
    scores = jnp.einsum(
        "ingd,jnd->ngij", grouped, rotated_keys, preferred_element_type=jnp.float32
    ) * grouped.shape[-1] ** (-0.5)
    places = jnp.arange(seg_ids.shape[0], dtype=jnp.int32)
    allowed = (seg_ids[:, None] == seg_ids[None, :]) & (places[None, :] <= places[:, None])
    weights = jnp.where(allowed, jnp.exp(scores), 0.0)
    probabilities = (weights / jnp.sum(weights, axis=-1, keepdims=True)).astype(jnp.bfloat16)
    mixed = jnp.einsum(
        "ngij,jnd->ingd", probabilities, value_rows, preferred_element_type=jnp.float32
    )
    return mixed.astype(jnp.bfloat16)


ROW_TILE = 128
SEGMENT_MOST = 64


def attention_kernel(heads, q_ref, k_ref, v_ref, cos_ref, sin_ref, row_seg_ref, col_seg_ref, o_ref):
    half = HEAD_DIM // 2

    def rope(x, rows):
        cosine, sine = cos_ref[rows, :], sin_ref[rows, :]
        a, b = x[:, :half], x[:, half:]
        return jnp.concatenate([a * cosine - b * sine, b * cosine + a * sine], axis=1)

    n_rows = q_ref.shape[0]
    keys = rope(k_ref[...].astype(jnp.float32), slice(0, n_rows)).astype(jnp.bfloat16)
    scale = HEAD_DIM ** (-0.5)
    reach = max(ROW_TILE, SEGMENT_MOST)
    for r0 in range(0, n_rows, ROW_TILE):
        c0 = max(0, r0 - reach)
        c1 = r0 + ROW_TILE
        rows = slice(r0, c1)
        places_i = lax.broadcasted_iota(jnp.int32, (ROW_TILE, c1 - c0), 0) + r0
        places_j = lax.broadcasted_iota(jnp.int32, (ROW_TILE, c1 - c0), 1) + c0
        allowed = (row_seg_ref[rows, :] == col_seg_ref[:, c0:c1]) & (places_j <= places_i)
        allowed = jnp.concatenate([allowed] * heads, axis=0)
        query = jnp.concatenate(
            [rope(q_ref[rows, h * HEAD_DIM : (h + 1) * HEAD_DIM], rows) for h in range(heads)],
            axis=0,
        ).astype(jnp.bfloat16)
        scores = lax.dot_general(
            query, keys[c0:c1], (((1,), (1,)), ((), ())), preferred_element_type=jnp.float32
        ) * scale
        weights = jnp.where(allowed, jnp.exp(scores), 0.0)
        total = jnp.sum(weights, axis=1, keepdims=True)
        probabilities = (weights / total).astype(jnp.bfloat16)
        mixed = jnp.dot(probabilities, v_ref[c0:c1, :], preferred_element_type=jnp.float32)
        for h in range(heads):
            o_ref[rows, h * HEAD_DIM : (h + 1) * HEAD_DIM] = mixed[
                h * ROW_TILE : (h + 1) * ROW_TILE
            ].astype(o_ref.dtype)


def rope_tables(positions):
    half_dim = HEAD_DIM // 2
    ratios = jnp.arange(half_dim, dtype=jnp.float32) * (2.0 / HEAD_DIM)
    frequency = jnp.exp(-math.log(ROPE_BASE) * ratios)
    angles = positions.astype(jnp.float32)[:, None] * frequency[None, :]
    return jnp.cos(angles), jnp.sin(angles)


def attention_kernel_call(projected, cols, key_rows, value_rows, cosine, sine, row_seg, col_seg):
    rows = projected.shape[0]
    half_dim = HEAD_DIM // 2
    vmem = pl.BlockSpec(memory_space=pltpu.VMEM)
    heads = cols // HEAD_DIM
    return pl.pallas_call(
        functools.partial(attention_kernel, heads),
        out_shape=jax.ShapeDtypeStruct((rows, cols), jnp.bfloat16),
        in_specs=[vmem] * 7,
        out_specs=vmem,
        cost_estimate=pl.CostEstimate(
            flops=4 * rows * rows * cols + 8 * rows * cols,
            transcendentals=heads * rows * rows,
            bytes_accessed=rows * cols * 6 + rows * HEAD_DIM * 4 + rows * half_dim * 8,
        ),
    )(
        projected,
        key_rows,
        value_rows,
        cosine,
        sine,
        row_seg,
        col_seg,
    )


def ring_gather(block, axis, stride, count):
    n = lax.psum(1, axis)
    me = lax.axis_index(axis)
    here = (me // stride) % count

    def moved(step):
        pairs = []
        for src in range(n):
            k = (src // stride) % count
            pairs.append((src, src + (((k + step) % count) - k) * stride))
        return pairs

    out = jnp.zeros((count,) + block.shape, block.dtype)
    out = lax.dynamic_update_index_in_dim(out, block, here, 0)
    from_right, from_left = block, block
    for step in range(1, count // 2 + 1):
        if step < count - step:
            from_right = lax.ppermute(from_right, axis, perm=moved(-1))
            out = lax.dynamic_update_index_in_dim(out, from_right, (here + step) % count, 0)
            from_left = lax.ppermute(from_left, axis, perm=moved(1))
        else:
            cut = block.shape[-2] // 2
            from_left = jnp.concatenate(
                [
                    lax.ppermute(from_left[..., :cut, :], axis, perm=moved(1)),
                    lax.ppermute(from_right[..., cut:, :], axis, perm=moved(-1)),
                ],
                axis=-2,
            )
        out = lax.dynamic_update_index_in_dim(out, from_left, (here - step) % count, 0)
    return out


def ring_matmul(rows, block, axis, stride, count, starts, wait_rows):
    n = lax.psum(1, axis)
    me = lax.axis_index(axis)
    here = (me // stride) % count
    depth = block.shape[1]

    def moved(step):
        pairs = []
        for src in range(n):
            k = (src // stride) % count
            pairs.append((src, src + (((k + step) % count) - k) * stride))
        return pairs

    def product(part, owner):
        result = None
        for piece, start in enumerate(starts(owner)):
            lhs = lax.dynamic_slice_in_dim(rows, start, depth, 1)
            term = jnp.dot(lhs, part[piece], preferred_element_type=jnp.float32)
            result = term if result is None else result + term
        return result

    total = product(block, here)
    from_right, from_left = block, block
    for step in range(1, count // 2 + 1):
        if step == 2 and wait_rows:
            rows, from_right, from_left = lax.optimization_barrier((rows, from_right, from_left))
        if step < count - step:
            from_right = lax.ppermute(from_right, axis, perm=moved(-1))
            total = total + product(from_right, (here + step) % count)
            from_left = lax.ppermute(from_left, axis, perm=moved(1))
        else:
            cut = block.shape[-2] // 2
            from_left = jnp.concatenate(
                [
                    lax.ppermute(from_left[..., :cut, :], axis, perm=moved(1)),
                    lax.ppermute(from_right[..., cut:, :], axis, perm=moved(-1)),
                ],
                axis=-2,
            )
        total = total + product(from_left, (here - step) % count)
    return total


def per_device(tokens, segment_ids, norm_gain, query_weight, key_weight, value_weight):
    head_dim = HEAD_DIM
    query_cols = query_weight.shape[1]
    heads_dev = query_cols // head_dim
    group_size = HEADS // KV_HEADS
    n_weight = lax.psum(1, "weight")
    me = lax.axis_index("weight")
    core = me % 2
    first_kv = me * heads_dev // group_size
    key_block = lax.dynamic_slice_in_dim(key_weight, first_kv * head_dim, head_dim, 1)
    value_block = lax.dynamic_slice_in_dim(value_weight, first_kv * head_dim, head_dim, 1)
    kv_block = jnp.where(core == 0, key_block, value_block)
    values = tokens.astype(jnp.float32)
    inverse_rms = lax.rsqrt(jnp.mean(values * values, axis=1, keepdims=True) + EPSILON)
    normed = (values * inverse_rms * norm_gain[None, :]).astype(jnp.bfloat16)
    local_weights = jnp.concatenate([query_weight, kv_block], axis=1)
    n_batch = lax.psum(1, "batch")
    y_hi = n_batch // Z_CHIPS
    shard = local_weights.shape[0]
    yh = lax.axis_index("batch") % y_hi
    near = ring_gather(local_weights, "batch", 1, y_hi)
    others = jnp.stack([near[(yh + r) % y_hi] for r in range(1, y_hi)])
    cosine, sine = rope_tables(positions_in_segment(segment_ids))
    row_seg, col_seg = segment_ids[:, None], segment_ids[None, :]
    own_blocks = ring_gather(local_weights, "batch", y_hi, Z_CHIPS)
    others, own_blocks, cosine, sine, row_seg, col_seg = lax.optimization_barrier(
        (others, own_blocks, cosine, sine, row_seg, col_seg)
    )
    gathered = lax.all_gather(normed, "weight", axis=0, tiled=True)
    pack_rows = gathered.shape[0]
    other_part = ring_matmul(
        gathered,
        others,
        "batch",
        y_hi,
        Z_CHIPS,
        lambda z: [(z * y_hi + (yh + r) % y_hi) * shard for r in range(1, y_hi)],
        True,
    )
    own_rows_of_z = lax.dynamic_index_in_dim(
        gathered.reshape(pack_rows, Z_CHIPS, y_hi, shard), yh, axis=2, keepdims=False
    )
    own_part = jnp.einsum(
        "tzr,zrc->tc", own_rows_of_z, own_blocks, preferred_element_type=jnp.float32
    )
    projected = own_part + other_part
    own_rows = projected[:, query_cols:].astype(jnp.bfloat16)
    partner = [(w, w ^ 1) for w in range(n_weight)]
    other_rows = lax.ppermute(own_rows, "weight", perm=partner)
    key_rows = jnp.where(core == 0, own_rows, other_rows)
    value_rows = jnp.where(core == 0, other_rows, own_rows)
    return attention_kernel_call(
        projected, query_cols, key_rows, value_rows, cosine, sine, row_seg, col_seg
    )


def solution(mesh):
    placed = (
        P(("batch", "weight"), None),
        P("batch"),
        P(),
        P("batch", "weight"),
        P("batch", None),
        P("batch", None),
    )
    return jax.shard_map(
        per_device, mesh=mesh, in_specs=placed, out_specs=P("batch", "weight"), check_vma=False
    )
```

```python
import functools
import math

import jax
import jax.numpy as jnp
from jax import lax
from jax.experimental import pallas as pl
from jax.experimental.pallas import tpu as pltpu
from jax.sharding import PartitionSpec as P

HEADS = 64
KV_HEADS = 8
HEAD_DIM = 128


ROPE_BASE = 500000.0
EPSILON = 1e-05

Z_CHIPS = 8


def positions_in_segment(seg_ids):
    places = jnp.arange(seg_ids.shape[0], dtype=jnp.int32)
    earlier = jnp.concatenate([seg_ids[:1] - 1, seg_ids[:-1]])
    starts = jnp.where(seg_ids != earlier, places, 0)
    leading = lax.cummax(starts, axis=0)
    return places - leading


def rotate(vectors, positions):
    half_dim = vectors.shape[-1] // 2
    ratios = jnp.arange(half_dim, dtype=jnp.float32) * (2.0 / vectors.shape[-1])
    frequency = jnp.exp(-math.log(ROPE_BASE) * ratios)
    angles = positions.astype(jnp.float32)[:, None] * frequency[None, :]
    cosine = jnp.cos(angles)[:, None, :]
    sine_part = jnp.sin(angles)[:, None, :]
    front_half = vectors[..., :half_dim]
    back_half = vectors[..., half_dim:]
    return jnp.concatenate(
        [front_half * cosine - back_half * sine_part, back_half * cosine + front_half * sine_part],
        axis=-1,
    )


def attend(grouped, rotated_keys, value_rows, seg_ids):
    scores = jnp.einsum(
        "ingd,jnd->ngij", grouped, rotated_keys, preferred_element_type=jnp.float32
    ) * grouped.shape[-1] ** (-0.5)
    places = jnp.arange(seg_ids.shape[0], dtype=jnp.int32)
    allowed = (seg_ids[:, None] == seg_ids[None, :]) & (places[None, :] <= places[:, None])
    weights = jnp.where(allowed, jnp.exp(scores), 0.0)
    probabilities = (weights / jnp.sum(weights, axis=-1, keepdims=True)).astype(jnp.bfloat16)
    mixed = jnp.einsum(
        "ngij,jnd->ingd", probabilities, value_rows, preferred_element_type=jnp.float32
    )
    return mixed.astype(jnp.bfloat16)


ROW_TILE = 128
SEGMENT_MOST = 64


def attention_kernel(heads, q_ref, k_ref, v_ref, cos_ref, sin_ref, row_seg_ref, col_seg_ref, o_ref):
    half = HEAD_DIM // 2

    def rope(x, rows):
        cosine, sine = cos_ref[rows, :], sin_ref[rows, :]
        a, b = x[:, :half], x[:, half:]
        return jnp.concatenate([a * cosine - b * sine, b * cosine + a * sine], axis=1)

    n_rows = q_ref.shape[0]
    keys = rope(k_ref[...].astype(jnp.float32), slice(0, n_rows)).astype(jnp.bfloat16)
    scale = HEAD_DIM ** (-0.5)
    reach = max(ROW_TILE, SEGMENT_MOST)
    for r0 in range(0, n_rows, ROW_TILE):
        c0 = max(0, r0 - reach)
        c1 = r0 + ROW_TILE
        rows = slice(r0, c1)
        places_i = lax.broadcasted_iota(jnp.int32, (ROW_TILE, c1 - c0), 0) + r0
        places_j = lax.broadcasted_iota(jnp.int32, (ROW_TILE, c1 - c0), 1) + c0
        allowed = (row_seg_ref[rows, :] == col_seg_ref[:, c0:c1]) & (places_j <= places_i)
        allowed = jnp.concatenate([allowed] * heads, axis=0)
        query = jnp.concatenate(
            [rope(q_ref[rows, h * HEAD_DIM : (h + 1) * HEAD_DIM], rows) for h in range(heads)],
            axis=0,
        ).astype(jnp.bfloat16)
        scores = lax.dot_general(
            query, keys[c0:c1], (((1,), (1,)), ((), ())), preferred_element_type=jnp.float32
        ) * scale
        weights = jnp.where(allowed, jnp.exp(scores), 0.0)
        total = jnp.sum(weights, axis=1, keepdims=True)
        probabilities = (weights / total).astype(jnp.bfloat16)
        mixed = jnp.dot(probabilities, v_ref[c0:c1, :], preferred_element_type=jnp.float32)
        for h in range(heads):
            o_ref[rows, h * HEAD_DIM : (h + 1) * HEAD_DIM] = mixed[
                h * ROW_TILE : (h + 1) * ROW_TILE
            ].astype(o_ref.dtype)


def rope_tables(positions):
    half_dim = HEAD_DIM // 2
    ratios = jnp.arange(half_dim, dtype=jnp.float32) * (2.0 / HEAD_DIM)
    frequency = jnp.exp(-math.log(ROPE_BASE) * ratios)
    angles = positions.astype(jnp.float32)[:, None] * frequency[None, :]
    return jnp.cos(angles), jnp.sin(angles)


def attention_kernel_call(projected, cols, key_rows, value_rows, cosine, sine, row_seg, col_seg):
    rows = projected.shape[0]
    half_dim = HEAD_DIM // 2
    vmem = pl.BlockSpec(memory_space=pltpu.VMEM)
    heads = cols // HEAD_DIM
    return pl.pallas_call(
        functools.partial(attention_kernel, heads),
        out_shape=jax.ShapeDtypeStruct((rows, cols), jnp.bfloat16),
        in_specs=[vmem] * 7,
        out_specs=vmem,
        cost_estimate=pl.CostEstimate(
            flops=4 * rows * rows * cols + 8 * rows * cols,
            transcendentals=heads * rows * rows,
            bytes_accessed=rows * cols * 6 + rows * HEAD_DIM * 4 + rows * half_dim * 8,
        ),
    )(
        projected,
        key_rows,
        value_rows,
        cosine,
        sine,
        row_seg,
        col_seg,
    )


def ring_gather(block, axis, stride, count):
    n = lax.psum(1, axis)
    me = lax.axis_index(axis)
    here = (me // stride) % count

    def moved(step):
        pairs = []
        for src in range(n):
            k = (src // stride) % count
            pairs.append((src, src + (((k + step) % count) - k) * stride))
        return pairs

    out = jnp.zeros((count,) + block.shape, block.dtype)
    out = lax.dynamic_update_index_in_dim(out, block, here, 0)
    from_right, from_left = block, block
    for step in range(1, count // 2 + 1):
        if step < count - step:
            from_right = lax.ppermute(from_right, axis, perm=moved(-1))
            out = lax.dynamic_update_index_in_dim(out, from_right, (here + step) % count, 0)
            from_left = lax.ppermute(from_left, axis, perm=moved(1))
        else:
            cut = block.shape[-2] // 2
            from_left = jnp.concatenate(
                [
                    lax.ppermute(from_left[..., :cut, :], axis, perm=moved(1)),
                    lax.ppermute(from_right[..., cut:, :], axis, perm=moved(-1)),
                ],
                axis=-2,
            )
        out = lax.dynamic_update_index_in_dim(out, from_left, (here - step) % count, 0)
    return out


def ring_others(block, axis, stride, count):
    n = lax.psum(1, axis)

    def moved(step):
        pairs = []
        for src in range(n):
            k = (src // stride) % count
            pairs.append((src, src + (((k + step) % count) - k) * stride))
        return pairs

    by_offset = {}
    from_right, from_left = block, block
    for step in range(1, count // 2 + 1):
        if step < count - step:
            from_right = lax.ppermute(from_right, axis, perm=moved(-1))
            from_left = lax.ppermute(from_left, axis, perm=moved(1))
            by_offset[step], by_offset[count - step] = from_right, from_left
        else:
            cut = block.shape[-2] // 2
            by_offset[step] = jnp.concatenate(
                [
                    lax.ppermute(from_left[..., :cut, :], axis, perm=moved(1)),
                    lax.ppermute(from_right[..., cut:, :], axis, perm=moved(-1)),
                ],
                axis=-2,
            )
    return jnp.stack([by_offset[r] for r in range(1, count)])


def ring_matmul(rows, block, axis, stride, count, starts, wait_rows):
    n = lax.psum(1, axis)
    me = lax.axis_index(axis)
    here = (me // stride) % count
    depth = block.shape[1]

    def moved(step):
        pairs = []
        for src in range(n):
            k = (src // stride) % count
            pairs.append((src, src + (((k + step) % count) - k) * stride))
        return pairs

    def product(part, owner):
        result = None
        for piece, start in enumerate(starts(owner)):
            lhs = lax.dynamic_slice_in_dim(rows, start, depth, 1)
            term = jnp.dot(lhs, part[piece], preferred_element_type=jnp.float32)
            result = term if result is None else result + term
        return result

    total = product(block, here)
    from_right, from_left = block, block
    for step in range(1, count // 2 + 1):
        if step == 2 and wait_rows:
            rows, from_right, from_left = lax.optimization_barrier((rows, from_right, from_left))
        if step < count - step:
            from_right = lax.ppermute(from_right, axis, perm=moved(-1))
            total = total + product(from_right, (here + step) % count)
            from_left = lax.ppermute(from_left, axis, perm=moved(1))
        else:
            cut = block.shape[-2] // 2
            from_left = jnp.concatenate(
                [
                    lax.ppermute(from_left[..., :cut, :], axis, perm=moved(1)),
                    lax.ppermute(from_right[..., cut:, :], axis, perm=moved(-1)),
                ],
                axis=-2,
            )
        total = total + product(from_left, (here - step) % count)
    return total


def per_device(tokens, segment_ids, norm_gain, query_weight, key_weight, value_weight):
    head_dim = HEAD_DIM
    query_cols = query_weight.shape[1]
    heads_dev = query_cols // head_dim
    group_size = HEADS // KV_HEADS
    n_weight = lax.psum(1, "weight")
    me = lax.axis_index("weight")
    core = me % 2
    first_kv = me * heads_dev // group_size
    key_block = lax.dynamic_slice_in_dim(key_weight, first_kv * head_dim, head_dim, 1)
    value_block = lax.dynamic_slice_in_dim(value_weight, first_kv * head_dim, head_dim, 1)
    kv_block = jnp.where(core == 0, key_block, value_block)
    values = tokens.astype(jnp.float32)
    inverse_rms = lax.rsqrt(jnp.mean(values * values, axis=1, keepdims=True) + EPSILON)
    normed = (values * inverse_rms * norm_gain[None, :]).astype(jnp.bfloat16)
    local_weights = jnp.concatenate([query_weight, kv_block], axis=1)
    n_batch = lax.psum(1, "batch")
    y_hi = n_batch // Z_CHIPS
    shard = local_weights.shape[0]
    yh = lax.axis_index("batch") % y_hi
    others = ring_others(local_weights, "batch", 1, y_hi)
    cosine, sine = rope_tables(positions_in_segment(segment_ids))
    row_seg, col_seg = segment_ids[:, None], segment_ids[None, :]
    others, cosine, sine, row_seg, col_seg = lax.optimization_barrier(
        (others, cosine, sine, row_seg, col_seg)
    )
    gathered = lax.all_gather(normed, "weight", axis=0, tiled=True)
    pack_rows = gathered.shape[0]
    own_part = ring_matmul(
        gathered,
        local_weights[None],
        "batch",
        y_hi,
        Z_CHIPS,
        lambda z: [(z * y_hi + yh) * shard],
        False,
    )
    other_part = ring_matmul(
        gathered,
        others,
        "batch",
        y_hi,
        Z_CHIPS,
        lambda z: [(z * y_hi + (yh + r) % y_hi) * shard for r in range(1, y_hi)],
        True,
    )
    projected = own_part + other_part
    own_rows = projected[:, query_cols:].astype(jnp.bfloat16)
    partner = [(w, w ^ 1) for w in range(n_weight)]
    other_rows = lax.ppermute(own_rows, "weight", perm=partner)
    key_rows = jnp.where(core == 0, own_rows, other_rows)
    value_rows = jnp.where(core == 0, other_rows, own_rows)
    return attention_kernel_call(
        projected, query_cols, key_rows, value_rows, cosine, sine, row_seg, col_seg
    )


def solution(mesh):
    placed = (
        P(("batch", "weight"), None),
        P("batch"),
        P(),
        P("batch", "weight"),
        P("batch", None),
        P("batch", None),
    )
    return jax.shard_map(
        per_device, mesh=mesh, in_specs=placed, out_specs=P("batch", "weight"), check_vma=False
    )
```

```python
import functools
import math

import jax
import jax.numpy as jnp
from jax import lax
from jax.experimental import pallas as pl
from jax.experimental.pallas import tpu as pltpu
from jax.sharding import PartitionSpec as P

HEADS = 64
KV_HEADS = 8
HEAD_DIM = 128


ROPE_BASE = 500000.0
EPSILON = 1e-05

Z_CHIPS = 8


def positions_in_segment(seg_ids):
    places = jnp.arange(seg_ids.shape[0], dtype=jnp.int32)
    earlier = jnp.concatenate([seg_ids[:1] - 1, seg_ids[:-1]])
    starts = jnp.where(seg_ids != earlier, places, 0)
    leading = lax.cummax(starts, axis=0)
    return places - leading


def rotate(vectors, positions):
    half_dim = vectors.shape[-1] // 2
    ratios = jnp.arange(half_dim, dtype=jnp.float32) * (2.0 / vectors.shape[-1])
    frequency = jnp.exp(-math.log(ROPE_BASE) * ratios)
    angles = positions.astype(jnp.float32)[:, None] * frequency[None, :]
    cosine = jnp.cos(angles)[:, None, :]
    sine_part = jnp.sin(angles)[:, None, :]
    front_half = vectors[..., :half_dim]
    back_half = vectors[..., half_dim:]
    return jnp.concatenate(
        [front_half * cosine - back_half * sine_part, back_half * cosine + front_half * sine_part],
        axis=-1,
    )


def attend(grouped, rotated_keys, value_rows, seg_ids):
    scores = jnp.einsum(
        "ingd,jnd->ngij", grouped, rotated_keys, preferred_element_type=jnp.float32
    ) * grouped.shape[-1] ** (-0.5)
    places = jnp.arange(seg_ids.shape[0], dtype=jnp.int32)
    allowed = (seg_ids[:, None] == seg_ids[None, :]) & (places[None, :] <= places[:, None])
    weights = jnp.where(allowed, jnp.exp(scores), 0.0)
    probabilities = (weights / jnp.sum(weights, axis=-1, keepdims=True)).astype(jnp.bfloat16)
    mixed = jnp.einsum(
        "ngij,jnd->ingd", probabilities, value_rows, preferred_element_type=jnp.float32
    )
    return mixed.astype(jnp.bfloat16)


ROW_TILE = 128
SEGMENT_MOST = 64


def attention_kernel(heads, q_ref, k_ref, v_ref, cos_ref, sin_ref, row_seg_ref, col_seg_ref, o_ref):
    half = HEAD_DIM // 2

    def rope(x, rows):
        cosine, sine = cos_ref[rows, :], sin_ref[rows, :]
        a, b = x[:, :half], x[:, half:]
        return jnp.concatenate([a * cosine - b * sine, b * cosine + a * sine], axis=1)

    n_rows = q_ref.shape[0]
    keys = rope(k_ref[...].astype(jnp.float32), slice(0, n_rows)).astype(jnp.bfloat16)
    scale = HEAD_DIM ** (-0.5)
    reach = max(ROW_TILE, SEGMENT_MOST)
    for r0 in range(0, n_rows, ROW_TILE):
        c0 = max(0, r0 - reach)
        c1 = r0 + ROW_TILE
        rows = slice(r0, c1)
        places_i = lax.broadcasted_iota(jnp.int32, (ROW_TILE, c1 - c0), 0) + r0
        places_j = lax.broadcasted_iota(jnp.int32, (ROW_TILE, c1 - c0), 1) + c0
        allowed = (row_seg_ref[rows, :] == col_seg_ref[:, c0:c1]) & (places_j <= places_i)
        allowed = jnp.concatenate([allowed] * heads, axis=0)
        query = jnp.concatenate(
            [rope(q_ref[rows, h * HEAD_DIM : (h + 1) * HEAD_DIM], rows) for h in range(heads)],
            axis=0,
        ).astype(jnp.bfloat16)
        scores = lax.dot_general(
            query, keys[c0:c1], (((1,), (1,)), ((), ())), preferred_element_type=jnp.float32
        ) * scale
        weights = jnp.where(allowed, jnp.exp(scores), 0.0)
        total = jnp.sum(weights, axis=1, keepdims=True)
        probabilities = (weights / total).astype(jnp.bfloat16)
        mixed = jnp.dot(probabilities, v_ref[c0:c1, :], preferred_element_type=jnp.float32)
        for h in range(heads):
            o_ref[rows, h * HEAD_DIM : (h + 1) * HEAD_DIM] = mixed[
                h * ROW_TILE : (h + 1) * ROW_TILE
            ].astype(o_ref.dtype)


def rope_tables(positions):
    half_dim = HEAD_DIM // 2
    ratios = jnp.arange(half_dim, dtype=jnp.float32) * (2.0 / HEAD_DIM)
    frequency = jnp.exp(-math.log(ROPE_BASE) * ratios)
    angles = positions.astype(jnp.float32)[:, None] * frequency[None, :]
    return jnp.cos(angles), jnp.sin(angles)


def attention_kernel_call(projected, cols, key_rows, value_rows, cosine, sine, row_seg, col_seg):
    rows = projected.shape[0]
    half_dim = HEAD_DIM // 2
    vmem = pl.BlockSpec(memory_space=pltpu.VMEM)
    heads = cols // HEAD_DIM
    return pl.pallas_call(
        functools.partial(attention_kernel, heads),
        out_shape=jax.ShapeDtypeStruct((rows, cols), jnp.bfloat16),
        in_specs=[vmem] * 7,
        out_specs=vmem,
        cost_estimate=pl.CostEstimate(
            flops=4 * rows * rows * cols + 8 * rows * cols,
            transcendentals=heads * rows * rows,
            bytes_accessed=rows * cols * 6 + rows * HEAD_DIM * 4 + rows * half_dim * 8,
        ),
    )(
        projected,
        key_rows,
        value_rows,
        cosine,
        sine,
        row_seg,
        col_seg,
    )


def ring_gather(block, axis, stride, count):
    n = lax.psum(1, axis)
    me = lax.axis_index(axis)
    here = (me // stride) % count

    def moved(step):
        pairs = []
        for src in range(n):
            k = (src // stride) % count
            pairs.append((src, src + (((k + step) % count) - k) * stride))
        return pairs

    out = jnp.zeros((count,) + block.shape, block.dtype)
    out = lax.dynamic_update_index_in_dim(out, block, here, 0)
    from_right, from_left = block, block
    for step in range(1, count // 2 + 1):
        if step < count - step:
            from_right = lax.ppermute(from_right, axis, perm=moved(-1))
            out = lax.dynamic_update_index_in_dim(out, from_right, (here + step) % count, 0)
            from_left = lax.ppermute(from_left, axis, perm=moved(1))
        else:
            cut = block.shape[-2] // 2
            from_left = jnp.concatenate(
                [
                    lax.ppermute(from_left[..., :cut, :], axis, perm=moved(1)),
                    lax.ppermute(from_right[..., cut:, :], axis, perm=moved(-1)),
                ],
                axis=-2,
            )
        out = lax.dynamic_update_index_in_dim(out, from_left, (here - step) % count, 0)
    return out


def ring_matmul(rows, block, axis, stride, count, starts, wait_rows, early=None):
    n = lax.psum(1, axis)
    me = lax.axis_index(axis)
    here = (me // stride) % count
    depth = block.shape[1]

    def moved(step):
        pairs = []
        for src in range(n):
            k = (src // stride) % count
            pairs.append((src, src + (((k + step) % count) - k) * stride))
        return pairs

    def early_product(part, piece_starts, owner):
        result = None
        for piece, start in enumerate(piece_starts(owner)):
            lhs = lax.dynamic_slice_in_dim(rows, start, depth, 1)
            term = jnp.dot(lhs, part[piece], preferred_element_type=jnp.float32)
            result = term if result is None else result + term
        return result

    def product(part, owner):
        result = None
        for piece, start in enumerate(starts(owner)):
            lhs = lax.dynamic_slice_in_dim(rows, start, depth, 1)
            term = jnp.dot(lhs, part[piece], preferred_element_type=jnp.float32)
            result = term if result is None else result + term
        return result

    total = product(block, here)
    from_right, from_left = block, block
    first = 1
    if early is not None:
        early_block, early_starts = early
        total = total + early_product(early_block, early_starts, here)
        early_right = lax.ppermute(early_block, axis, perm=moved(-1))
        early_left = lax.ppermute(early_block, axis, perm=moved(1))
        from_right = lax.ppermute(block, axis, perm=moved(-1))
        from_left = lax.ppermute(block, axis, perm=moved(1))
        total = total + early_product(early_right, early_starts, (here + 1) % count)
        total = total + product(from_right, (here + 1) % count)
        total = total + early_product(early_left, early_starts, (here - 1) % count)
        total = total + product(from_left, (here - 1) % count)
        from_right = jnp.concatenate([early_right, from_right], axis=0)
        from_left = jnp.concatenate([early_left, from_left], axis=0)
        block_starts = starts
        starts = lambda owner: early_starts(owner) + block_starts(owner)
        first = 2
    for step in range(first, count // 2 + 1):
        if step == 2 and wait_rows:
            rows, from_right, from_left = lax.optimization_barrier((rows, from_right, from_left))
        if step < count - step:
            from_right = lax.ppermute(from_right, axis, perm=moved(-1))
            total = total + product(from_right, (here + step) % count)
            from_left = lax.ppermute(from_left, axis, perm=moved(1))
        else:
            cut = block.shape[-2] // 2
            from_left = jnp.concatenate(
                [
                    lax.ppermute(from_left[..., :cut, :], axis, perm=moved(1)),
                    lax.ppermute(from_right[..., cut:, :], axis, perm=moved(-1)),
                ],
                axis=-2,
            )
        total = total + product(from_left, (here - step) % count)
    return total


def per_device(tokens, segment_ids, norm_gain, query_weight, key_weight, value_weight):
    head_dim = HEAD_DIM
    query_cols = query_weight.shape[1]
    heads_dev = query_cols // head_dim
    group_size = HEADS // KV_HEADS
    n_weight = lax.psum(1, "weight")
    me = lax.axis_index("weight")
    core = me % 2
    first_kv = me * heads_dev // group_size
    key_block = lax.dynamic_slice_in_dim(key_weight, first_kv * head_dim, head_dim, 1)
    value_block = lax.dynamic_slice_in_dim(value_weight, first_kv * head_dim, head_dim, 1)
    kv_block = jnp.where(core == 0, key_block, value_block)
    values = tokens.astype(jnp.float32)
    inverse_rms = lax.rsqrt(jnp.mean(values * values, axis=1, keepdims=True) + EPSILON)
    normed = (values * inverse_rms * norm_gain[None, :]).astype(jnp.bfloat16)
    local_weights = jnp.concatenate([query_weight, kv_block], axis=1)
    n_batch = lax.psum(1, "batch")
    y_hi = n_batch // Z_CHIPS
    shard = local_weights.shape[0]
    yh = lax.axis_index("batch") % y_hi
    near = ring_gather(local_weights, "batch", 1, y_hi)
    others = jnp.stack([near[(yh + r) % y_hi] for r in range(1, y_hi)])
    cosine, sine = rope_tables(positions_in_segment(segment_ids))
    row_seg, col_seg = segment_ids[:, None], segment_ids[None, :]
    others, cosine, sine, row_seg, col_seg = lax.optimization_barrier(
        (others, cosine, sine, row_seg, col_seg)
    )
    gathered = lax.all_gather(normed, "weight", axis=0, tiled=True)
    pack_rows = gathered.shape[0]
    projected = ring_matmul(
        gathered,
        others,
        "batch",
        y_hi,
        Z_CHIPS,
        lambda z: [(z * y_hi + (yh + r) % y_hi) * shard for r in range(1, y_hi)],
        True,
        early=(local_weights[None], lambda z: [(z * y_hi + yh) * shard]),
    )
    own_rows = projected[:, query_cols:].astype(jnp.bfloat16)
    partner = [(w, w ^ 1) for w in range(n_weight)]
    other_rows = lax.ppermute(own_rows, "weight", perm=partner)
    key_rows = jnp.where(core == 0, own_rows, other_rows)
    value_rows = jnp.where(core == 0, other_rows, own_rows)
    return attention_kernel_call(
        projected, query_cols, key_rows, value_rows, cosine, sine, row_seg, col_seg
    )


def solution(mesh):
    placed = (
        P(("batch", "weight"), None),
        P("batch"),
        P(),
        P("batch", "weight"),
        P("batch", None),
        P("batch", None),
    )
    return jax.shard_map(
        per_device, mesh=mesh, in_specs=placed, out_specs=P("batch", "weight"), check_vma=False
    )
```

```python
import functools
import math

import jax
import jax.numpy as jnp
from jax import lax
from jax.experimental import pallas as pl
from jax.experimental.pallas import tpu as pltpu
from jax.sharding import PartitionSpec as P

HEADS = 64
KV_HEADS = 8
HEAD_DIM = 128


ROPE_BASE = 500000.0
EPSILON = 1e-05

Z_CHIPS = 8


def positions_in_segment(seg_ids):
    places = jnp.arange(seg_ids.shape[0], dtype=jnp.int32)
    earlier = jnp.concatenate([seg_ids[:1] - 1, seg_ids[:-1]])
    starts = jnp.where(seg_ids != earlier, places, 0)
    leading = lax.cummax(starts, axis=0)
    return places - leading


def rotate(vectors, positions):
    half_dim = vectors.shape[-1] // 2
    ratios = jnp.arange(half_dim, dtype=jnp.float32) * (2.0 / vectors.shape[-1])
    frequency = jnp.exp(-math.log(ROPE_BASE) * ratios)
    angles = positions.astype(jnp.float32)[:, None] * frequency[None, :]
    cosine = jnp.cos(angles)[:, None, :]
    sine_part = jnp.sin(angles)[:, None, :]
    front_half = vectors[..., :half_dim]
    back_half = vectors[..., half_dim:]
    return jnp.concatenate(
        [front_half * cosine - back_half * sine_part, back_half * cosine + front_half * sine_part],
        axis=-1,
    )


def attend(grouped, rotated_keys, value_rows, seg_ids):
    scores = jnp.einsum(
        "ingd,jnd->ngij", grouped, rotated_keys, preferred_element_type=jnp.float32
    ) * grouped.shape[-1] ** (-0.5)
    places = jnp.arange(seg_ids.shape[0], dtype=jnp.int32)
    allowed = (seg_ids[:, None] == seg_ids[None, :]) & (places[None, :] <= places[:, None])
    weights = jnp.where(allowed, jnp.exp(scores), 0.0)
    probabilities = (weights / jnp.sum(weights, axis=-1, keepdims=True)).astype(jnp.bfloat16)
    mixed = jnp.einsum(
        "ngij,jnd->ingd", probabilities, value_rows, preferred_element_type=jnp.float32
    )
    return mixed.astype(jnp.bfloat16)


ROW_TILE = 128
SEGMENT_MOST = 64


def attention_kernel(heads, q_ref, k_ref, v_ref, cos_ref, sin_ref, row_seg_ref, col_seg_ref, o_ref):
    half = HEAD_DIM // 2

    def rope(x, rows):
        cosine, sine = cos_ref[rows, :], sin_ref[rows, :]
        a, b = x[:, :half], x[:, half:]
        return jnp.concatenate([a * cosine - b * sine, b * cosine + a * sine], axis=1)

    n_rows = q_ref.shape[0]
    keys = rope(k_ref[...].astype(jnp.float32), slice(0, n_rows)).astype(jnp.bfloat16)
    scale = HEAD_DIM ** (-0.5)
    reach = max(ROW_TILE, SEGMENT_MOST)
    for r0 in range(0, n_rows, ROW_TILE):
        c0 = max(0, r0 - reach)
        c1 = r0 + ROW_TILE
        rows = slice(r0, c1)
        places_i = lax.broadcasted_iota(jnp.int32, (ROW_TILE, c1 - c0), 0) + r0
        places_j = lax.broadcasted_iota(jnp.int32, (ROW_TILE, c1 - c0), 1) + c0
        allowed = (row_seg_ref[rows, :] == col_seg_ref[:, c0:c1]) & (places_j <= places_i)
        allowed = jnp.concatenate([allowed] * heads, axis=0)
        query = jnp.concatenate(
            [rope(q_ref[rows, h * HEAD_DIM : (h + 1) * HEAD_DIM], rows) for h in range(heads)],
            axis=0,
        ).astype(jnp.bfloat16)
        scores = lax.dot_general(
            query, keys[c0:c1], (((1,), (1,)), ((), ())), preferred_element_type=jnp.float32
        ) * scale
        weights = jnp.where(allowed, jnp.exp(scores), 0.0)
        total = jnp.sum(weights, axis=1, keepdims=True)
        probabilities = (weights / total).astype(jnp.bfloat16)
        mixed = jnp.dot(probabilities, v_ref[c0:c1, :], preferred_element_type=jnp.float32)
        for h in range(heads):
            o_ref[rows, h * HEAD_DIM : (h + 1) * HEAD_DIM] = mixed[
                h * ROW_TILE : (h + 1) * ROW_TILE
            ].astype(o_ref.dtype)


def rope_tables(positions):
    half_dim = HEAD_DIM // 2
    ratios = jnp.arange(half_dim, dtype=jnp.float32) * (2.0 / HEAD_DIM)
    frequency = jnp.exp(-math.log(ROPE_BASE) * ratios)
    angles = positions.astype(jnp.float32)[:, None] * frequency[None, :]
    return jnp.cos(angles), jnp.sin(angles)


def attention_kernel_call(projected, cols, key_rows, value_rows, cosine, sine, row_seg, col_seg):
    rows = projected.shape[0]
    half_dim = HEAD_DIM // 2
    vmem = pl.BlockSpec(memory_space=pltpu.VMEM)
    heads = cols // HEAD_DIM
    return pl.pallas_call(
        functools.partial(attention_kernel, heads),
        out_shape=jax.ShapeDtypeStruct((rows, cols), jnp.bfloat16),
        in_specs=[vmem] * 7,
        out_specs=vmem,
        cost_estimate=pl.CostEstimate(
            flops=4 * rows * rows * cols + 8 * rows * cols,
            transcendentals=heads * rows * rows,
            bytes_accessed=rows * cols * 6 + rows * HEAD_DIM * 4 + rows * half_dim * 8,
        ),
    )(
        projected,
        key_rows,
        value_rows,
        cosine,
        sine,
        row_seg,
        col_seg,
    )


def ring_gather(block, axis, stride, count):
    n = lax.psum(1, axis)
    me = lax.axis_index(axis)
    here = (me // stride) % count

    def moved(step):
        pairs = []
        for src in range(n):
            k = (src // stride) % count
            pairs.append((src, src + (((k + step) % count) - k) * stride))
        return pairs

    out = jnp.zeros((count,) + block.shape, block.dtype)
    out = lax.dynamic_update_index_in_dim(out, block, here, 0)
    from_right, from_left = block, block
    for step in range(1, count // 2 + 1):
        if step < count - step:
            from_right = lax.ppermute(from_right, axis, perm=moved(-1))
            out = lax.dynamic_update_index_in_dim(out, from_right, (here + step) % count, 0)
            from_left = lax.ppermute(from_left, axis, perm=moved(1))
        else:
            cut = block.shape[-2] // 2
            from_left = jnp.concatenate(
                [
                    lax.ppermute(from_left[..., :cut, :], axis, perm=moved(1)),
                    lax.ppermute(from_right[..., cut:, :], axis, perm=moved(-1)),
                ],
                axis=-2,
            )
        out = lax.dynamic_update_index_in_dim(out, from_left, (here - step) % count, 0)
    return out


def ring_matmul(rows, block, axis, stride, count, starts, wait_rows):
    n = lax.psum(1, axis)
    me = lax.axis_index(axis)
    here = (me // stride) % count
    depth = block.shape[1]

    def moved(step):
        pairs = []
        for src in range(n):
            k = (src // stride) % count
            pairs.append((src, src + (((k + step) % count) - k) * stride))
        return pairs

    def product(part, owner):
        result = None
        for piece, start in enumerate(starts(owner)):
            lhs = lax.dynamic_slice_in_dim(rows, start, depth, 1)
            term = jnp.dot(lhs, part[piece], preferred_element_type=jnp.float32)
            result = term if result is None else result + term
        return result

    total = product(block, here)
    from_right, from_left = block, block
    for step in range(1, count // 2 + 1):
        if step == 3 and wait_rows:
            rows, from_right, from_left = lax.optimization_barrier((rows, from_right, from_left))
        if step < count - step:
            from_right = lax.ppermute(from_right, axis, perm=moved(-1))
            total = total + product(from_right, (here + step) % count)
            from_left = lax.ppermute(from_left, axis, perm=moved(1))
        else:
            cut = block.shape[-2] // 2
            from_left = jnp.concatenate(
                [
                    lax.ppermute(from_left[..., :cut, :], axis, perm=moved(1)),
                    lax.ppermute(from_right[..., cut:, :], axis, perm=moved(-1)),
                ],
                axis=-2,
            )
        total = total + product(from_left, (here - step) % count)
    return total


def per_device(tokens, segment_ids, norm_gain, query_weight, key_weight, value_weight):
    head_dim = HEAD_DIM
    query_cols = query_weight.shape[1]
    heads_dev = query_cols // head_dim
    group_size = HEADS // KV_HEADS
    n_weight = lax.psum(1, "weight")
    me = lax.axis_index("weight")
    core = me % 2
    first_kv = me * heads_dev // group_size
    key_block = lax.dynamic_slice_in_dim(key_weight, first_kv * head_dim, head_dim, 1)
    value_block = lax.dynamic_slice_in_dim(value_weight, first_kv * head_dim, head_dim, 1)
    kv_block = jnp.where(core == 0, key_block, value_block)
    values = tokens.astype(jnp.float32)
    inverse_rms = lax.rsqrt(jnp.mean(values * values, axis=1, keepdims=True) + EPSILON)
    normed = (values * inverse_rms * norm_gain[None, :]).astype(jnp.bfloat16)
    local_weights = jnp.concatenate([query_weight, kv_block], axis=1)
    n_batch = lax.psum(1, "batch")
    y_hi = n_batch // Z_CHIPS
    shard = local_weights.shape[0]
    yh = lax.axis_index("batch") % y_hi
    near = ring_gather(local_weights, "batch", 1, y_hi)
    others = jnp.stack([near[(yh + r) % y_hi] for r in range(1, y_hi)])
    cosine, sine = rope_tables(positions_in_segment(segment_ids))
    row_seg, col_seg = segment_ids[:, None], segment_ids[None, :]
    others, cosine, sine, row_seg, col_seg = lax.optimization_barrier(
        (others, cosine, sine, row_seg, col_seg)
    )
    gathered = lax.all_gather(normed, "weight", axis=0, tiled=True)
    pack_rows = gathered.shape[0]
    own_part = ring_matmul(
        gathered,
        local_weights[None],
        "batch",
        y_hi,
        Z_CHIPS,
        lambda z: [(z * y_hi + yh) * shard],
        False,
    )
    other_part = ring_matmul(
        gathered,
        others,
        "batch",
        y_hi,
        Z_CHIPS,
        lambda z: [(z * y_hi + (yh + r) % y_hi) * shard for r in range(1, y_hi)],
        True,
    )
    projected = own_part + other_part
    own_rows = projected[:, query_cols:].astype(jnp.bfloat16)
    partner = [(w, w ^ 1) for w in range(n_weight)]
    other_rows = lax.ppermute(own_rows, "weight", perm=partner)
    key_rows = jnp.where(core == 0, own_rows, other_rows)
    value_rows = jnp.where(core == 0, other_rows, own_rows)
    return attention_kernel_call(
        projected, query_cols, key_rows, value_rows, cosine, sine, row_seg, col_seg
    )


def solution(mesh):
    placed = (
        P(("batch", "weight"), None),
        P("batch"),
        P(),
        P("batch", "weight"),
        P("batch", None),
        P("batch", None),
    )
    return jax.shard_map(
        per_device, mesh=mesh, in_specs=placed, out_specs=P("batch", "weight"), check_vma=False
    )
```

```python
import functools
import math

import jax
import jax.numpy as jnp
from jax import lax
from jax.experimental import pallas as pl
from jax.experimental.pallas import tpu as pltpu
from jax.sharding import PartitionSpec as P

HEADS = 64
KV_HEADS = 8
HEAD_DIM = 128


ROPE_BASE = 500000.0
EPSILON = 1e-05

Z_CHIPS = 8


def positions_in_segment(seg_ids):
    places = jnp.arange(seg_ids.shape[0], dtype=jnp.int32)
    earlier = jnp.concatenate([seg_ids[:1] - 1, seg_ids[:-1]])
    starts = jnp.where(seg_ids != earlier, places, 0)
    leading = lax.cummax(starts, axis=0)
    return places - leading


def rotate(vectors, positions):
    half_dim = vectors.shape[-1] // 2
    ratios = jnp.arange(half_dim, dtype=jnp.float32) * (2.0 / vectors.shape[-1])
    frequency = jnp.exp(-math.log(ROPE_BASE) * ratios)
    angles = positions.astype(jnp.float32)[:, None] * frequency[None, :]
    cosine = jnp.cos(angles)[:, None, :]
    sine_part = jnp.sin(angles)[:, None, :]
    front_half = vectors[..., :half_dim]
    back_half = vectors[..., half_dim:]
    return jnp.concatenate(
        [front_half * cosine - back_half * sine_part, back_half * cosine + front_half * sine_part],
        axis=-1,
    )


def attend(grouped, rotated_keys, value_rows, seg_ids):
    scores = jnp.einsum(
        "ingd,jnd->ngij", grouped, rotated_keys, preferred_element_type=jnp.float32
    ) * grouped.shape[-1] ** (-0.5)
    places = jnp.arange(seg_ids.shape[0], dtype=jnp.int32)
    allowed = (seg_ids[:, None] == seg_ids[None, :]) & (places[None, :] <= places[:, None])
    weights = jnp.where(allowed, jnp.exp(scores), 0.0)
    probabilities = (weights / jnp.sum(weights, axis=-1, keepdims=True)).astype(jnp.bfloat16)
    mixed = jnp.einsum(
        "ngij,jnd->ingd", probabilities, value_rows, preferred_element_type=jnp.float32
    )
    return mixed.astype(jnp.bfloat16)


ROW_TILE = 128
SEGMENT_MOST = 64


def attention_kernel(heads, q_ref, k_ref, v_ref, cos_ref, sin_ref, row_seg_ref, col_seg_ref, o_ref):
    half = HEAD_DIM // 2

    def rope(x, rows):
        cosine, sine = cos_ref[rows, :], sin_ref[rows, :]
        a, b = x[:, :half], x[:, half:]
        return jnp.concatenate([a * cosine - b * sine, b * cosine + a * sine], axis=1)

    n_rows = q_ref.shape[0]
    keys = rope(k_ref[...].astype(jnp.float32), slice(0, n_rows)).astype(jnp.bfloat16)
    scale = HEAD_DIM ** (-0.5)
    reach = max(ROW_TILE, SEGMENT_MOST)
    for r0 in range(0, n_rows, ROW_TILE):
        c0 = max(0, r0 - reach)
        c1 = r0 + ROW_TILE
        rows = slice(r0, c1)
        places_i = lax.broadcasted_iota(jnp.int32, (ROW_TILE, c1 - c0), 0) + r0
        places_j = lax.broadcasted_iota(jnp.int32, (ROW_TILE, c1 - c0), 1) + c0
        allowed = (row_seg_ref[rows, :] == col_seg_ref[:, c0:c1]) & (places_j <= places_i)
        allowed = jnp.concatenate([allowed] * heads, axis=0)
        query = jnp.concatenate(
            [rope(q_ref[rows, h * HEAD_DIM : (h + 1) * HEAD_DIM], rows) for h in range(heads)],
            axis=0,
        ).astype(jnp.bfloat16)
        scores = lax.dot_general(
            query, keys[c0:c1], (((1,), (1,)), ((), ())), preferred_element_type=jnp.float32
        ) * scale
        weights = jnp.where(allowed, jnp.exp(scores), 0.0)
        total = jnp.sum(weights, axis=1, keepdims=True)
        probabilities = (weights / total).astype(jnp.bfloat16)
        mixed = jnp.dot(probabilities, v_ref[c0:c1, :], preferred_element_type=jnp.float32)
        for h in range(heads):
            o_ref[rows, h * HEAD_DIM : (h + 1) * HEAD_DIM] = mixed[
                h * ROW_TILE : (h + 1) * ROW_TILE
            ].astype(o_ref.dtype)


def rope_tables(positions):
    half_dim = HEAD_DIM // 2
    ratios = jnp.arange(half_dim, dtype=jnp.float32) * (2.0 / HEAD_DIM)
    frequency = jnp.exp(-math.log(ROPE_BASE) * ratios)
    angles = positions.astype(jnp.float32)[:, None] * frequency[None, :]
    return jnp.cos(angles), jnp.sin(angles)


def attention_kernel_call(projected, cols, key_rows, value_rows, cosine, sine, row_seg, col_seg):
    rows = projected.shape[0]
    half_dim = HEAD_DIM // 2
    vmem = pl.BlockSpec(memory_space=pltpu.VMEM)
    heads = cols // HEAD_DIM
    return pl.pallas_call(
        functools.partial(attention_kernel, heads),
        out_shape=jax.ShapeDtypeStruct((rows, cols), jnp.bfloat16),
        in_specs=[vmem] * 7,
        out_specs=vmem,
        cost_estimate=pl.CostEstimate(
            flops=4 * rows * 2 * ROW_TILE * cols + 8 * rows * cols,
            transcendentals=heads * rows * 2 * ROW_TILE,
            bytes_accessed=rows * cols * 6 + rows * HEAD_DIM * 4 + rows * half_dim * 8,
        ),
    )(
        projected,
        key_rows,
        value_rows,
        cosine,
        sine,
        row_seg,
        col_seg,
    )


def ring_gather(block, axis, stride, count):
    n = lax.psum(1, axis)
    me = lax.axis_index(axis)
    here = (me // stride) % count

    def moved(step):
        pairs = []
        for src in range(n):
            k = (src // stride) % count
            pairs.append((src, src + (((k + step) % count) - k) * stride))
        return pairs

    out = jnp.zeros((count,) + block.shape, block.dtype)
    out = lax.dynamic_update_index_in_dim(out, block, here, 0)
    from_right, from_left = block, block
    for step in range(1, count // 2 + 1):
        if step < count - step:
            from_right = lax.ppermute(from_right, axis, perm=moved(-1))
            out = lax.dynamic_update_index_in_dim(out, from_right, (here + step) % count, 0)
            from_left = lax.ppermute(from_left, axis, perm=moved(1))
        else:
            cut = block.shape[-2] // 2
            from_left = jnp.concatenate(
                [
                    lax.ppermute(from_left[..., :cut, :], axis, perm=moved(1)),
                    lax.ppermute(from_right[..., cut:, :], axis, perm=moved(-1)),
                ],
                axis=-2,
            )
        out = lax.dynamic_update_index_in_dim(out, from_left, (here - step) % count, 0)
    return out


def ring_matmul(rows, block, axis, stride, count, starts, wait_rows):
    n = lax.psum(1, axis)
    me = lax.axis_index(axis)
    here = (me // stride) % count
    depth = block.shape[1]

    def moved(step):
        pairs = []
        for src in range(n):
            k = (src // stride) % count
            pairs.append((src, src + (((k + step) % count) - k) * stride))
        return pairs

    def product(part, owner):
        result = None
        for piece, start in enumerate(starts(owner)):
            lhs = lax.dynamic_slice_in_dim(rows, start, depth, 1)
            term = jnp.dot(lhs, part[piece], preferred_element_type=jnp.float32)
            result = term if result is None else result + term
        return result

    total = product(block, here)
    from_right, from_left = block, block
    for step in range(1, count // 2 + 1):
        if step == 2 and wait_rows:
            rows, from_right, from_left = lax.optimization_barrier((rows, from_right, from_left))
        if step < count - step:
            from_right = lax.ppermute(from_right, axis, perm=moved(-1))
            total = total + product(from_right, (here + step) % count)
            from_left = lax.ppermute(from_left, axis, perm=moved(1))
        else:
            cut = block.shape[-2] // 2
            from_left = jnp.concatenate(
                [
                    lax.ppermute(from_left[..., :cut, :], axis, perm=moved(1)),
                    lax.ppermute(from_right[..., cut:, :], axis, perm=moved(-1)),
                ],
                axis=-2,
            )
        total = total + product(from_left, (here - step) % count)
    return total


def per_device(tokens, segment_ids, norm_gain, query_weight, key_weight, value_weight):
    head_dim = HEAD_DIM
    query_cols = query_weight.shape[1]
    heads_dev = query_cols // head_dim
    group_size = HEADS // KV_HEADS
    n_weight = lax.psum(1, "weight")
    me = lax.axis_index("weight")
    core = me % 2
    first_kv = me * heads_dev // group_size
    key_block = lax.dynamic_slice_in_dim(key_weight, first_kv * head_dim, head_dim, 1)
    value_block = lax.dynamic_slice_in_dim(value_weight, first_kv * head_dim, head_dim, 1)
    kv_block = jnp.where(core == 0, key_block, value_block)
    values = tokens.astype(jnp.float32)
    inverse_rms = lax.rsqrt(jnp.mean(values * values, axis=1, keepdims=True) + EPSILON)
    normed = (values * inverse_rms * norm_gain[None, :]).astype(jnp.bfloat16)
    local_weights = jnp.concatenate([query_weight, kv_block], axis=1)
    n_batch = lax.psum(1, "batch")
    y_hi = n_batch // Z_CHIPS
    shard = local_weights.shape[0]
    yh = lax.axis_index("batch") % y_hi
    near = ring_gather(local_weights, "batch", 1, y_hi)
    others = jnp.stack([near[(yh + r) % y_hi] for r in range(1, y_hi)])
    cosine, sine = rope_tables(positions_in_segment(segment_ids))
    row_seg, col_seg = segment_ids[:, None], segment_ids[None, :]
    others, cosine, sine, row_seg, col_seg = lax.optimization_barrier(
        (others, cosine, sine, row_seg, col_seg)
    )
    gathered = lax.all_gather(normed, "weight", axis=0, tiled=True)
    pack_rows = gathered.shape[0]
    own_part = ring_matmul(
        gathered,
        local_weights[None],
        "batch",
        y_hi,
        Z_CHIPS,
        lambda z: [(z * y_hi + yh) * shard],
        False,
    )
    other_part = ring_matmul(
        gathered,
        others,
        "batch",
        y_hi,
        Z_CHIPS,
        lambda z: [(z * y_hi + (yh + r) % y_hi) * shard for r in range(1, y_hi)],
        True,
    )
    projected = own_part + other_part
    own_rows = projected[:, query_cols:].astype(jnp.bfloat16)
    partner = [(w, w ^ 1) for w in range(n_weight)]
    other_rows = lax.ppermute(own_rows, "weight", perm=partner)
    key_rows = jnp.where(core == 0, own_rows, other_rows)
    value_rows = jnp.where(core == 0, other_rows, own_rows)
    return attention_kernel_call(
        projected, query_cols, key_rows, value_rows, cosine, sine, row_seg, col_seg
    )


def solution(mesh):
    placed = (
        P(("batch", "weight"), None),
        P("batch"),
        P(),
        P("batch", "weight"),
        P("batch", None),
        P("batch", None),
    )
    return jax.shard_map(
        per_device, mesh=mesh, in_specs=placed, out_specs=P("batch", "weight"), check_vma=False
    )
```
